32 devices in a mesh: gx: 8 (over z, x), gy: 4 (over y, core).
Axes of the slice: x: 2, y: 2, z: 4, core: 2. Of those that a mesh axis runs over, the one named last changes fastest.
Arguments:
- facies: int32 [64, 64, 128], P('gx', 'gy'), may hold values from 0 to 7
- source: float32 [64, 64, 128], P('gx', 'gy'), may hold values from -5 to 5
- facies_perm: float32 [8], replicated, may hold values from 0.5 to 5
- facies_store: float32 [8], replicated, may hold values from 0.0002 to 0.001
- well_x: int32 [64], replicated, may hold values from 0 to 63
- well_y: int32 [64], replicated, may hold values from 0 to 63
- well_rate: float32 [64], replicated, may hold values from -2000 to 2000
Outputs:
- pressure: float32 [64, 64, 128], P('gx', 'gy')
The draws below stay inside these ranges and needn't reach their ends.
All inputs are finite; a program needn't handle non-finite values.
Results may differ from the reference program's by a relative error of at most 0.0003.
Values sent between devices are 32-bit elements; how exact they have to be, the bound alone decides.
No kernel may reach another device: no remote copies, remote signals or barrier semaphores. Data moves between devices by JAX's collectives and lax.ppermute only.
A program may use at most 128 MiB of HBM per device.

```python
import math
import jax
import jax.numpy as jnp
import numpy as np
from jax import lax

CELLS_Z = 128
BLOCK_X = 64
BLOCK_Y = 64
BLOCK_Z = 16
SWEEPS = 3
FACIES = 8
WELL_COUNT = 64
GRID_X = 64
GRID_Y = 64
BLOCKS_X = 1
BLOCKS_Y = 1
BLOCKS_Z = 8
COARSE = 8
SEGMENTS = 9


def draw_source(key, part):
    rough_part = jnp.clip(jax.random.normal(key, (GRID_X, GRID_Y, CELLS_Z), jnp.float32), -4.0, 4.0)
    layer_pos = (jnp.arange(CELLS_Z, dtype=jnp.float32) + 0.5) / BLOCK_Z
    layered = jnp.sin(3.14159265 * layer_pos)
    return rough_part + 0.5 * layered[None, None, :]


def place_ends(entries, stream_key, low, high):
    spot = [jax.random.randint(jax.random.fold_in(stream_key, axis), (), 0, length) for axis, length in enumerate(entries.shape)]
    longest = entries.shape.index(max(entries.shape))
    neighbour = spot[:longest] + [(spot[longest] + 1) % entries.shape[longest]] + spot[longest + 1:]
    return entries.at[tuple(spot)].set(low).at[tuple(neighbour)].set(high)


def setup_inputs(seed: int = 0) -> dict:
    streams_of = jax.random.split(jax.random.key(seed), 8)
    facies = place_ends(jax.random.randint(streams_of[0], (GRID_X, GRID_Y, CELLS_Z), 0, FACIES), jax.random.fold_in(streams_of[0], 1), 0, FACIES - 1).astype(jnp.int32)
    source = draw_source(jax.random.fold_in(streams_of[7], 71), 0)
    facies_perm = jnp.clip(jnp.exp(jax.random.uniform(streams_of[2], (FACIES,), jnp.float32, math.log(0.5), math.log(5.0))), 0.5, 5.0)
    facies_store = jnp.clip(jnp.exp(jax.random.uniform(streams_of[3], (FACIES,), jnp.float32, math.log(0.0002), math.log(0.001))), 0.0002, 0.001)
    well_x = place_ends(jax.random.randint(streams_of[4], (WELL_COUNT,), 0, GRID_X), jax.random.fold_in(streams_of[4], 1), 0, GRID_X - 1).astype(jnp.int32)
    well_y = place_ends(jax.random.randint(streams_of[5], (WELL_COUNT,), 0, GRID_Y), jax.random.fold_in(streams_of[5], 1), 0, GRID_Y - 1).astype(jnp.int32)
    well_rate = jnp.clip(jax.random.uniform(streams_of[6], (WELL_COUNT,), jnp.float32, -2000.0, 2000.0), -2000.0, 2000.0)
    return dict(facies=facies, source=source, facies_perm=facies_perm, facies_store=facies_store, well_x=well_x, well_y=well_y, well_rate=well_rate)


RELAX_WEIGHT = 2.0 / 3.0
HIGHEST = lax.Precision.HIGHEST
first_bits = np.array([0, 0, 0, 0, 1, 1, 1, 1], dtype=np.int32)
second_bits = np.array([0, 0, 1, 1, 0, 0, 1, 1], dtype=np.int32)
third_bits = np.array([0, 1, 0, 1, 0, 1, 0, 1], dtype=np.int32)
shift_along_x = np.array([0, 2, -2, 0, 0, 0, 0], dtype=np.int32)
shift_along_y = np.array([0, 0, 0, 2, -2, 0, 0], dtype=np.int32)
shift_along_z = np.array([0, 0, 0, 0, 0, 2, -2], dtype=np.int32)

def support_of(coords, block_size, parity):
    return (parity + 2 * jnp.floor_divide(coords + block_size // 2 - block_size * parity, 2 * block_size)).astype(jnp.int32)

def parity_nodes(coords, block_size):
    return jnp.stack([support_of(coords, block_size, 0), support_of(coords, block_size, 1)])

def parity_start(coords, block_size):
    node_ids = parity_nodes(coords, block_size)
    return (node_ids == jnp.floor_divide(coords, block_size)[None]).astype(jnp.float32)

def parity_same(coords, block_size):
    node_here = parity_nodes(coords[:-1], block_size)
    node_next = parity_nodes(coords[1:], block_size)
    return (node_here == node_next).astype(jnp.float32)

def harmonic(left_perm, right_perm):
    return 2.0 * left_perm * right_perm / (left_perm + right_perm)

def face_pad(values_in, dim_id, before):
    widths = [(0, 0), (0, 0), (0, 0)]
    widths[dim_id] = (1, 0) if before else (0, 1)
    return jnp.pad(values_in, widths)

def expand(line_in, dim_id):
    new_shape = [1, 1, 1]
    new_shape[dim_id] = line_in.shape[0]
    return line_in.reshape(new_shape)

def split_faces(values_in, dim_id):
    length = values_in.shape[dim_id]
    below_part = lax.slice_in_dim(values_in, 0, length - 1, axis=dim_id)
    above_part = lax.slice_in_dim(values_in, 1, length, axis=dim_id)
    return (below_part, above_part)

def cut_apply(values_in, storage, trans_all, same_all):
    result = storage * values_in
    for dim_id in range(3):
        trans_face = trans_all[dim_id]
        same_line = expand(same_all[dim_id], dim_id)
        below_part, above_part = split_faces(values_in, dim_id)
        result = result + face_pad(trans_face * (below_part - same_line * above_part), dim_id, False)
        result = result + face_pad(trans_face * (above_part - same_line * below_part), dim_id, True)
    return result

def rim_terms(values_in, trans_all, same_all):
    result = []
    for dim_id in range(3):
        trans_face = trans_all[dim_id]
        cross_mask = 1.0 - expand(same_all[dim_id], dim_id)
        below_part, above_part = split_faces(values_in, dim_id)
        result.append(face_pad(-trans_face * cross_mask * above_part, dim_id, False))
        result.append(face_pad(-trans_face * cross_mask * below_part, dim_id, True))
    return result

def diagonal_of(storage, trans_all):
    result = storage
    for dim_id in range(3):
        result = result + face_pad(trans_all[dim_id], dim_id, False) + face_pad(trans_all[dim_id], dim_id, True)
    return result

def lookup(facies, code_table):
    result = jnp.zeros(facies.shape, jnp.float32)
    for code_id in range(code_table.shape[0]):
        result = result + jnp.where(facies == code_id, code_table[code_id], 0.0)
    return result

def flatten_node(index_x, index_y, index_z, counts):
    count_x, count_y, count_z = counts
    flat_ids = (jnp.clip(index_x, 0, count_x - 1) * count_y + jnp.clip(index_y, 0, count_y - 1)) * count_z
    return (flat_ids + jnp.clip(index_z, 0, count_z - 1)).astype(jnp.int32)

def tile_indices(anchor_x, anchor_y, counts, layers):
    count_x, count_y, count_z = counts
    row_x = parity_nodes(jnp.reshape(anchor_x, (1,)).astype(jnp.int32), BLOCK_X)[first_bits][:, 0]
    row_y = parity_nodes(jnp.reshape(anchor_y, (1,)).astype(jnp.int32), BLOCK_Y)[second_bits][:, 0]
    seg_first = jnp.maximum(jnp.arange(count_z + 1, dtype=jnp.int32) * BLOCK_Z - BLOCK_Z // 2, 0).astype(jnp.int32)
    row_z = parity_nodes(seg_first, BLOCK_Z)[third_bits]
    row_ids = flatten_node(row_x[:, None], row_y[:, None], row_z, counts)
    col_ids = flatten_node(row_x[:, None, None] + jnp.asarray(shift_along_x)[None, :, None], row_y[:, None, None] + jnp.asarray(shift_along_y)[None, :, None], row_z[:, None, :] + jnp.asarray(shift_along_z)[None, :, None], counts)
    entry_ids = (row_ids[None, :, None, :] * (count_x * count_y * count_z) + col_ids[:, None, :, :]).astype(jnp.int32)
    return (entry_ids, row_ids)

def segment_matrix(layers, segment_count):
    seg_of = (jnp.arange(layers, dtype=jnp.int32) + BLOCK_Z // 2) // BLOCK_Z
    return (seg_of[:, None] == jnp.arange(segment_count, dtype=jnp.int32)[None, :]).astype(jnp.float32)

def solve_coarse(coarse, coarse_rhs):
    factor = jnp.linalg.cholesky(coarse)
    middle = lax.linalg.triangular_solve(factor, coarse_rhs[:, None], left_side=True, lower=True)
    return lax.linalg.triangular_solve(factor, middle, left_side=True, lower=True, transpose_a=True)[:, 0]

def reference(facies, source, facies_perm, facies_store, well_x, well_y, well_rate):
    perm_cell = lookup(facies, facies_perm)
    storage = lookup(facies, facies_store)
    trans_all = tuple((harmonic(*split_faces(perm_cell, dim_id)) for dim_id in range(3)))
    diagonal = diagonal_of(storage, trans_all)
    coord_x = jnp.arange(GRID_X, dtype=jnp.int32)
    coord_y = jnp.arange(GRID_Y, dtype=jnp.int32)
    coord_z = jnp.arange(CELLS_Z, dtype=jnp.int32)
    start_x = parity_start(coord_x, BLOCK_X)[first_bits]
    start_y = parity_start(coord_y, BLOCK_Y)[second_bits]
    start_z = parity_start(coord_z, BLOCK_Z)[third_bits]
    basis_now = start_x[:, :, None, None] * start_y[:, None, :, None] * start_z[:, None, None, :]
    same_x8 = parity_same(coord_x, BLOCK_X)[first_bits]
    same_y8 = parity_same(coord_y, BLOCK_Y)[second_bits]
    same_z8 = parity_same(coord_z, BLOCK_Z)[third_bits]

    def change_of(item_set):
        return -RELAX_WEIGHT * cut_apply(item_set[0], storage, trans_all, (item_set[1], item_set[2], item_set[3])) / diagonal
    for sweep_id in range(SWEEPS):
        changes = lax.map(change_of, (basis_now, same_x8, same_y8, same_z8))
        change_sum = jnp.sum(changes, axis=0)
        basis_now = basis_now + changes - basis_now * change_sum[None]
    hit_x = (well_x[:, None] == coord_x[None, :]).astype(jnp.float32)
    hit_y = (well_y[:, None] == coord_y[None, :]).astype(jnp.float32)
    column = jnp.einsum('w,wx,wy->xy', well_rate, hit_x, hit_y, precision=HIGHEST)
    rhs_fine = source + column[:, :, None] / CELLS_Z
    half_x = BLOCK_X // 2
    half_y = BLOCK_Y // 2
    tiles_x = GRID_X // half_x
    tiles_y = GRID_Y // half_y
    zmatrix = segment_matrix(CELLS_Z, SEGMENTS)
    shaped = basis_now.reshape(8, tiles_x, half_x, tiles_y, half_y, CELLS_Z)

    def gram_of(item_set):
        same_three = (item_set[1], item_set[2], item_set[3])
        term_list = [cut_apply(item_set[0], storage, trans_all, same_three)] + rim_terms(item_set[0], trans_all, same_three)
        term_stack = jnp.stack(term_list).reshape(7, tiles_x, half_x, tiles_y, half_y, CELLS_Z)
        gram_tile = jnp.einsum('aipjqz,sipjqz->ijasz', shaped, term_stack, precision=HIGHEST)
        return jnp.einsum('ijasz,zg->ijasg', gram_tile, zmatrix, precision=HIGHEST)
    grams = lax.map(gram_of, (basis_now, same_x8, same_y8, same_z8))
    grams = jnp.transpose(grams, (1, 2, 0, 3, 4, 5))
    counts = (BLOCKS_X, BLOCKS_Y, BLOCKS_Z)

    def indices_for(first_x, first_y):
        return tile_indices(first_x, first_y, counts, CELLS_Z)
    anchors_x = jnp.arange(tiles_x, dtype=jnp.int32) * half_x
    anchors_y = jnp.arange(tiles_y, dtype=jnp.int32) * half_y
    entry_ids, row_ids = jax.vmap(jax.vmap(indices_for, in_axes=(None, 0)), in_axes=(0, None))(anchors_x, anchors_y)
    coarse = jnp.zeros((COARSE * COARSE,), jnp.float32).at[entry_ids.reshape(-1)].add(grams.reshape(-1)).reshape(COARSE, COARSE)
    rhs_tile = jnp.einsum('aipjqz,ipjqz->ijaz', shaped, rhs_fine.reshape(tiles_x, half_x, tiles_y, half_y, CELLS_Z), precision=HIGHEST)
    rhs_tile = jnp.einsum('ijaz,zg->ijag', rhs_tile, zmatrix, precision=HIGHEST)
    coarse_rhs = jnp.zeros((COARSE,), jnp.float32).at[row_ids.reshape(-1)].add(rhs_tile.reshape(-1))
    coarse_solution = solve_coarse(coarse, coarse_rhs)
    values_at = coarse_solution[row_ids]
    per_layer = jnp.einsum('ijag,zg->ijaz', values_at, zmatrix, precision=HIGHEST)
    prolonged = jnp.einsum('aipjqz,ijaz->ipjqz', shaped, per_layer, precision=HIGHEST).reshape(GRID_X, GRID_Y, CELLS_Z)
    ones_all = (jnp.ones((GRID_X - 1,), jnp.float32), jnp.ones((GRID_Y - 1,), jnp.float32), jnp.ones((CELLS_Z - 1,), jnp.float32))
    applied = cut_apply(prolonged, storage, trans_all, ones_all)
    return prolonged + RELAX_WEIGHT * (rhs_fine - applied) / diagonal
```

```python
import jax
import jax.numpy as jnp
import numpy as np
from jax import lax
from jax.experimental import pallas as pl
from jax.experimental.pallas import tpu as pltpu
from jax.sharding import PartitionSpec as P

BLOCK_X = 64
BLOCK_Y = 64
BLOCK_Z = 16
SWEEPS = 3


RELAX_WEIGHT = 2.0 / 3.0
HIGHEST = lax.Precision.HIGHEST
first_bits = np.array([0, 0, 0, 0, 1, 1, 1, 1], dtype=np.int32)
second_bits = np.array([0, 0, 1, 1, 0, 0, 1, 1], dtype=np.int32)
third_bits = np.array([0, 1, 0, 1, 0, 1, 0, 1], dtype=np.int32)
shift_along_x = np.array([0, 2, -2, 0, 0, 0, 0], dtype=np.int32)
shift_along_y = np.array([0, 0, 0, 2, -2, 0, 0], dtype=np.int32)
shift_along_z = np.array([0, 0, 0, 0, 0, 2, -2], dtype=np.int32)


def with_halo(value, sides, width):
    for axis, dim in sides:
        size, length = (lax.axis_size(axis), value.shape[dim])
        up = [(i, (i + 1) % size) for i in range(size - 1)]
        down = [(j, i) for i, j in up]
        last = lax.slice_in_dim(value, length - width, length, axis=dim)
        initial = lax.slice_in_dim(value, 0, width, axis=dim)
        before = lax.ppermute(last, axis, up)
        after = lax.ppermute(initial, axis, down)
        value = jnp.concatenate([before, value, after], axis=dim)
    return value


def support_of(coords, block_size, parity):
    return parity + 2 * jnp.floor_divide(
        coords + block_size // 2 - block_size * parity, 2 * block_size
    )


def parity_nodes(coords, block_size):
    return jnp.stack([support_of(coords, block_size, 0), support_of(coords, block_size, 1)])


def parity_start(coords, block_size):
    node_ids = parity_nodes(coords, block_size)
    return (node_ids == jnp.floor_divide(coords, block_size)[None]).astype(jnp.float32)


def parity_same(coords, block_size):
    node_here = parity_nodes(coords[:-1], block_size)
    node_next = parity_nodes(coords[1:], block_size)
    return (node_here == node_next).astype(jnp.float32)


def harmonic(left_perm, right_perm):
    return 2.0 * left_perm * right_perm / (left_perm + right_perm)


def face_pad(values_in, dim_id, before):
    widths = [(0, 0), (0, 0), (0, 0)]
    widths[dim_id] = (1, 0) if before else (0, 1)
    return jnp.pad(values_in, widths)


def expand(line_in, dim_id):
    new_shape = [1, 1, 1]
    new_shape[dim_id] = line_in.shape[0]
    return line_in.reshape(new_shape)


def split_faces(values_in, dim_id):
    length = values_in.shape[dim_id]
    below_part = lax.slice_in_dim(values_in, 0, length - 1, axis=dim_id)
    above_part = lax.slice_in_dim(values_in, 1, length, axis=dim_id)
    return (below_part, above_part)


def cut_apply(values_in, storage, trans_all, same_all):
    result = storage * values_in
    for dim_id in range(3):
        trans_face = trans_all[dim_id]
        same_line = expand(same_all[dim_id], dim_id)
        below_part, above_part = split_faces(values_in, dim_id)
        result = result + face_pad(
            trans_face * (below_part - same_line * above_part), dim_id, False
        )
        result = result + face_pad(trans_face * (above_part - same_line * below_part), dim_id, True)
    return result


def rim_terms(values_in, trans_all, same_all):
    result = []
    for dim_id in range(3):
        trans_face = trans_all[dim_id]
        cross_mask = 1.0 - expand(same_all[dim_id], dim_id)
        below_part, above_part = split_faces(values_in, dim_id)
        result.append(face_pad(-trans_face * cross_mask * above_part, dim_id, False))
        result.append(face_pad(-trans_face * cross_mask * below_part, dim_id, True))
    return result


def diagonal_of(storage, trans_all):
    result = storage
    for dim_id in range(3):
        result = (
            result
            + face_pad(trans_all[dim_id], dim_id, False)
            + face_pad(trans_all[dim_id], dim_id, True)
        )
    return result


def lookup(facies, code_table):
    result = jnp.zeros(facies.shape, jnp.float32)
    for code_id in range(code_table.shape[0]):
        result = result + jnp.where(facies == code_id, code_table[code_id], 0.0)
    return result


def flatten_node(index_x, index_y, index_z, counts):
    count_x, count_y, count_z = counts
    flat_ids = (
        jnp.clip(index_x, 0, count_x - 1) * count_y + jnp.clip(index_y, 0, count_y - 1)
    ) * count_z
    return (flat_ids + jnp.clip(index_z, 0, count_z - 1)).astype(jnp.int32)


def tile_indices(anchor_x, anchor_y, counts):
    count_x, count_y, count_z = counts
    row_x = parity_nodes(jnp.reshape(anchor_x, (1,)), BLOCK_X)[first_bits][:, 0]
    row_y = parity_nodes(jnp.reshape(anchor_y, (1,)), BLOCK_Y)[second_bits][:, 0]
    seg_first = jnp.maximum(jnp.arange(count_z + 1, dtype=jnp.int32) * BLOCK_Z - BLOCK_Z // 2, 0)
    row_z = parity_nodes(seg_first, BLOCK_Z)[third_bits]
    row_ids = flatten_node(row_x[:, None], row_y[:, None], row_z, counts)
    col_ids = flatten_node(
        row_x[:, None, None] + jnp.asarray(shift_along_x)[None, :, None],
        row_y[:, None, None] + jnp.asarray(shift_along_y)[None, :, None],
        row_z[:, None, :] + jnp.asarray(shift_along_z)[None, :, None],
        counts,
    )
    entry_ids = row_ids[None, :, None, :] * (count_x * count_y * count_z) + col_ids[:, None, :, :]
    return (entry_ids, row_ids)


def segment_matrix(layers, segment_count):
    seg_of = (jnp.arange(layers, dtype=jnp.int32) + BLOCK_Z // 2) // BLOCK_Z
    return (seg_of[:, None] == jnp.arange(segment_count, dtype=jnp.int32)[None, :]).astype(
        jnp.float32
    )


def solve_coarse(coarse, coarse_rhs):
    factor = jnp.linalg.cholesky(coarse)
    middle = lax.linalg.triangular_solve(factor, coarse_rhs[:, None], left_side=True, lower=True)
    return lax.linalg.triangular_solve(
        factor, middle, left_side=True, lower=True, transpose_a=True
    )[:, 0]


def geometry(coeffs, margin, anchor_x, anchor_y, total_x, total_y):
    coord_x = anchor_x - margin + jnp.arange(coeffs.shape[1], dtype=jnp.int32)
    coord_y = anchor_y - margin + jnp.arange(coeffs.shape[2], dtype=jnp.int32)
    coord_z = jnp.arange(coeffs.shape[3], dtype=jnp.int32)
    inside_x = (coord_x >= 0) & (coord_x < total_x)
    inside_y = (coord_y >= 0) & (coord_y < total_y)
    inside = inside_x[:, None, None] & inside_y[None, :, None]
    perm_safe = jnp.where(inside, coeffs[0], 1.0)
    storage = jnp.where(inside, coeffs[1], 1.0)
    valid_x = (inside_x[:-1] & inside_x[1:]).astype(jnp.float32)
    valid_y = (inside_y[:-1] & inside_y[1:]).astype(jnp.float32)
    trans_x = harmonic(perm_safe[:-1], perm_safe[1:]) * valid_x[:, None, None]
    trans_y = harmonic(perm_safe[:, :-1], perm_safe[:, 1:]) * valid_y[None, :, None]
    trans_z = harmonic(perm_safe[:, :, :-1], perm_safe[:, :, 1:])
    trans_all = (trans_x, trans_y, trans_z)
    same_all = (
        parity_same(coord_x, BLOCK_X)[first_bits],
        parity_same(coord_y, BLOCK_Y)[second_bits],
        parity_same(coord_z, BLOCK_Z)[third_bits],
    )
    starts = (
        parity_start(coord_x, BLOCK_X)[first_bits],
        parity_start(coord_y, BLOCK_Y)[second_bits],
        parity_start(coord_z, BLOCK_Z)[third_bits],
    )
    return (storage, trans_all, diagonal_of(storage, trans_all), same_all, starts)


def initial(geo_set):
    start_x, start_y, start_z = geo_set[4]
    return start_x[:, :, None, None] * start_y[:, None, :, None] * start_z[:, None, None, :]


def smooth(basis_ext, geo_set):
    storage, trans_all, diagonal, same_all, starts = geo_set

    def change_of(values_in, same_x, same_y, same_z):
        return (
            -RELAX_WEIGHT
            * cut_apply(values_in, storage, trans_all, (same_x, same_y, same_z))
            / diagonal
        )

    changes = jax.vmap(change_of)(basis_ext, same_all[0], same_all[1], same_all[2])[:, 1:-1, 1:-1]
    interior = basis_ext[:, 1:-1, 1:-1]
    change_sum = jnp.sum(changes, axis=0)
    return interior + changes - interior * change_sum[None]


def basis_halo(basis_now):
    return with_halo(basis_now, (("gx", 1), ("gy", 2)), 1)


def general_step(facies, source, facies_perm, facies_store, well_x, well_y, well_rate):
    tile_x, tile_y, layers = facies.shape
    devs_x = lax.axis_size("gx")
    devs_y = lax.axis_size("gy")
    total_x = tile_x * devs_x
    total_y = tile_y * devs_y
    anchor_x = lax.axis_index("gx") * tile_x
    anchor_y = lax.axis_index("gy") * tile_y
    coeffs = jnp.stack([lookup(facies, facies_perm), lookup(facies, facies_store)])
    coeff_wide = with_halo(coeffs, (("gx", 1), ("gy", 2)), 1)
    geo_one = geometry(coeff_wide, 1, anchor_x, anchor_y, total_x, total_y)
    basis_now = initial(geo_one)[:, 1:-1, 1:-1]
    for sweep_id in range(SWEEPS):
        basis_now = smooth(basis_halo(basis_now), geo_one)
    basis_now = basis_halo(basis_now)
    storage, trans_all, diagonal, same_all, starts = geo_one

    def terms_of(values_in, same_x, same_y, same_z):
        same_three = (same_x, same_y, same_z)
        return jnp.stack(
            [cut_apply(values_in, storage, trans_all, same_three)]
            + rim_terms(values_in, trans_all, same_three)
        )

    term_stack = jax.vmap(terms_of)(basis_now, same_all[0], same_all[1], same_all[2])[
        :, :, 1:-1, 1:-1
    ]
    interior = basis_now[:, 1:-1, 1:-1]
    count_x = total_x // BLOCK_X
    count_y = total_y // BLOCK_Y
    count_z = layers // BLOCK_Z
    counts = (count_x, count_y, count_z)
    coarse_count = count_x * count_y * count_z
    zmatrix = segment_matrix(layers, count_z + 1)
    gram_local = jnp.einsum("apqz,cspqz->casz", interior, term_stack, precision=HIGHEST)
    gram_local = jnp.einsum("casz,zg->casg", gram_local, zmatrix, precision=HIGHEST)
    cell_x = anchor_x + jnp.arange(tile_x, dtype=jnp.int32)
    cell_y = anchor_y + jnp.arange(tile_y, dtype=jnp.int32)
    hit_x = (well_x[:, None] == cell_x[None, :]).astype(jnp.float32)
    hit_y = (well_y[:, None] == cell_y[None, :]).astype(jnp.float32)
    column = jnp.einsum("w,wx,wy->xy", well_rate, hit_x, hit_y, precision=HIGHEST)
    rhs_fine = source + column[:, :, None] / layers
    rhs_local = jnp.einsum("apqz,pqz->az", interior, rhs_fine, precision=HIGHEST)
    rhs_local = jnp.einsum("az,zg->ag", rhs_local, zmatrix, precision=HIGHEST)
    entry_ids, row_ids = tile_indices(anchor_x, anchor_y, counts)
    local_matrix = (
        jnp.zeros((coarse_count * coarse_count,), jnp.float32)
        .at[entry_ids.reshape(-1)]
        .add(gram_local.reshape(-1))
    )
    local_matrix = local_matrix.reshape(coarse_count, coarse_count)
    local_rhs = (
        jnp.zeros((coarse_count,), jnp.float32).at[row_ids.reshape(-1)].add(rhs_local.reshape(-1))
    )
    coarse, coarse_rhs = lax.psum((local_matrix, local_rhs), ("gx", "gy"))
    coarse_solution = solve_coarse(coarse, coarse_rhs)
    values_at = coarse_solution[row_ids]
    per_layer = jnp.einsum("ag,zg->az", values_at, zmatrix, precision=HIGHEST)
    prolonged = jnp.einsum("apqz,az->pqz", interior, per_layer, precision=HIGHEST)
    prolonged_ext = with_halo(prolonged, (("gx", 0), ("gy", 1)), 1)
    ones_all = (
        jnp.ones((tile_x + 1,), jnp.float32),
        jnp.ones((tile_y + 1,), jnp.float32),
        jnp.ones((layers - 1,), jnp.float32),
    )
    applied = cut_apply(prolonged_ext, storage, trans_all, ones_all)[1:-1, 1:-1]
    return prolonged + RELAX_WEIGHT * (rhs_fine - applied) / diagonal[1:-1, 1:-1]


MARGIN = SWEEPS + 1
AXES = ("gx", "gy")
ROWS = 8


def pair_swaps(value, dim, axis, width):
    size, length = (lax.axis_size(axis), value.shape[dim])
    last = lax.slice_in_dim(value, length - width, length, axis=dim)
    first = lax.slice_in_dim(value, 0, width, axis=dim)
    even = lax.axis_index(axis) % 2 == 0
    pairs_near = [(i, i + 1) for i in range(0, size - 1, 2)]
    pairs_far = [(i, i + 1) for i in range(1, size - 1, 2)]
    near = lax.ppermute(
        jnp.where(even, last, first), axis, pairs_near + [(j, i) for i, j in pairs_near]
    )
    far = lax.ppermute(
        jnp.where(even, first, last), axis, pairs_far + [(j, i) for i, j in pairs_far]
    )
    return jnp.where(even, far, near), jnp.where(even, near, far)


def wide_facies(facies):
    before, after = pair_swaps(facies, 1, "gy", MARGIN)
    rows = jnp.concatenate([facies, after, before], axis=1)
    before, after = pair_swaps(rows, 0, "gx", MARGIN)
    return jnp.concatenate([before, rows, after], axis=0)


def lane_iota(shape):
    return lax.broadcasted_iota(jnp.int32, shape, len(shape) - 1)


def face_ends(layer, parity):
    return lax.rem(layer + 1 + BLOCK_Z // 2 + BLOCK_Z * parity, 2 * BLOCK_Z) == 0


def table_select(table_ref, codes):
    result = jnp.full(codes.shape, table_ref[0], jnp.float32)
    for code_id in range(1, table_ref.shape[0]):
        result = jnp.where(codes == code_id, table_ref[code_id], result)
    return result


def basis_kernel(
    facies_ref, source_ref, perm_ref, store_ref, well_x_ref, well_y_ref, well_rate_ref,
    rows_ref, basis_ref, side_ref, rhs_ref, store_out_ref, up_ref, down_ref,
    trans_x, trans_y, trans_z0, trans_z1, scale, storage, field_a, field_b,
):
    planes, rows, layers = facies_ref.shape
    tile_x, tile_y = (source_ref.shape[0], source_ref.shape[1])
    anchor_x = lax.axis_index("gx") * tile_x
    anchor_y = lax.axis_index("gy") * tile_y
    total_x = lax.axis_size("gx") * tile_x
    total_y = lax.axis_size("gy") * tile_y
    shape = (rows, layers)
    layer = lane_iota(shape)
    row = lax.broadcasted_iota(jnp.int32, shape, 0)
    offset_y = jnp.where(row < tile_y + MARGIN, row, row - rows)
    face_y = (
        (anchor_y + offset_y >= 0)
        & (anchor_y + offset_y + 1 < total_y)
        & (row != tile_y + MARGIN - 1)
    )
    top = layer == layers - 1
    ends_0 = face_ends(layer, 0)
    ends_1 = face_ends(layer, 1)
    start = jnp.where(lax.rem(layer // BLOCK_Z, 2) == 0, 1.0, 0.0)

    def row_up(value):
        return pltpu.roll(value, rows - 1, 0)

    def row_down(value):
        return pltpu.roll(value, 1, 0)

    def layer_up(value):
        return pltpu.roll(value, layers - 1, 1)

    def layer_down(value):
        return pltpu.roll(value, 1, 1)

    def coefficients(plane, carry):
        resist, store, face_before = carry
        codes = facies_ref[plane]
        resist_next = 1.0 / table_select(perm_ref, codes)
        store_next = table_select(store_ref, codes)
        here = anchor_x + plane - 1 - MARGIN
        face_x = 2.0 / (resist + resist_next)
        face_x = jnp.where((here >= 0) & (here + 1 < total_x), face_x, 0.0)
        y_face = jnp.where(face_y, 2.0 / (resist + row_up(resist)), 0.0)
        z_face = jnp.where(top, 0.0, 2.0 / (resist + layer_up(resist)))
        diagonal = (
            store + face_x + face_before + y_face + row_down(y_face) + z_face + layer_down(z_face)
        )
        trans_x[plane - 1] = face_x
        trans_y[plane - 1] = y_face
        trans_z0[plane - 1] = jnp.where(ends_0, 0.0, z_face)
        trans_z1[plane - 1] = jnp.where(ends_1, 0.0, z_face)
        scale[plane - 1] = RELAX_WEIGHT / diagonal
        storage[plane - 1] = store
        field_a[plane - 1] = start
        return resist_next, store_next, face_x

    codes = facies_ref[0]
    carry = (
        1.0 / table_select(perm_ref, codes),
        table_select(store_ref, codes),
        jnp.zeros(shape, jnp.float32),
    )
    lax.fori_loop(1, planes, coefficients, carry)
    field_a[planes - 1] = start

    def sweep(old_ref, new_ref, low, high):
        def step(plane, carry):
            here, flux_before = carry
            beyond = old_ref[plane + 1]
            flux = trans_x[plane] * (beyond - here)
            flux_y = trans_y[plane] * (row_up(here) - here)
            above = layer_up(here)
            gain = above * (1.0 - here)
            loss = here * (1.0 - above)
            z0, z1 = (trans_z0[plane], trans_z1[plane])
            total = (flux - flux_before) + (flux_y - row_down(flux_y))
            total = total + (z0 * gain - z1 * loss) + layer_down(z0 * loss - z1 * gain)
            new_ref[plane] = here + scale[plane] * total
            return beyond, flux

        here = old_ref[low]
        lax.fori_loop(low, high, step, (here, trans_x[low - 1] * (here - old_ref[low - 1])))

    refs = (field_a, field_b)
    for sweep_id in range(SWEEPS):
        sweep(
            refs[sweep_id % 2], refs[(sweep_id + 1) % 2], 1 + sweep_id, planes - 1 - sweep_id
        )
    final = refs[SWEEPS % 2]

    tile = (tile_y, layers)
    tile_layer = lane_iota(tile)
    cut_0 = face_ends(tile_layer, 0)
    cut_any = cut_0 | face_ends(tile_layer, 1)
    well_hit_y = (
        lax.broadcasted_iota(jnp.int32, (tile_y, well_y_ref.shape[1]), 0) + anchor_y
        == well_y_ref[...]
    )

    def inner(value):
        return value[:tile_y]

    def gather(plane, sums):
        at = plane + MARGIN
        here_all = final[at]
        here = inner(here_all)
        y_all = trans_y[at]
        flux_y_all = y_all * (row_up(here_all) - here_all)
        step_y = inner(row_up(here_all)) - here
        step_x = inner(final[at + 1]) - here
        flux_x = inner(trans_x[at]) * step_x
        flux_before = inner(trans_x[at - 1]) * (here - inner(final[at - 1]))
        flux_y = inner(flux_y_all)
        z_face = jnp.maximum(inner(trans_z0[at]), inner(trans_z1[at]))
        above = layer_up(here)
        step_z = above - here
        energy_z = z_face * step_z * step_z
        other = 1.0 - here
        store = inner(storage[at])
        factor = inner(scale[at])
        hit = well_hit_y & (well_x_ref[...] == anchor_x + plane)
        column = jnp.sum(jnp.where(hit, well_rate_ref[...], 0.0), axis=1, keepdims=True)
        rhs = source_ref[plane] + column / layers
        below_end = jnp.where(cut_0, here, other)
        above_end = jnp.where(cut_0, above, 1.0 - above)
        z_cut = jnp.where(cut_any, z_face, 0.0)
        basis_ref[plane] = here
        side_ref[plane] = factor * (
            (flux_before - flux_x) + (inner(row_down(flux_y_all)) - flux_y)
        )
        rhs_ref[plane] = factor * rhs
        store_out_ref[plane] = factor * store
        up_ref[plane] = factor * z_face
        down_ref[plane] = factor * layer_down(z_face)
        terms = (
            store * here * here,
            store * here * other,
            store * other * other,
            flux_x * step_x + flux_y * step_y + jnp.where(cut_any, 0.0, energy_z),
            jnp.where(cut_any, energy_z, 0.0),
            z_cut * below_end * below_end,
            z_cut * above_end * above_end,
            z_cut * below_end * above_end,
            here * rhs,
            other * rhs,
        )
        return tuple(total + term for total, term in zip(sums, terms))

    sums = lax.fori_loop(0, tile_x, gather, (jnp.zeros(tile, jnp.float32),) * 10)
    mass_00, mass_01, mass_11, energy, cut, low_2, high_2, low_high, rhs_0, rhs_1 = (
        jnp.sum(total, axis=0, keepdims=True) for total in sums
    )
    line = lane_iota((1, layers))
    ends_0 = face_ends(line, 0)
    ends_1 = face_ends(line, 1)

    def layer_after(value):
        return pltpu.roll(value, 1, 1)

    rows_ref[0:1] = (
        mass_00
        + energy
        + jnp.where(ends_0, low_2, cut)
        + layer_after(jnp.where(ends_0, high_2, 0.0))
    )
    rows_ref[1:2] = (
        mass_11
        + energy
        + jnp.where(ends_1, low_2, cut)
        + layer_after(jnp.where(ends_1, high_2, 0.0))
    )
    rows_ref[2:3] = mass_01 - energy + (low_high - low_2) + layer_after(low_high - high_2)
    rows_ref[3:4] = -low_high
    rows_ref[4:5] = rhs_0
    rows_ref[5:6] = rhs_1
    rows_ref[6:8] = jnp.zeros((2, layers), jnp.float32)


def pressure_kernel(
    rows_ref, basis_ref, side_ref, rhs_ref, store_ref, up_ref, down_ref, out_ref, entries
):
    tile_x, tile_y, layers = basis_ref.shape
    count = layers // BLOCK_Z
    shape = (count, layers)
    node = lax.broadcasted_iota(jnp.int32, shape, 0)
    layer = lane_iota(shape)
    base = node * BLOCK_Z
    half = BLOCK_Z // 2
    inside = (layer >= base - half) & (layer < base + 3 * half)
    even = lax.rem(node, 2) == 0
    rows = REDUCE(rows_ref)
    total = [rows[i : i + 1] for i in range(6)]
    parts = (
        jnp.where(inside, jnp.where(even, total[0], total[1]), 0.0),
        jnp.where((layer >= base + half) & (layer < base + 3 * half), total[2], 0.0),
        jnp.where(layer == base + 3 * half - 1, total[3], 0.0),
        jnp.where(inside, jnp.where(even, total[4], total[5]), 0.0),
    )
    for part_id, part in enumerate(parts):
        entries[part_id] = jnp.broadcast_to(jnp.sum(part, axis=1, keepdims=True), shape)
    diagonal, first, second, right = (
        [entries[part_id, k : k + 1] for k in range(count)] for part_id in range(4)
    )
    inverses, firsts, seconds = ([], [], [])
    for k in range(count):
        inverse = 1.0 / diagonal[k]
        inverses.append(inverse)
        if k + 1 < count:
            lower = first[k] * inverse
            firsts.append(lower)
            diagonal[k + 1] = diagonal[k + 1] - lower * first[k]
            right[k + 1] = right[k + 1] - lower * right[k]
        if k + 2 < count:
            far = second[k] * inverse
            seconds.append(far)
            first[k + 1] = first[k + 1] - firsts[k] * second[k]
            diagonal[k + 2] = diagonal[k + 2] - far * second[k]
            right[k + 2] = right[k + 2] - far * right[k]
    values = [None] * count
    for k in reversed(range(count)):
        value = right[k] * inverses[k]
        if k + 1 < count:
            value = value - firsts[k] * values[k + 1]
        if k + 2 < count:
            value = value - seconds[k] * values[k + 2]
        values[k] = value
    line = lane_iota((1, layers))
    fields = [jnp.zeros((1, layers), jnp.float32)] * 2
    for k in range(count):
        held = (line >= k * BLOCK_Z - half) & (line < k * BLOCK_Z + 3 * half)
        fields[k % 2] = jnp.where(held, values[k], fields[k % 2])
    value_1 = jnp.broadcast_to(fields[1], (tile_y, layers))
    value_0 = jnp.broadcast_to(fields[0], (tile_y, layers))
    apart = value_0 - value_1
    for plane in range(tile_x):
        here = basis_ref[plane]
        prolonged = here * value_0 + (1.0 - here) * value_1
        above = pltpu.roll(prolonged, layers - 1, 1)
        below = pltpu.roll(prolonged, 1, 1)
        applied = (
            store_ref[plane] * prolonged
            + apart * side_ref[plane]
            + up_ref[plane] * (prolonged - above)
            + down_ref[plane] * (prolonged - below)
        )
        out_ref[plane] = prolonged + (rhs_ref[plane] - applied)


def column_step(facies, source, facies_perm, facies_store, well_x, well_y, well_rate):
    tile_x, tile_y, layers = facies.shape
    planes, rows = (tile_x + 2 * MARGIN, tile_y + 2 * MARGIN)
    wide = wide_facies(facies)
    f32 = jnp.float32
    tile = jax.ShapeDtypeStruct(facies.shape, f32)
    vmem = pl.BlockSpec(memory_space=pltpu.VMEM)
    smem = pl.BlockSpec(memory_space=pltpu.SMEM)
    partial, *fields = pl.pallas_call(
        basis_kernel,
        out_shape=(jax.ShapeDtypeStruct((ROWS, layers), f32),) + (tile,) * 6,
        in_specs=[vmem, vmem, smem, smem, vmem, vmem, vmem],
        out_specs=(vmem,) * 7,
        scratch_shapes=[pltpu.VMEM((planes, rows, layers), f32)] * 8,
        compiler_params=pltpu.CompilerParams(vmem_limit_bytes=VMEM_BYTES),
        name="basis",
    )(
        wide,
        source,
        facies_perm,
        facies_store,
        well_x[None, :],
        well_y[None, :],
        well_rate[None, :],
    )
    total = reduce_rows(partial)
    return pl.pallas_call(
        pressure_kernel,
        out_shape=tile,
        in_specs=[vmem] * 7,
        out_specs=vmem,
        scratch_shapes=[pltpu.VMEM((4, layers // BLOCK_Z, layers), f32)],
        compiler_params=pltpu.CompilerParams(vmem_limit_bytes=VMEM_BYTES),
        name="pressure",
    )(total, *fields)


VMEM_BYTES = 16 * 2**20


def REDUCE(rows_ref):
    return rows_ref[...]


def reduce_rows(partial):
    size = lax.axis_size(AXES)
    if size & (size - 1):
        return lax.psum(partial, AXES)
    step = 1
    while step < size:
        partial = partial + lax.ppermute(partial, AXES, [(i, i ^ step) for i in range(size)])
        step *= 2
    return partial


def solution(mesh):
    def per_device(facies, *others):
        tile_x, tile_y, layers = facies.shape
        total_x = tile_x * mesh.shape["gx"]
        total_y = tile_y * mesh.shape["gy"]
        one_column = total_x == BLOCK_X and total_y == BLOCK_Y
        fits = layers % 128 == 0 and tile_y % 8 == 0 and min(tile_x, tile_y) >= MARGIN
        step = column_step if one_column and fits else general_step
        return step(facies, *others)

    in_specs = (P("gx", "gy", None), P("gx", "gy", None), P(), P(), P(), P(), P())
    out_specs = P("gx", "gy", None)
    return jax.shard_map(
        per_device, mesh=mesh, in_specs=in_specs, out_specs=out_specs, check_vma=False
    )
```

```python
import jax
import jax.numpy as jnp
import numpy as np
from jax import lax
from jax.experimental import pallas as pl
from jax.experimental.pallas import tpu as pltpu
from jax.sharding import PartitionSpec as P

BLOCK_X = 64
BLOCK_Y = 64
BLOCK_Z = 16
SWEEPS = 3


RELAX_WEIGHT = 2.0 / 3.0
HIGHEST = lax.Precision.HIGHEST
first_bits = np.array([0, 0, 0, 0, 1, 1, 1, 1], dtype=np.int32)
second_bits = np.array([0, 0, 1, 1, 0, 0, 1, 1], dtype=np.int32)
third_bits = np.array([0, 1, 0, 1, 0, 1, 0, 1], dtype=np.int32)
shift_along_x = np.array([0, 2, -2, 0, 0, 0, 0], dtype=np.int32)
shift_along_y = np.array([0, 0, 0, 2, -2, 0, 0], dtype=np.int32)
shift_along_z = np.array([0, 0, 0, 0, 0, 2, -2], dtype=np.int32)


def with_halo(value, sides, width):
    for axis, dim in sides:
        size, length = (lax.axis_size(axis), value.shape[dim])
        up = [(i, (i + 1) % size) for i in range(size - 1)]
        down = [(j, i) for i, j in up]
        last = lax.slice_in_dim(value, length - width, length, axis=dim)
        initial = lax.slice_in_dim(value, 0, width, axis=dim)
        before = lax.ppermute(last, axis, up)
        after = lax.ppermute(initial, axis, down)
        value = jnp.concatenate([before, value, after], axis=dim)
    return value


def support_of(coords, block_size, parity):
    return parity + 2 * jnp.floor_divide(
        coords + block_size // 2 - block_size * parity, 2 * block_size
    )


def parity_nodes(coords, block_size):
    return jnp.stack([support_of(coords, block_size, 0), support_of(coords, block_size, 1)])


def parity_start(coords, block_size):
    node_ids = parity_nodes(coords, block_size)
    return (node_ids == jnp.floor_divide(coords, block_size)[None]).astype(jnp.float32)


def parity_same(coords, block_size):
    node_here = parity_nodes(coords[:-1], block_size)
    node_next = parity_nodes(coords[1:], block_size)
    return (node_here == node_next).astype(jnp.float32)


def harmonic(left_perm, right_perm):
    return 2.0 * left_perm * right_perm / (left_perm + right_perm)


def face_pad(values_in, dim_id, before):
    widths = [(0, 0), (0, 0), (0, 0)]
    widths[dim_id] = (1, 0) if before else (0, 1)
    return jnp.pad(values_in, widths)


def expand(line_in, dim_id):
    new_shape = [1, 1, 1]
    new_shape[dim_id] = line_in.shape[0]
    return line_in.reshape(new_shape)


def split_faces(values_in, dim_id):
    length = values_in.shape[dim_id]
    below_part = lax.slice_in_dim(values_in, 0, length - 1, axis=dim_id)
    above_part = lax.slice_in_dim(values_in, 1, length, axis=dim_id)
    return (below_part, above_part)


def cut_apply(values_in, storage, trans_all, same_all):
    result = storage * values_in
    for dim_id in range(3):
        trans_face = trans_all[dim_id]
        same_line = expand(same_all[dim_id], dim_id)
        below_part, above_part = split_faces(values_in, dim_id)
        result = result + face_pad(
            trans_face * (below_part - same_line * above_part), dim_id, False
        )
        result = result + face_pad(trans_face * (above_part - same_line * below_part), dim_id, True)
    return result


def rim_terms(values_in, trans_all, same_all):
    result = []
    for dim_id in range(3):
        trans_face = trans_all[dim_id]
        cross_mask = 1.0 - expand(same_all[dim_id], dim_id)
        below_part, above_part = split_faces(values_in, dim_id)
        result.append(face_pad(-trans_face * cross_mask * above_part, dim_id, False))
        result.append(face_pad(-trans_face * cross_mask * below_part, dim_id, True))
    return result


def diagonal_of(storage, trans_all):
    result = storage
    for dim_id in range(3):
        result = (
            result
            + face_pad(trans_all[dim_id], dim_id, False)
            + face_pad(trans_all[dim_id], dim_id, True)
        )
    return result


def lookup(facies, code_table):
    result = jnp.zeros(facies.shape, jnp.float32)
    for code_id in range(code_table.shape[0]):
        result = result + jnp.where(facies == code_id, code_table[code_id], 0.0)
    return result


def flatten_node(index_x, index_y, index_z, counts):
    count_x, count_y, count_z = counts
    flat_ids = (
        jnp.clip(index_x, 0, count_x - 1) * count_y + jnp.clip(index_y, 0, count_y - 1)
    ) * count_z
    return (flat_ids + jnp.clip(index_z, 0, count_z - 1)).astype(jnp.int32)


def tile_indices(anchor_x, anchor_y, counts):
    count_x, count_y, count_z = counts
    row_x = parity_nodes(jnp.reshape(anchor_x, (1,)), BLOCK_X)[first_bits][:, 0]
    row_y = parity_nodes(jnp.reshape(anchor_y, (1,)), BLOCK_Y)[second_bits][:, 0]
    seg_first = jnp.maximum(jnp.arange(count_z + 1, dtype=jnp.int32) * BLOCK_Z - BLOCK_Z // 2, 0)
    row_z = parity_nodes(seg_first, BLOCK_Z)[third_bits]
    row_ids = flatten_node(row_x[:, None], row_y[:, None], row_z, counts)
    col_ids = flatten_node(
        row_x[:, None, None] + jnp.asarray(shift_along_x)[None, :, None],
        row_y[:, None, None] + jnp.asarray(shift_along_y)[None, :, None],
        row_z[:, None, :] + jnp.asarray(shift_along_z)[None, :, None],
        counts,
    )
    entry_ids = row_ids[None, :, None, :] * (count_x * count_y * count_z) + col_ids[:, None, :, :]
    return (entry_ids, row_ids)


def segment_matrix(layers, segment_count):
    seg_of = (jnp.arange(layers, dtype=jnp.int32) + BLOCK_Z // 2) // BLOCK_Z
    return (seg_of[:, None] == jnp.arange(segment_count, dtype=jnp.int32)[None, :]).astype(
        jnp.float32
    )


def solve_coarse(coarse, coarse_rhs):
    factor = jnp.linalg.cholesky(coarse)
    middle = lax.linalg.triangular_solve(factor, coarse_rhs[:, None], left_side=True, lower=True)
    return lax.linalg.triangular_solve(
        factor, middle, left_side=True, lower=True, transpose_a=True
    )[:, 0]


def geometry(coeffs, margin, anchor_x, anchor_y, total_x, total_y):
    coord_x = anchor_x - margin + jnp.arange(coeffs.shape[1], dtype=jnp.int32)
    coord_y = anchor_y - margin + jnp.arange(coeffs.shape[2], dtype=jnp.int32)
    coord_z = jnp.arange(coeffs.shape[3], dtype=jnp.int32)
    inside_x = (coord_x >= 0) & (coord_x < total_x)
    inside_y = (coord_y >= 0) & (coord_y < total_y)
    inside = inside_x[:, None, None] & inside_y[None, :, None]
    perm_safe = jnp.where(inside, coeffs[0], 1.0)
    storage = jnp.where(inside, coeffs[1], 1.0)
    valid_x = (inside_x[:-1] & inside_x[1:]).astype(jnp.float32)
    valid_y = (inside_y[:-1] & inside_y[1:]).astype(jnp.float32)
    trans_x = harmonic(perm_safe[:-1], perm_safe[1:]) * valid_x[:, None, None]
    trans_y = harmonic(perm_safe[:, :-1], perm_safe[:, 1:]) * valid_y[None, :, None]
    trans_z = harmonic(perm_safe[:, :, :-1], perm_safe[:, :, 1:])
    trans_all = (trans_x, trans_y, trans_z)
    same_all = (
        parity_same(coord_x, BLOCK_X)[first_bits],
        parity_same(coord_y, BLOCK_Y)[second_bits],
        parity_same(coord_z, BLOCK_Z)[third_bits],
    )
    starts = (
        parity_start(coord_x, BLOCK_X)[first_bits],
        parity_start(coord_y, BLOCK_Y)[second_bits],
        parity_start(coord_z, BLOCK_Z)[third_bits],
    )
    return (storage, trans_all, diagonal_of(storage, trans_all), same_all, starts)


def initial(geo_set):
    start_x, start_y, start_z = geo_set[4]
    return start_x[:, :, None, None] * start_y[:, None, :, None] * start_z[:, None, None, :]


def smooth(basis_ext, geo_set):
    storage, trans_all, diagonal, same_all, starts = geo_set

    def change_of(values_in, same_x, same_y, same_z):
        return (
            -RELAX_WEIGHT
            * cut_apply(values_in, storage, trans_all, (same_x, same_y, same_z))
            / diagonal
        )

    changes = jax.vmap(change_of)(basis_ext, same_all[0], same_all[1], same_all[2])[:, 1:-1, 1:-1]
    interior = basis_ext[:, 1:-1, 1:-1]
    change_sum = jnp.sum(changes, axis=0)
    return interior + changes - interior * change_sum[None]


def basis_halo(basis_now):
    return with_halo(basis_now, (("gx", 1), ("gy", 2)), 1)


def general_step(facies, source, facies_perm, facies_store, well_x, well_y, well_rate):
    tile_x, tile_y, layers = facies.shape
    devs_x = lax.axis_size("gx")
    devs_y = lax.axis_size("gy")
    total_x = tile_x * devs_x
    total_y = tile_y * devs_y
    anchor_x = lax.axis_index("gx") * tile_x
    anchor_y = lax.axis_index("gy") * tile_y
    coeffs = jnp.stack([lookup(facies, facies_perm), lookup(facies, facies_store)])
    coeff_wide = with_halo(coeffs, (("gx", 1), ("gy", 2)), 1)
    geo_one = geometry(coeff_wide, 1, anchor_x, anchor_y, total_x, total_y)
    basis_now = initial(geo_one)[:, 1:-1, 1:-1]
    for sweep_id in range(SWEEPS):
        basis_now = smooth(basis_halo(basis_now), geo_one)
    basis_now = basis_halo(basis_now)
    storage, trans_all, diagonal, same_all, starts = geo_one

    def terms_of(values_in, same_x, same_y, same_z):
        same_three = (same_x, same_y, same_z)
        return jnp.stack(
            [cut_apply(values_in, storage, trans_all, same_three)]
            + rim_terms(values_in, trans_all, same_three)
        )

    term_stack = jax.vmap(terms_of)(basis_now, same_all[0], same_all[1], same_all[2])[
        :, :, 1:-1, 1:-1
    ]
    interior = basis_now[:, 1:-1, 1:-1]
    count_x = total_x // BLOCK_X
    count_y = total_y // BLOCK_Y
    count_z = layers // BLOCK_Z
    counts = (count_x, count_y, count_z)
    coarse_count = count_x * count_y * count_z
    zmatrix = segment_matrix(layers, count_z + 1)
    gram_local = jnp.einsum("apqz,cspqz->casz", interior, term_stack, precision=HIGHEST)
    gram_local = jnp.einsum("casz,zg->casg", gram_local, zmatrix, precision=HIGHEST)
    cell_x = anchor_x + jnp.arange(tile_x, dtype=jnp.int32)
    cell_y = anchor_y + jnp.arange(tile_y, dtype=jnp.int32)
    hit_x = (well_x[:, None] == cell_x[None, :]).astype(jnp.float32)
    hit_y = (well_y[:, None] == cell_y[None, :]).astype(jnp.float32)
    column = jnp.einsum("w,wx,wy->xy", well_rate, hit_x, hit_y, precision=HIGHEST)
    rhs_fine = source + column[:, :, None] / layers
    rhs_local = jnp.einsum("apqz,pqz->az", interior, rhs_fine, precision=HIGHEST)
    rhs_local = jnp.einsum("az,zg->ag", rhs_local, zmatrix, precision=HIGHEST)
    entry_ids, row_ids = tile_indices(anchor_x, anchor_y, counts)
    local_matrix = (
        jnp.zeros((coarse_count * coarse_count,), jnp.float32)
        .at[entry_ids.reshape(-1)]
        .add(gram_local.reshape(-1))
    )
    local_matrix = local_matrix.reshape(coarse_count, coarse_count)
    local_rhs = (
        jnp.zeros((coarse_count,), jnp.float32).at[row_ids.reshape(-1)].add(rhs_local.reshape(-1))
    )
    coarse, coarse_rhs = lax.psum((local_matrix, local_rhs), ("gx", "gy"))
    coarse_solution = solve_coarse(coarse, coarse_rhs)
    values_at = coarse_solution[row_ids]
    per_layer = jnp.einsum("ag,zg->az", values_at, zmatrix, precision=HIGHEST)
    prolonged = jnp.einsum("apqz,az->pqz", interior, per_layer, precision=HIGHEST)
    prolonged_ext = with_halo(prolonged, (("gx", 0), ("gy", 1)), 1)
    ones_all = (
        jnp.ones((tile_x + 1,), jnp.float32),
        jnp.ones((tile_y + 1,), jnp.float32),
        jnp.ones((layers - 1,), jnp.float32),
    )
    applied = cut_apply(prolonged_ext, storage, trans_all, ones_all)[1:-1, 1:-1]
    return prolonged + RELAX_WEIGHT * (rhs_fine - applied) / diagonal[1:-1, 1:-1]


MARGIN = SWEEPS + 1
AXES = ("gx", "gy")
VMEM_BYTES = 16 * 2**20


def pair_swaps(value, dim, axis, width):
    size, length = (lax.axis_size(axis), value.shape[dim])
    last = lax.slice_in_dim(value, length - width, length, axis=dim)
    first = lax.slice_in_dim(value, 0, width, axis=dim)
    even = lax.axis_index(axis) % 2 == 0
    pairs_near = [(i, i + 1) for i in range(0, size - 1, 2)]
    pairs_far = [(i, i + 1) for i in range(1, size - 1, 2)]
    near = lax.ppermute(
        jnp.where(even, last, first), axis, pairs_near + [(j, i) for i, j in pairs_near]
    )
    far = lax.ppermute(
        jnp.where(even, first, last), axis, pairs_far + [(j, i) for i, j in pairs_far]
    )
    return jnp.where(even, far, near), jnp.where(even, near, far)


def lane_iota(shape):
    return lax.broadcasted_iota(jnp.int32, shape, len(shape) - 1)


def face_ends(layer, parity):
    return lax.rem(layer + 1 + BLOCK_Z // 2 + BLOCK_Z * parity, 2 * BLOCK_Z) == 0


def in_grid(layer, parity, count):
    shifted = layer + BLOCK_Z // 2 + BLOCK_Z * parity
    node = 2 * (shifted // (2 * BLOCK_Z)) - parity
    return (node >= 0) & (node < count)


def up(value, axis):
    return pltpu.roll(value, value.shape[axis] - 1, axis)


def down(value, axis):
    return pltpu.roll(value, 1, axis)


def code_select(table, codes):
    result = jnp.broadcast_to(table[0], codes.shape)
    for code_id in range(1, len(table)):
        result = jnp.where(codes == code_id, table[code_id], result)
    return result


def plane_faces(resist, store, face_y):
    layer = lane_iota(resist.shape)
    y_face = jnp.where(face_y, 2.0 / (resist + up(resist, 0)), 0.0)
    z_face = jnp.where(layer == resist.shape[1] - 1, 0.0, 2.0 / (resist + up(resist, 1)))
    part = store + y_face + down(y_face, 0) + z_face + down(z_face, 1)
    z_faces = [jnp.where(face_ends(layer, parity), 0.0, z_face) for parity in (0, 1)]
    return y_face, z_faces[0], z_faces[1], part


def y_face_mask(shape, tile_y):
    row = lax.broadcasted_iota(jnp.int32, shape, 0)
    place = lax.axis_index("gy") * tile_y + jnp.where(row < tile_y + MARGIN, row, row - shape[0])
    inside = (place >= 0) & (place + 1 < lax.axis_size("gy") * tile_y)
    return inside & (row != tile_y + MARGIN - 1)


def tile_kernel(
    rows_ref, source_ref, perm_ref, store_ref, well_x_ref, well_y_ref, well_rate_ref,
    table_ref, resist_ref, storage_ref, x_ref, y_ref, z0_ref, z1_ref, part_ref, rhs_ref,
):
    tile_x, rows, layers = rows_ref.shape
    tile_y = source_ref.shape[1]
    anchor_x = lax.axis_index("gx") * tile_x
    anchor_y = lax.axis_index("gy") * tile_y
    codes = perm_ref.shape[0]
    resists = [
        1.0 / jnp.full((1, layers), perm_ref[code], jnp.float32) for code in range(codes)
    ]
    stores = [jnp.full((1, layers), store_ref[code], jnp.float32) for code in range(codes)]
    for code in range(codes):
        table_ref[code : code + 1] = resists[code]
        table_ref[codes + code : codes + code + 1] = stores[code]
    face_y = y_face_mask((rows, layers), tile_y)
    hit_y = (
        lax.broadcasted_iota(jnp.int32, (tile_y, well_y_ref.shape[1]), 0) + anchor_y
        == well_y_ref[...]
    )
    before = None
    for plane in range(tile_x):
        resist = code_select(resists, rows_ref[plane])
        store = code_select(stores, rows_ref[plane])
        y_face, z0, z1, part = plane_faces(resist, store, face_y)
        resist_ref[plane] = resist
        storage_ref[plane] = store
        y_ref[plane] = y_face
        z0_ref[plane] = z0
        z1_ref[plane] = z1
        part_ref[plane] = part
        if plane:
            x_ref[plane - 1] = 2.0 / (before + resist)
        before = resist
        hit = hit_y & (well_x_ref[...] == anchor_x + plane)
        column = jnp.sum(jnp.where(hit, well_rate_ref[...], 0.0), axis=1, keepdims=True)
        rhs_ref[plane] = source_ref[plane] + column / layers


def basis_kernel(
    before_ref, after_ref,
    table_ref, resist_ref, storage_ref, x_ref, y_ref, z0_ref, z1_ref, part_ref, rhs_ref,
    packed_ref, basis_ref, side_ref, rhs_out_ref, store_out_ref, up_ref, down_ref,
    scale, field_a, field_b, x_far, y_far, z0_far, z1_far, sums_ref,
):
    tile_x, tile_y, layers = rhs_ref.shape
    rows = resist_ref.shape[1]
    planes = tile_x + 2 * MARGIN
    shape = (rows, layers)
    anchor_x = lax.axis_index("gx") * tile_x
    total_x = lax.axis_size("gx") * tile_x
    face_y = y_face_mask(shape, tile_y)
    codes = table_ref.shape[0] // 2
    table = [table_ref[i : i + 1] for i in range(2 * codes)]
    start = jnp.where(lax.rem(lane_iota(shape) // BLOCK_Z, 2) == 0, 1.0, 0.0)

    def own(plane):
        return MARGIN <= plane < MARGIN + tile_x

    def face_x(plane):
        inner = own(plane) and own(plane + 1)
        return x_ref[plane - MARGIN] if inner else x_far[plane]

    def other_face(near, far, plane):
        return near[plane - MARGIN] if own(plane) else far[plane]

    resist_last = None
    x_last = None
    part_last = None
    for plane in range(planes):
        if own(plane):
            resist = resist_ref[plane - MARGIN]
            part = part_ref[plane - MARGIN]
        else:
            strip = before_ref if plane < MARGIN else after_ref
            facies = strip[plane if plane < MARGIN else plane - MARGIN - tile_x]
            resist = code_select(table[:codes], facies)
            store = code_select(table[codes:], facies)
            y_far[plane], z0_far[plane], z1_far[plane], part = plane_faces(resist, store, face_y)
        if plane:
            if own(plane - 1) and own(plane):
                x_face = face_x(plane - 1)
            else:
                here = anchor_x + plane - 1 - MARGIN
                x_face = 2.0 / (resist_last + resist)
                x_face = jnp.where((here >= 0) & (here + 1 < total_x), x_face, 0.0)
                x_far[plane - 1] = x_face
            if plane > 1:
                scale[plane - 1] = RELAX_WEIGHT / (part_last + x_face + x_last)
            x_last = x_face
        resist_last, part_last = (resist, part)

    def sweep(read, new_ref, low, high):
        here = read(low)
        flux_before = face_x(low - 1) * (here - read(low - 1))
        for plane in range(low, high):
            beyond = read(plane + 1)
            flux = face_x(plane) * (beyond - here)
            flux_y = other_face(y_ref, y_far, plane) * (up(here, 0) - here)
            above = up(here, 1)
            gain = above * (1.0 - here)
            loss = here * (1.0 - above)
            z0 = other_face(z0_ref, z0_far, plane)
            z1 = other_face(z1_ref, z1_far, plane)
            total = (flux - flux_before) + (flux_y - down(flux_y, 0))
            total = total + (z0 * gain - z1 * loss) + down(z0 * loss - z1 * gain, 1)
            new_ref[plane] = here + scale[plane] * total
            here, flux_before = (beyond, flux)

    fields = (field_a, field_b)
    read = lambda plane: start
    for sweep_id in range(SWEEPS):
        target = fields[sweep_id % 2]
        sweep(read, target, 1 + sweep_id, planes - 1 - sweep_id)
        read = lambda plane, ref=target: ref[plane]

    tile = (tile_y, layers)
    cut_0 = face_ends(lane_iota(tile), 0)
    cut_any = cut_0 | face_ends(lane_iota(tile), 1)

    def inner(value):
        return value[:tile_y]

    sums = None
    for plane in range(tile_x):
        at = plane + MARGIN
        here_all = read(at)
        here = inner(here_all)
        step_y_all = up(here_all, 0) - here_all
        flux_y_all = y_ref[plane] * step_y_all
        flux_y = inner(flux_y_all)
        step_x = inner(read(at + 1)) - here
        flux_x = inner(face_x(at)) * step_x
        flux_before = inner(face_x(at - 1)) * (here - inner(read(at - 1)))
        z_face = jnp.maximum(inner(z0_ref[plane]), inner(z1_ref[plane]))
        above = up(here, 1)
        step_z = above - here
        energy_z = z_face * step_z * step_z
        other = 1.0 - here
        store = inner(storage_ref[plane])
        factor = inner(scale[at])
        rhs = rhs_ref[plane]
        below_end = jnp.where(cut_0, here, other)
        above_end = jnp.where(cut_0, above, 1.0 - above)
        z_cut = jnp.where(cut_any, z_face, 0.0)
        basis_ref[plane] = here
        side_ref[plane] = factor * (
            (flux_before - flux_x) + (inner(down(flux_y_all, 0)) - flux_y)
        )
        rhs_out_ref[plane] = factor * rhs
        store_out_ref[plane] = factor * store
        up_ref[plane] = factor * z_face
        down_ref[plane] = factor * down(z_face, 1)
        terms = (
            store * here * here,
            store * here * other,
            store * other * other,
            flux_x * step_x + flux_y * inner(step_y_all) + jnp.where(cut_any, 0.0, energy_z),
            jnp.where(cut_any, energy_z, 0.0),
            z_cut * below_end * below_end,
            z_cut * above_end * above_end,
            z_cut * below_end * above_end,
            here * rhs,
            other * rhs,
        )
        sums = terms if sums is None else [a + b for a, b in zip(sums, terms)]
    mass_00, mass_01, mass_11, energy, cut, low_2, high_2, low_high, rhs_0, rhs_1 = (
        jnp.sum(total, axis=0, keepdims=True) for total in sums
    )
    line = lane_iota((1, layers))
    count = layers // BLOCK_Z
    ends = (face_ends(line, 0), face_ends(line, 1))
    inside = (in_grid(line, 0, count), in_grid(line, 1, count))
    for parity, mass, right in ((0, mass_00, rhs_0), (1, mass_11, rhs_1)):
        own_end = jnp.where(ends[parity], low_2, cut)
        beyond_end = down(jnp.where(ends[parity], high_2, 0.0), 1)
        entry = mass + energy + own_end + beyond_end
        sums_ref[parity : parity + 1] = jnp.where(inside[parity], entry, 0.0)
        sums_ref[4 + parity : 5 + parity] = jnp.where(inside[parity], right, 0.0)
    sums_ref[2:3] = mass_01 - energy + (low_high - low_2) + down(low_high - high_2, 1)
    sums_ref[3:4] = -low_high
    sums_ref[6:8] = jnp.zeros((2, layers), jnp.float32)
    window = pltpu.roll(sums_ref[...], 0, 1, stride=1, stride_axis=0)
    width = 1
    while width < BLOCK_Z:
        window = window + pltpu.roll(window, width, 1)
        width *= 2
    row = lax.broadcasted_iota(jnp.int32, window.shape, 0)
    keep = lax.rem(lane_iota(window.shape) + layers - BLOCK_Z // 2 + 1 - row, BLOCK_Z) == 0
    packed = jnp.sum(jnp.where(keep, window, 0.0), axis=0, keepdims=True)
    packed_ref[...] = jnp.broadcast_to(packed, packed_ref.shape)


def pressure_kernel(
    rows_ref, basis_ref, side_ref, rhs_ref, store_ref, up_ref, down_ref, out_ref, entries
):
    tile_x, tile_y, layers = basis_ref.shape
    count = layers // BLOCK_Z
    half = BLOCK_Z // 2
    shape = (count, layers)
    node = lax.broadcasted_iota(jnp.int32, shape, 0)
    layer = lane_iota(shape)
    packed = jnp.sum(rows_ref[...], axis=0, keepdims=True)

    def held(segment, kind):
        return layer == lax.rem(segment * BLOCK_Z + half - 1 + kind, layers)

    parity = lax.rem(node, 2)
    own = held(node, parity) | held(node + 1, parity)
    right = held(node, parity + 4) | held(node + 1, parity + 4)
    masks = (own, held(node + 1, 2), held(node + 1, 3), right)
    for part_id, mask in enumerate(masks):
        part = jnp.where(mask, packed, 0.0)
        entries[part_id] = jnp.broadcast_to(jnp.sum(part, axis=1, keepdims=True), shape)
    diagonal, first, second, right = (
        [entries[part_id, k : k + 1] for k in range(count)] for part_id in range(4)
    )
    inverses, firsts, seconds = ([], [], [])
    for k in range(count):
        inverse = 1.0 / diagonal[k]
        inverses.append(inverse)
        if k + 1 < count:
            lower = first[k] * inverse
            firsts.append(lower)
            diagonal[k + 1] = diagonal[k + 1] - lower * first[k]
            right[k + 1] = right[k + 1] - lower * right[k]
        if k + 2 < count:
            far = second[k] * inverse
            seconds.append(far)
            first[k + 1] = first[k + 1] - firsts[k] * second[k]
            diagonal[k + 2] = diagonal[k + 2] - far * second[k]
            right[k + 2] = right[k + 2] - far * right[k]
    values = [None] * count
    for k in reversed(range(count)):
        value = right[k] * inverses[k]
        if k + 1 < count:
            value = value - firsts[k] * values[k + 1]
        if k + 2 < count:
            value = value - seconds[k] * values[k + 2]
        values[k] = value
    line = lane_iota((1, layers))
    fields = [jnp.zeros((1, layers), jnp.float32)] * 2
    for k in range(count):
        support = (line >= k * BLOCK_Z - half) & (line < k * BLOCK_Z + 3 * half)
        fields[k % 2] = jnp.where(support, values[k], fields[k % 2])
    value_0 = jnp.broadcast_to(fields[0], (tile_y, layers))
    value_1 = jnp.broadcast_to(fields[1], (tile_y, layers))
    apart = value_0 - value_1
    for plane in range(tile_x):
        here = basis_ref[plane]
        prolonged = here * value_0 + (1.0 - here) * value_1
        applied = (
            store_ref[plane] * prolonged
            + apart * side_ref[plane]
            + up_ref[plane] * (prolonged - up(prolonged, 1))
            + down_ref[plane] * (prolonged - down(prolonged, 1))
        )
        out_ref[plane] = prolonged + (rhs_ref[plane] - applied)


def column_step(facies, source, facies_perm, facies_store, well_x, well_y, well_rate):
    tile_x, tile_y, layers = facies.shape
    rows = tile_y + 2 * MARGIN
    planes = tile_x + 2 * MARGIN
    size = lax.axis_size(AXES)
    f32 = jnp.float32
    tile = jax.ShapeDtypeStruct(facies.shape, f32)
    wide = jax.ShapeDtypeStruct((tile_x, rows, layers), f32)
    vmem = pl.BlockSpec(memory_space=pltpu.VMEM)
    smem = pl.BlockSpec(memory_space=pltpu.SMEM)
    params = pltpu.CompilerParams(vmem_limit_bytes=VMEM_BYTES)

    before, after = pair_swaps(facies, 1, "gy", MARGIN)
    own = jnp.concatenate([facies, after, before], axis=1)
    before, after = pair_swaps(own, 0, "gx", MARGIN)
    near = pl.pallas_call(
        tile_kernel,
        out_shape=(jax.ShapeDtypeStruct((2 * facies_perm.shape[0], layers), f32),)
        + (wide,) * 7
        + (tile,),
        in_specs=[vmem, vmem, smem, smem, vmem, vmem, vmem],
        out_specs=(vmem,) * 9,
        compiler_params=params,
        cost_estimate=pl.CostEstimate(flops=3000000, bytes_accessed=1000000, transcendentals=0),
        name="tile",
    )(
        own,
        source,
        facies_perm,
        facies_store,
        well_x[None, :],
        well_y[None, :],
        well_rate[None, :],
    )
    copies, *fields = pl.pallas_call(
        basis_kernel,
        out_shape=(jax.ShapeDtypeStruct((size, layers), f32),) + (tile,) * 6,
        in_specs=[vmem] * 11,
        out_specs=(vmem,) * 7,
        scratch_shapes=[pltpu.VMEM((planes, rows, layers), f32)] * 7
        + [pltpu.VMEM((8, layers), f32)],
        compiler_params=params,
        name="basis",
    )(before, after, *near)
    everyone = lax.all_to_all(copies, AXES, 0, 0, tiled=True)
    return pl.pallas_call(
        pressure_kernel,
        out_shape=tile,
        in_specs=[vmem] * 7,
        out_specs=vmem,
        scratch_shapes=[pltpu.VMEM((4, layers // BLOCK_Z, layers), f32)],
        compiler_params=params,
        name="pressure",
    )(everyone, *fields)


def solution(mesh):
    def per_device(facies, *others):
        tile_x, tile_y, layers = facies.shape
        total_x = tile_x * mesh.shape["gx"]
        total_y = tile_y * mesh.shape["gy"]
        one_column = total_x == BLOCK_X and total_y == BLOCK_Y
        fits = layers % 128 == 0 and tile_y % 8 == 0 and min(tile_x, tile_y) >= MARGIN
        step = column_step if one_column and fits else general_step
        return step(facies, *others)

    in_specs = (P("gx", "gy", None), P("gx", "gy", None), P(), P(), P(), P(), P())
    out_specs = P("gx", "gy", None)
    return jax.shard_map(
        per_device, mesh=mesh, in_specs=in_specs, out_specs=out_specs, check_vma=False
    )
```

```python
import jax
import jax.numpy as jnp
import numpy as np
from jax import lax
from jax.experimental import pallas as pl
from jax.experimental.pallas import tpu as pltpu
from jax.sharding import PartitionSpec as P

BLOCK_X = 64
BLOCK_Y = 64
BLOCK_Z = 16
SWEEPS = 3


RELAX_WEIGHT = 2.0 / 3.0
HIGHEST = lax.Precision.HIGHEST
first_bits = np.array([0, 0, 0, 0, 1, 1, 1, 1], dtype=np.int32)
second_bits = np.array([0, 0, 1, 1, 0, 0, 1, 1], dtype=np.int32)
third_bits = np.array([0, 1, 0, 1, 0, 1, 0, 1], dtype=np.int32)
shift_along_x = np.array([0, 2, -2, 0, 0, 0, 0], dtype=np.int32)
shift_along_y = np.array([0, 0, 0, 2, -2, 0, 0], dtype=np.int32)
shift_along_z = np.array([0, 0, 0, 0, 0, 2, -2], dtype=np.int32)


def with_halo(value, sides, width):
    for axis, dim in sides:
        size, length = (lax.axis_size(axis), value.shape[dim])
        up = [(i, (i + 1) % size) for i in range(size - 1)]
        down = [(j, i) for i, j in up]
        last = lax.slice_in_dim(value, length - width, length, axis=dim)
        initial = lax.slice_in_dim(value, 0, width, axis=dim)
        before = lax.ppermute(last, axis, up)
        after = lax.ppermute(initial, axis, down)
        value = jnp.concatenate([before, value, after], axis=dim)
    return value


def support_of(coords, block_size, parity):
    return parity + 2 * jnp.floor_divide(
        coords + block_size // 2 - block_size * parity, 2 * block_size
    )


def parity_nodes(coords, block_size):
    return jnp.stack([support_of(coords, block_size, 0), support_of(coords, block_size, 1)])


def parity_start(coords, block_size):
    node_ids = parity_nodes(coords, block_size)
    return (node_ids == jnp.floor_divide(coords, block_size)[None]).astype(jnp.float32)


def parity_same(coords, block_size):
    node_here = parity_nodes(coords[:-1], block_size)
    node_next = parity_nodes(coords[1:], block_size)
    return (node_here == node_next).astype(jnp.float32)


def harmonic(left_perm, right_perm):
    return 2.0 * left_perm * right_perm / (left_perm + right_perm)


def face_pad(values_in, dim_id, before):
    widths = [(0, 0), (0, 0), (0, 0)]
    widths[dim_id] = (1, 0) if before else (0, 1)
    return jnp.pad(values_in, widths)


def expand(line_in, dim_id):
    new_shape = [1, 1, 1]
    new_shape[dim_id] = line_in.shape[0]
    return line_in.reshape(new_shape)


def split_faces(values_in, dim_id):
    length = values_in.shape[dim_id]
    below_part = lax.slice_in_dim(values_in, 0, length - 1, axis=dim_id)
    above_part = lax.slice_in_dim(values_in, 1, length, axis=dim_id)
    return (below_part, above_part)


def cut_apply(values_in, storage, trans_all, same_all):
    result = storage * values_in
    for dim_id in range(3):
        trans_face = trans_all[dim_id]
        same_line = expand(same_all[dim_id], dim_id)
        below_part, above_part = split_faces(values_in, dim_id)
        result = result + face_pad(
            trans_face * (below_part - same_line * above_part), dim_id, False
        )
        result = result + face_pad(trans_face * (above_part - same_line * below_part), dim_id, True)
    return result


def rim_terms(values_in, trans_all, same_all):
    result = []
    for dim_id in range(3):
        trans_face = trans_all[dim_id]
        cross_mask = 1.0 - expand(same_all[dim_id], dim_id)
        below_part, above_part = split_faces(values_in, dim_id)
        result.append(face_pad(-trans_face * cross_mask * above_part, dim_id, False))
        result.append(face_pad(-trans_face * cross_mask * below_part, dim_id, True))
    return result


def diagonal_of(storage, trans_all):
    result = storage
    for dim_id in range(3):
        result = (
            result
            + face_pad(trans_all[dim_id], dim_id, False)
            + face_pad(trans_all[dim_id], dim_id, True)
        )
    return result


def lookup(facies, code_table):
    result = jnp.zeros(facies.shape, jnp.float32)
    for code_id in range(code_table.shape[0]):
        result = result + jnp.where(facies == code_id, code_table[code_id], 0.0)
    return result


def flatten_node(index_x, index_y, index_z, counts):
    count_x, count_y, count_z = counts
    flat_ids = (
        jnp.clip(index_x, 0, count_x - 1) * count_y + jnp.clip(index_y, 0, count_y - 1)
    ) * count_z
    return (flat_ids + jnp.clip(index_z, 0, count_z - 1)).astype(jnp.int32)


def tile_indices(anchor_x, anchor_y, counts):
    count_x, count_y, count_z = counts
    row_x = parity_nodes(jnp.reshape(anchor_x, (1,)), BLOCK_X)[first_bits][:, 0]
    row_y = parity_nodes(jnp.reshape(anchor_y, (1,)), BLOCK_Y)[second_bits][:, 0]
    seg_first = jnp.maximum(jnp.arange(count_z + 1, dtype=jnp.int32) * BLOCK_Z - BLOCK_Z // 2, 0)
    row_z = parity_nodes(seg_first, BLOCK_Z)[third_bits]
    row_ids = flatten_node(row_x[:, None], row_y[:, None], row_z, counts)
    col_ids = flatten_node(
        row_x[:, None, None] + jnp.asarray(shift_along_x)[None, :, None],
        row_y[:, None, None] + jnp.asarray(shift_along_y)[None, :, None],
        row_z[:, None, :] + jnp.asarray(shift_along_z)[None, :, None],
        counts,
    )
    entry_ids = row_ids[None, :, None, :] * (count_x * count_y * count_z) + col_ids[:, None, :, :]
    return (entry_ids, row_ids)


def segment_matrix(layers, segment_count):
    seg_of = (jnp.arange(layers, dtype=jnp.int32) + BLOCK_Z // 2) // BLOCK_Z
    return (seg_of[:, None] == jnp.arange(segment_count, dtype=jnp.int32)[None, :]).astype(
        jnp.float32
    )


def solve_coarse(coarse, coarse_rhs):
    factor = jnp.linalg.cholesky(coarse)
    middle = lax.linalg.triangular_solve(factor, coarse_rhs[:, None], left_side=True, lower=True)
    return lax.linalg.triangular_solve(
        factor, middle, left_side=True, lower=True, transpose_a=True
    )[:, 0]


def geometry(coeffs, margin, anchor_x, anchor_y, total_x, total_y):
    coord_x = anchor_x - margin + jnp.arange(coeffs.shape[1], dtype=jnp.int32)
    coord_y = anchor_y - margin + jnp.arange(coeffs.shape[2], dtype=jnp.int32)
    coord_z = jnp.arange(coeffs.shape[3], dtype=jnp.int32)
    inside_x = (coord_x >= 0) & (coord_x < total_x)
    inside_y = (coord_y >= 0) & (coord_y < total_y)
    inside = inside_x[:, None, None] & inside_y[None, :, None]
    perm_safe = jnp.where(inside, coeffs[0], 1.0)
    storage = jnp.where(inside, coeffs[1], 1.0)
    valid_x = (inside_x[:-1] & inside_x[1:]).astype(jnp.float32)
    valid_y = (inside_y[:-1] & inside_y[1:]).astype(jnp.float32)
    trans_x = harmonic(perm_safe[:-1], perm_safe[1:]) * valid_x[:, None, None]
    trans_y = harmonic(perm_safe[:, :-1], perm_safe[:, 1:]) * valid_y[None, :, None]
    trans_z = harmonic(perm_safe[:, :, :-1], perm_safe[:, :, 1:])
    trans_all = (trans_x, trans_y, trans_z)
    same_all = (
        parity_same(coord_x, BLOCK_X)[first_bits],
        parity_same(coord_y, BLOCK_Y)[second_bits],
        parity_same(coord_z, BLOCK_Z)[third_bits],
    )
    starts = (
        parity_start(coord_x, BLOCK_X)[first_bits],
        parity_start(coord_y, BLOCK_Y)[second_bits],
        parity_start(coord_z, BLOCK_Z)[third_bits],
    )
    return (storage, trans_all, diagonal_of(storage, trans_all), same_all, starts)


def initial(geo_set):
    start_x, start_y, start_z = geo_set[4]
    return start_x[:, :, None, None] * start_y[:, None, :, None] * start_z[:, None, None, :]


def smooth(basis_ext, geo_set):
    storage, trans_all, diagonal, same_all, _ = geo_set

    def change_of(values_in, same_x, same_y, same_z):
        return (
            -RELAX_WEIGHT
            * cut_apply(values_in, storage, trans_all, (same_x, same_y, same_z))
            / diagonal
        )

    changes = jax.vmap(change_of)(basis_ext, same_all[0], same_all[1], same_all[2])[:, 1:-1, 1:-1]
    interior = basis_ext[:, 1:-1, 1:-1]
    change_sum = jnp.sum(changes, axis=0)
    return interior + changes - interior * change_sum[None]


def basis_halo(basis_now):
    return with_halo(basis_now, (("gx", 1), ("gy", 2)), 1)


def general_step(facies, source, facies_perm, facies_store, well_x, well_y, well_rate):
    tile_x, tile_y, layers = facies.shape
    devs_x = lax.axis_size("gx")
    devs_y = lax.axis_size("gy")
    total_x = tile_x * devs_x
    total_y = tile_y * devs_y
    anchor_x = lax.axis_index("gx") * tile_x
    anchor_y = lax.axis_index("gy") * tile_y
    coeffs = jnp.stack([lookup(facies, facies_perm), lookup(facies, facies_store)])
    coeff_wide = with_halo(coeffs, (("gx", 1), ("gy", 2)), 1)
    geo_one = geometry(coeff_wide, 1, anchor_x, anchor_y, total_x, total_y)
    basis_now = initial(geo_one)[:, 1:-1, 1:-1]
    for _ in range(SWEEPS):
        basis_now = smooth(basis_halo(basis_now), geo_one)
    basis_now = basis_halo(basis_now)
    storage, trans_all, diagonal, same_all, _ = geo_one

    def terms_of(values_in, same_x, same_y, same_z):
        same_three = (same_x, same_y, same_z)
        return jnp.stack(
            [cut_apply(values_in, storage, trans_all, same_three)]
            + rim_terms(values_in, trans_all, same_three)
        )

    term_stack = jax.vmap(terms_of)(basis_now, same_all[0], same_all[1], same_all[2])[
        :, :, 1:-1, 1:-1
    ]
    interior = basis_now[:, 1:-1, 1:-1]
    count_x = total_x // BLOCK_X
    count_y = total_y // BLOCK_Y
    count_z = layers // BLOCK_Z
    counts = (count_x, count_y, count_z)
    coarse_count = count_x * count_y * count_z
    zmatrix = segment_matrix(layers, count_z + 1)
    gram_local = jnp.einsum("apqz,cspqz->casz", interior, term_stack, precision=HIGHEST)
    gram_local = jnp.einsum("casz,zg->casg", gram_local, zmatrix, precision=HIGHEST)
    cell_x = anchor_x + jnp.arange(tile_x, dtype=jnp.int32)
    cell_y = anchor_y + jnp.arange(tile_y, dtype=jnp.int32)
    hit_x = (well_x[:, None] == cell_x[None, :]).astype(jnp.float32)
    hit_y = (well_y[:, None] == cell_y[None, :]).astype(jnp.float32)
    column = jnp.einsum("w,wx,wy->xy", well_rate, hit_x, hit_y, precision=HIGHEST)
    rhs_fine = source + column[:, :, None] / layers
    rhs_local = jnp.einsum("apqz,pqz->az", interior, rhs_fine, precision=HIGHEST)
    rhs_local = jnp.einsum("az,zg->ag", rhs_local, zmatrix, precision=HIGHEST)
    entry_ids, row_ids = tile_indices(anchor_x, anchor_y, counts)
    local_matrix = (
        jnp.zeros((coarse_count * coarse_count,), jnp.float32)
        .at[entry_ids.reshape(-1)]
        .add(gram_local.reshape(-1))
    )
    local_matrix = local_matrix.reshape(coarse_count, coarse_count)
    local_rhs = (
        jnp.zeros((coarse_count,), jnp.float32).at[row_ids.reshape(-1)].add(rhs_local.reshape(-1))
    )
    coarse, coarse_rhs = lax.psum((local_matrix, local_rhs), ("gx", "gy"))
    coarse_solution = solve_coarse(coarse, coarse_rhs)
    values_at = coarse_solution[row_ids]
    per_layer = jnp.einsum("ag,zg->az", values_at, zmatrix, precision=HIGHEST)
    prolonged = jnp.einsum("apqz,az->pqz", interior, per_layer, precision=HIGHEST)
    prolonged_ext = with_halo(prolonged, (("gx", 0), ("gy", 1)), 1)
    ones_all = (
        jnp.ones((tile_x + 1,), jnp.float32),
        jnp.ones((tile_y + 1,), jnp.float32),
        jnp.ones((layers - 1,), jnp.float32),
    )
    applied = cut_apply(prolonged_ext, storage, trans_all, ones_all)[1:-1, 1:-1]
    return prolonged + RELAX_WEIGHT * (rhs_fine - applied) / diagonal[1:-1, 1:-1]


MARGIN = SWEEPS + 1
AXES = ("gx", "gy")
VMEM_BYTES = 16 * 2**20


def named_permute(value, axis, pairs):
    return lax.ppermute(value, axis, pairs + [(j, i) for i, j in pairs])


def pair_swaps(value, dim, axis, width):
    size, length = (lax.axis_size(axis), value.shape[dim])
    last = lax.slice_in_dim(value, length - width, length, axis=dim)
    first = lax.slice_in_dim(value, 0, width, axis=dim)
    even = lax.axis_index(axis) % 2 == 0
    pairs_near = [(i, i + 1) for i in range(0, size - 1, 2)]
    pairs_far = [(i, i + 1) for i in range(1, size - 1, 2)]
    far = named_permute(jnp.where(even, first, last), axis, pairs_far)
    near = named_permute(jnp.where(even, last, first), axis, pairs_near)
    return jnp.where(even, far, near), jnp.where(even, near, far)


def lane_iota(shape):
    return lax.broadcasted_iota(jnp.int32, shape, len(shape) - 1)


def face_ends(layer, parity):
    return lax.rem(layer + 1 + BLOCK_Z // 2 + BLOCK_Z * parity, 2 * BLOCK_Z) == 0


def in_grid(layer, parity, count):
    shifted = layer + BLOCK_Z // 2 + BLOCK_Z * parity
    node = 2 * (shifted // (2 * BLOCK_Z)) - parity
    return (node >= 0) & (node < count)


def up(value, axis):
    return pltpu.roll(value, value.shape[axis] - 1, axis)


def down(value, axis):
    return pltpu.roll(value, 1, axis)


def code_select(table, codes):
    result = jnp.broadcast_to(table[0], codes.shape)
    for code_id in range(1, len(table)):
        result = jnp.where(codes == code_id, table[code_id], result)
    return result


def plane_faces(resist, store, face_y):
    layer = lane_iota(resist.shape)
    y_face = jnp.where(face_y, 2.0 / (resist + up(resist, 0)), 0.0)
    z_face = jnp.where(layer == resist.shape[1] - 1, 0.0, 2.0 / (resist + up(resist, 1)))
    part = store + y_face + down(y_face, 0) + z_face + down(z_face, 1)
    z_faces = [jnp.where(face_ends(layer, parity), 0.0, z_face) for parity in (0, 1)]
    return y_face, z_faces[0], z_faces[1], part


def y_face_mask(shape, tile_y):
    row = lax.broadcasted_iota(jnp.int32, shape, 0)
    place = lax.axis_index("gy") * tile_y + jnp.where(row < tile_y + MARGIN, row, row - shape[0])
    inside = (place >= 0) & (place + 1 < lax.axis_size("gy") * tile_y)
    return inside & (row != tile_y + MARGIN - 1)


def tile_kernel(
    rows_ref, source_ref, perm_ref, store_ref, well_x_ref, well_y_ref, well_rate_ref,
    table_ref, resist_ref, storage_ref, x_ref, y_ref, z0_ref, z1_ref, part_ref, rhs_ref,
):
    tile_x, rows, layers = rows_ref.shape
    tile_y = source_ref.shape[1]
    anchor_x = lax.axis_index("gx") * tile_x
    anchor_y = lax.axis_index("gy") * tile_y
    codes = perm_ref.shape[0]
    resists = [
        1.0 / jnp.full((1, layers), perm_ref[code], jnp.float32) for code in range(codes)
    ]
    stores = [jnp.full((1, layers), store_ref[code], jnp.float32) for code in range(codes)]
    for code in range(codes):
        table_ref[code : code + 1] = resists[code]
        table_ref[codes + code : codes + code + 1] = stores[code]
    face_y = y_face_mask((rows, layers), tile_y)
    hit_y = (
        lax.broadcasted_iota(jnp.int32, (tile_y, well_y_ref.shape[1]), 0) + anchor_y
        == well_y_ref[...]
    )
    before = None
    for plane in range(tile_x):
        resist = code_select(resists, rows_ref[plane])
        store = code_select(stores, rows_ref[plane])
        y_face, z0, z1, part = plane_faces(resist, store, face_y)
        resist_ref[plane] = resist
        storage_ref[plane] = store
        y_ref[plane] = y_face
        z0_ref[plane] = z0
        z1_ref[plane] = z1
        part_ref[plane] = part
        if plane:
            x_ref[plane - 1] = 2.0 / (before + resist)
        before = resist
        hit = hit_y & (well_x_ref[...] == anchor_x + plane)
        column = jnp.sum(jnp.where(hit, well_rate_ref[...], 0.0), axis=1, keepdims=True)
        rhs_ref[plane] = source_ref[plane] + column / layers


def basis_kernel(
    before_ref, after_ref,
    table_ref, resist_ref, storage_ref, x_ref, y_ref, z0_ref, z1_ref, part_ref, rhs_ref,
    packed_ref, basis_ref, side_ref, rhs_out_ref, store_out_ref, up_ref, down_ref,
    scale, field_a, field_b, x_far, y_far, z0_far, z1_far, sums_ref,
):
    tile_x, tile_y, layers = rhs_ref.shape
    rows = resist_ref.shape[1]
    planes = tile_x + 2 * MARGIN
    shape = (rows, layers)
    anchor_x = lax.axis_index("gx") * tile_x
    total_x = lax.axis_size("gx") * tile_x
    face_y = y_face_mask(shape, tile_y)
    codes = table_ref.shape[0] // 2
    table = [table_ref[i : i + 1] for i in range(2 * codes)]
    start = jnp.where(lax.rem(lane_iota(shape) // BLOCK_Z, 2) == 0, 1.0, 0.0)

    def own(plane):
        return MARGIN <= plane < MARGIN + tile_x

    def face_x(plane):
        inner = own(plane) and own(plane + 1)
        return x_ref[plane - MARGIN] if inner else x_far[plane]

    def other_face(near, far, plane):
        return near[plane - MARGIN] if own(plane) else far[plane]

    resist_last = None
    x_last = None
    part_last = None
    for plane in range(planes):
        if own(plane):
            resist = resist_ref[plane - MARGIN]
            part = part_ref[plane - MARGIN]
        else:
            strip = before_ref if plane < MARGIN else after_ref
            facies = strip[plane if plane < MARGIN else plane - MARGIN - tile_x]
            resist = code_select(table[:codes], facies)
            store = code_select(table[codes:], facies)
            y_far[plane], z0_far[plane], z1_far[plane], part = plane_faces(resist, store, face_y)
        if plane:
            if own(plane - 1) and own(plane):
                x_face = face_x(plane - 1)
            else:
                here = anchor_x + plane - 1 - MARGIN
                x_face = 2.0 / (resist_last + resist)
                x_face = jnp.where((here >= 0) & (here + 1 < total_x), x_face, 0.0)
                x_far[plane - 1] = x_face
            if plane > 1:
                scale[plane - 1] = RELAX_WEIGHT / (part_last + x_face + x_last)
            x_last = x_face
        resist_last, part_last = (resist, part)

    def sweep(read, new_ref, low, high):
        here = read(low)
        flux_before = face_x(low - 1) * (here - read(low - 1))
        for plane in range(low, high):
            beyond = read(plane + 1)
            flux = face_x(plane) * (beyond - here)
            flux_y = other_face(y_ref, y_far, plane) * (up(here, 0) - here)
            above = up(here, 1)
            gain = above * (1.0 - here)
            loss = here * (1.0 - above)
            z0 = other_face(z0_ref, z0_far, plane)
            z1 = other_face(z1_ref, z1_far, plane)
            total = (flux - flux_before) + (flux_y - down(flux_y, 0))
            total = total + (z0 * gain - z1 * loss) + down(z0 * loss - z1 * gain, 1)
            new_ref[plane] = here + scale[plane] * total
            here, flux_before = (beyond, flux)

    fields = (field_a, field_b)
    read = lambda plane: start
    for sweep_id in range(SWEEPS):
        target = fields[sweep_id % 2]
        sweep(read, target, 1 + sweep_id, planes - 1 - sweep_id)
        read = lambda plane, ref=target: ref[plane]

    tile = (tile_y, layers)
    cut_0 = face_ends(lane_iota(tile), 0)
    cut_any = cut_0 | face_ends(lane_iota(tile), 1)

    def inner(value):
        return value[:tile_y]

    sums = None
    for plane in range(tile_x):
        at = plane + MARGIN
        here_all = read(at)
        here = inner(here_all)
        step_y_all = up(here_all, 0) - here_all
        flux_y_all = y_ref[plane] * step_y_all
        flux_y = inner(flux_y_all)
        step_x = inner(read(at + 1)) - here
        flux_x = inner(face_x(at)) * step_x
        flux_before = inner(face_x(at - 1)) * (here - inner(read(at - 1)))
        z_face = jnp.maximum(inner(z0_ref[plane]), inner(z1_ref[plane]))
        above = up(here, 1)
        step_z = above - here
        energy_z = z_face * step_z * step_z
        other = 1.0 - here
        store = inner(storage_ref[plane])
        factor = inner(scale[at])
        rhs = rhs_ref[plane]
        below_end = jnp.where(cut_0, here, other)
        above_end = jnp.where(cut_0, above, 1.0 - above)
        z_cut = jnp.where(cut_any, z_face, 0.0)
        basis_ref[plane] = here
        side_ref[plane] = factor * (
            (flux_before - flux_x) + (inner(down(flux_y_all, 0)) - flux_y)
        )
        rhs_out_ref[plane] = factor * rhs
        store_out_ref[plane] = factor * store
        up_ref[plane] = factor * z_face
        down_ref[plane] = factor * down(z_face, 1)
        terms = (
            store * here * here,
            store * here * other,
            store * other * other,
            flux_x * step_x + flux_y * inner(step_y_all) + jnp.where(cut_any, 0.0, energy_z),
            jnp.where(cut_any, energy_z, 0.0),
            z_cut * below_end * below_end,
            z_cut * above_end * above_end,
            z_cut * below_end * above_end,
            here * rhs,
            other * rhs,
        )
        sums = terms if sums is None else [a + b for a, b in zip(sums, terms)]
    mass_00, mass_01, mass_11, energy, cut, low_2, high_2, low_high, rhs_0, rhs_1 = (
        jnp.sum(total, axis=0, keepdims=True) for total in sums
    )
    line = lane_iota((1, layers))
    count = layers // BLOCK_Z
    ends = (face_ends(line, 0), face_ends(line, 1))
    inside = (in_grid(line, 0, count), in_grid(line, 1, count))
    for parity, mass, right in ((0, mass_00, rhs_0), (1, mass_11, rhs_1)):
        own_end = jnp.where(ends[parity], low_2, cut)
        beyond_end = down(jnp.where(ends[parity], high_2, 0.0), 1)
        entry = mass + energy + own_end + beyond_end
        sums_ref[parity : parity + 1] = jnp.where(inside[parity], entry, 0.0)
        sums_ref[4 + parity : 5 + parity] = jnp.where(inside[parity], right, 0.0)
    sums_ref[2:3] = mass_01 - energy + (low_high - low_2) + down(low_high - high_2, 1)
    sums_ref[3:4] = -low_high
    sums_ref[6:8] = jnp.zeros((2, layers), jnp.float32)
    window = pltpu.roll(sums_ref[...], 0, 1, stride=1, stride_axis=0)
    width = 1
    while width < BLOCK_Z:
        window = window + pltpu.roll(window, width, 1)
        width *= 2
    row = lax.broadcasted_iota(jnp.int32, window.shape, 0)
    keep = lax.rem(lane_iota(window.shape) + layers - BLOCK_Z // 2 + 1 - row, BLOCK_Z) == 0
    packed = jnp.sum(jnp.where(keep, window, 0.0), axis=0, keepdims=True)
    packed_ref[...] = jnp.broadcast_to(packed, packed_ref.shape)


def pressure_kernel(
    rows_ref, basis_ref, side_ref, rhs_ref, store_ref, up_ref, down_ref, out_ref, entries
):
    tile_x, tile_y, layers = basis_ref.shape
    count = layers // BLOCK_Z
    half = BLOCK_Z // 2
    shape = (count, layers)
    node = lax.broadcasted_iota(jnp.int32, shape, 0)
    layer = lane_iota(shape)
    packed = jnp.sum(rows_ref[...], axis=0, keepdims=True)

    def held(segment, kind):
        return layer == lax.rem(segment * BLOCK_Z + half - 1 + kind, layers)

    parity = lax.rem(node, 2)
    own = held(node, parity) | held(node + 1, parity)
    right = held(node, parity + 4) | held(node + 1, parity + 4)
    masks = (own, held(node + 1, 2), held(node + 1, 3), right)
    for part_id, mask in enumerate(masks):
        part = jnp.where(mask, packed, 0.0)
        entries[part_id] = jnp.broadcast_to(jnp.sum(part, axis=1, keepdims=True), shape)
    diagonal, first, second, right = (
        [entries[part_id, k : k + 1] for k in range(count)] for part_id in range(4)
    )
    inverses, firsts, seconds = ([], [], [])
    for k in range(count):
        inverse = 1.0 / diagonal[k]
        inverses.append(inverse)
        if k + 1 < count:
            lower = first[k] * inverse
            firsts.append(lower)
            diagonal[k + 1] = diagonal[k + 1] - lower * first[k]
            right[k + 1] = right[k + 1] - lower * right[k]
        if k + 2 < count:
            far = second[k] * inverse
            seconds.append(far)
            first[k + 1] = first[k + 1] - firsts[k] * second[k]
            diagonal[k + 2] = diagonal[k + 2] - far * second[k]
            right[k + 2] = right[k + 2] - far * right[k]
    values = [None] * count
    for k in reversed(range(count)):
        value = right[k] * inverses[k]
        if k + 1 < count:
            value = value - firsts[k] * values[k + 1]
        if k + 2 < count:
            value = value - seconds[k] * values[k + 2]
        values[k] = value
    line = lane_iota((1, layers))
    fields = [jnp.zeros((1, layers), jnp.float32)] * 2
    for k in range(count):
        support = (line >= k * BLOCK_Z - half) & (line < k * BLOCK_Z + 3 * half)
        fields[k % 2] = jnp.where(support, values[k], fields[k % 2])
    value_0 = jnp.broadcast_to(fields[0], (tile_y, layers))
    value_1 = jnp.broadcast_to(fields[1], (tile_y, layers))
    apart = value_0 - value_1
    for plane in range(tile_x):
        here = basis_ref[plane]
        prolonged = here * value_0 + (1.0 - here) * value_1
        applied = (
            store_ref[plane] * prolonged
            + apart * side_ref[plane]
            + up_ref[plane] * (prolonged - up(prolonged, 1))
            + down_ref[plane] * (prolonged - down(prolonged, 1))
        )
        out_ref[plane] = prolonged + (rhs_ref[plane] - applied)


def column_step(facies, source, facies_perm, facies_store, well_x, well_y, well_rate):
    tile_x, tile_y, layers = facies.shape
    rows = tile_y + 2 * MARGIN
    planes = tile_x + 2 * MARGIN
    size = lax.axis_size(AXES)
    f32 = jnp.float32
    tile = jax.ShapeDtypeStruct(facies.shape, f32)
    wide = jax.ShapeDtypeStruct((tile_x, rows, layers), f32)
    vmem = pl.BlockSpec(memory_space=pltpu.VMEM)
    smem = pl.BlockSpec(memory_space=pltpu.SMEM)
    params = pltpu.CompilerParams(vmem_limit_bytes=VMEM_BYTES)

    before, after = pair_swaps(facies, 1, "gy", MARGIN)
    own = jnp.concatenate([facies, after, before], axis=1)
    before, after = pair_swaps(own, 0, "gx", MARGIN)
    near = pl.pallas_call(
        tile_kernel,
        out_shape=(jax.ShapeDtypeStruct((2 * facies_perm.shape[0], layers), f32),)
        + (wide,) * 7
        + (tile,),
        in_specs=[vmem, vmem, smem, smem, vmem, vmem, vmem],
        out_specs=(vmem,) * 9,
        compiler_params=params,
        cost_estimate=pl.CostEstimate(flops=3000000, bytes_accessed=1000000, transcendentals=0),
        name="tile",
    )(
        own,
        source,
        facies_perm,
        facies_store,
        well_x[None, :],
        well_y[None, :],
        well_rate[None, :],
    )
    copies, *fields = pl.pallas_call(
        basis_kernel,
        out_shape=(jax.ShapeDtypeStruct((size, layers), f32),) + (tile,) * 6,
        in_specs=[vmem] * 11,
        out_specs=(vmem,) * 7,
        scratch_shapes=[pltpu.VMEM((planes, rows, layers), f32)] * 7
        + [pltpu.VMEM((8, layers), f32)],
        compiler_params=params,
        name="basis",
    )(before, after, *near)
    everyone = lax.all_to_all(copies, AXES, 0, 0, tiled=True)
    return pl.pallas_call(
        pressure_kernel,
        out_shape=tile,
        in_specs=[vmem] * 7,
        out_specs=vmem,
        scratch_shapes=[pltpu.VMEM((4, layers // BLOCK_Z, layers), f32)],
        compiler_params=params,
        name="pressure",
    )(everyone, *fields)


def solution(mesh):
    def per_device(facies, *others):
        tile_x, tile_y, layers = facies.shape
        total_x = tile_x * mesh.shape["gx"]
        total_y = tile_y * mesh.shape["gy"]
        one_column = total_x == BLOCK_X and total_y == BLOCK_Y
        fits = layers % 128 == 0 and tile_y % 8 == 0 and min(tile_x, tile_y) >= MARGIN
        step = column_step if one_column and fits else general_step
        return step(facies, *others)

    in_specs = (P("gx", "gy", None), P("gx", "gy", None), P(), P(), P(), P(), P())
    out_specs = P("gx", "gy", None)
    return jax.shard_map(
        per_device, mesh=mesh, in_specs=in_specs, out_specs=out_specs, check_vma=False
    )
```

```python
import jax
import jax.numpy as jnp
import numpy as np
from jax import lax
from jax.experimental import pallas as pl
from jax.experimental.pallas import tpu as pltpu
from jax.sharding import PartitionSpec as P

BLOCK_X = 64
BLOCK_Y = 64
BLOCK_Z = 16
SWEEPS = 3


RELAX_WEIGHT = 2.0 / 3.0
HIGHEST = lax.Precision.HIGHEST
first_bits = np.array([0, 0, 0, 0, 1, 1, 1, 1], dtype=np.int32)
second_bits = np.array([0, 0, 1, 1, 0, 0, 1, 1], dtype=np.int32)
third_bits = np.array([0, 1, 0, 1, 0, 1, 0, 1], dtype=np.int32)
shift_along_x = np.array([0, 2, -2, 0, 0, 0, 0], dtype=np.int32)
shift_along_y = np.array([0, 0, 0, 2, -2, 0, 0], dtype=np.int32)
shift_along_z = np.array([0, 0, 0, 0, 0, 2, -2], dtype=np.int32)


def with_halo(value, sides, width):
    for axis, dim in sides:
        size, length = (lax.axis_size(axis), value.shape[dim])
        up = [(i, (i + 1) % size) for i in range(size - 1)]
        down = [(j, i) for i, j in up]
        last = lax.slice_in_dim(value, length - width, length, axis=dim)
        initial = lax.slice_in_dim(value, 0, width, axis=dim)
        before = lax.ppermute(last, axis, up)
        after = lax.ppermute(initial, axis, down)
        value = jnp.concatenate([before, value, after], axis=dim)
    return value


def support_of(coords, block_size, parity):
    return parity + 2 * jnp.floor_divide(
        coords + block_size // 2 - block_size * parity, 2 * block_size
    )


def parity_nodes(coords, block_size):
    return jnp.stack([support_of(coords, block_size, 0), support_of(coords, block_size, 1)])


def parity_start(coords, block_size):
    node_ids = parity_nodes(coords, block_size)
    return (node_ids == jnp.floor_divide(coords, block_size)[None]).astype(jnp.float32)


def parity_same(coords, block_size):
    node_here = parity_nodes(coords[:-1], block_size)
    node_next = parity_nodes(coords[1:], block_size)
    return (node_here == node_next).astype(jnp.float32)


def harmonic(left_perm, right_perm):
    return 2.0 * left_perm * right_perm / (left_perm + right_perm)


def face_pad(values_in, dim_id, before):
    widths = [(0, 0), (0, 0), (0, 0)]
    widths[dim_id] = (1, 0) if before else (0, 1)
    return jnp.pad(values_in, widths)


def expand(line_in, dim_id):
    new_shape = [1, 1, 1]
    new_shape[dim_id] = line_in.shape[0]
    return line_in.reshape(new_shape)


def split_faces(values_in, dim_id):
    length = values_in.shape[dim_id]
    below_part = lax.slice_in_dim(values_in, 0, length - 1, axis=dim_id)
    above_part = lax.slice_in_dim(values_in, 1, length, axis=dim_id)
    return (below_part, above_part)


def cut_apply(values_in, storage, trans_all, same_all):
    result = storage * values_in
    for dim_id in range(3):
        trans_face = trans_all[dim_id]
        same_line = expand(same_all[dim_id], dim_id)
        below_part, above_part = split_faces(values_in, dim_id)
        result = result + face_pad(
            trans_face * (below_part - same_line * above_part), dim_id, False
        )
        result = result + face_pad(trans_face * (above_part - same_line * below_part), dim_id, True)
    return result


def rim_terms(values_in, trans_all, same_all):
    result = []
    for dim_id in range(3):
        trans_face = trans_all[dim_id]
        cross_mask = 1.0 - expand(same_all[dim_id], dim_id)
        below_part, above_part = split_faces(values_in, dim_id)
        result.append(face_pad(-trans_face * cross_mask * above_part, dim_id, False))
        result.append(face_pad(-trans_face * cross_mask * below_part, dim_id, True))
    return result


def diagonal_of(storage, trans_all):
    result = storage
    for dim_id in range(3):
        result = (
            result
            + face_pad(trans_all[dim_id], dim_id, False)
            + face_pad(trans_all[dim_id], dim_id, True)
        )
    return result


def lookup(facies, code_table):
    result = jnp.zeros(facies.shape, jnp.float32)
    for code_id in range(code_table.shape[0]):
        result = result + jnp.where(facies == code_id, code_table[code_id], 0.0)
    return result


def flatten_node(index_x, index_y, index_z, counts):
    count_x, count_y, count_z = counts
    flat_ids = (
        jnp.clip(index_x, 0, count_x - 1) * count_y + jnp.clip(index_y, 0, count_y - 1)
    ) * count_z
    return (flat_ids + jnp.clip(index_z, 0, count_z - 1)).astype(jnp.int32)


def tile_indices(anchor_x, anchor_y, counts):
    count_x, count_y, count_z = counts
    row_x = parity_nodes(jnp.reshape(anchor_x, (1,)), BLOCK_X)[first_bits][:, 0]
    row_y = parity_nodes(jnp.reshape(anchor_y, (1,)), BLOCK_Y)[second_bits][:, 0]
    seg_first = jnp.maximum(jnp.arange(count_z + 1, dtype=jnp.int32) * BLOCK_Z - BLOCK_Z // 2, 0)
    row_z = parity_nodes(seg_first, BLOCK_Z)[third_bits]
    row_ids = flatten_node(row_x[:, None], row_y[:, None], row_z, counts)
    col_ids = flatten_node(
        row_x[:, None, None] + jnp.asarray(shift_along_x)[None, :, None],
        row_y[:, None, None] + jnp.asarray(shift_along_y)[None, :, None],
        row_z[:, None, :] + jnp.asarray(shift_along_z)[None, :, None],
        counts,
    )
    entry_ids = row_ids[None, :, None, :] * (count_x * count_y * count_z) + col_ids[:, None, :, :]
    return (entry_ids, row_ids)


def segment_matrix(layers, segment_count):
    seg_of = (jnp.arange(layers, dtype=jnp.int32) + BLOCK_Z // 2) // BLOCK_Z
    return (seg_of[:, None] == jnp.arange(segment_count, dtype=jnp.int32)[None, :]).astype(
        jnp.float32
    )


def solve_coarse(coarse, coarse_rhs):
    factor = jnp.linalg.cholesky(coarse)
    middle = lax.linalg.triangular_solve(factor, coarse_rhs[:, None], left_side=True, lower=True)
    return lax.linalg.triangular_solve(
        factor, middle, left_side=True, lower=True, transpose_a=True
    )[:, 0]


def geometry(coeffs, margin, anchor_x, anchor_y, total_x, total_y):
    coord_x = anchor_x - margin + jnp.arange(coeffs.shape[1], dtype=jnp.int32)
    coord_y = anchor_y - margin + jnp.arange(coeffs.shape[2], dtype=jnp.int32)
    coord_z = jnp.arange(coeffs.shape[3], dtype=jnp.int32)
    inside_x = (coord_x >= 0) & (coord_x < total_x)
    inside_y = (coord_y >= 0) & (coord_y < total_y)
    inside = inside_x[:, None, None] & inside_y[None, :, None]
    perm_safe = jnp.where(inside, coeffs[0], 1.0)
    storage = jnp.where(inside, coeffs[1], 1.0)
    valid_x = (inside_x[:-1] & inside_x[1:]).astype(jnp.float32)
    valid_y = (inside_y[:-1] & inside_y[1:]).astype(jnp.float32)
    trans_x = harmonic(perm_safe[:-1], perm_safe[1:]) * valid_x[:, None, None]
    trans_y = harmonic(perm_safe[:, :-1], perm_safe[:, 1:]) * valid_y[None, :, None]
    trans_z = harmonic(perm_safe[:, :, :-1], perm_safe[:, :, 1:])
    trans_all = (trans_x, trans_y, trans_z)
    same_all = (
        parity_same(coord_x, BLOCK_X)[first_bits],
        parity_same(coord_y, BLOCK_Y)[second_bits],
        parity_same(coord_z, BLOCK_Z)[third_bits],
    )
    starts = (
        parity_start(coord_x, BLOCK_X)[first_bits],
        parity_start(coord_y, BLOCK_Y)[second_bits],
        parity_start(coord_z, BLOCK_Z)[third_bits],
    )
    return (storage, trans_all, diagonal_of(storage, trans_all), same_all, starts)


def initial(geo_set):
    start_x, start_y, start_z = geo_set[4]
    return start_x[:, :, None, None] * start_y[:, None, :, None] * start_z[:, None, None, :]


def smooth(basis_ext, geo_set):
    storage, trans_all, diagonal, same_all, _ = geo_set

    def change_of(values_in, same_x, same_y, same_z):
        return (
            -RELAX_WEIGHT
            * cut_apply(values_in, storage, trans_all, (same_x, same_y, same_z))
            / diagonal
        )

    changes = jax.vmap(change_of)(basis_ext, same_all[0], same_all[1], same_all[2])[:, 1:-1, 1:-1]
    interior = basis_ext[:, 1:-1, 1:-1]
    change_sum = jnp.sum(changes, axis=0)
    return interior + changes - interior * change_sum[None]


def basis_halo(basis_now):
    return with_halo(basis_now, (("gx", 1), ("gy", 2)), 1)


def general_step(facies, source, facies_perm, facies_store, well_x, well_y, well_rate):
    tile_x, tile_y, layers = facies.shape
    devs_x = lax.axis_size("gx")
    devs_y = lax.axis_size("gy")
    total_x = tile_x * devs_x
    total_y = tile_y * devs_y
    anchor_x = lax.axis_index("gx") * tile_x
    anchor_y = lax.axis_index("gy") * tile_y
    coeffs = jnp.stack([lookup(facies, facies_perm), lookup(facies, facies_store)])
    coeff_wide = with_halo(coeffs, (("gx", 1), ("gy", 2)), 1)
    geo_one = geometry(coeff_wide, 1, anchor_x, anchor_y, total_x, total_y)
    basis_now = initial(geo_one)[:, 1:-1, 1:-1]
    for _ in range(SWEEPS):
        basis_now = smooth(basis_halo(basis_now), geo_one)
    basis_now = basis_halo(basis_now)
    storage, trans_all, diagonal, same_all, _ = geo_one

    def terms_of(values_in, same_x, same_y, same_z):
        same_three = (same_x, same_y, same_z)
        return jnp.stack(
            [cut_apply(values_in, storage, trans_all, same_three)]
            + rim_terms(values_in, trans_all, same_three)
        )

    term_stack = jax.vmap(terms_of)(basis_now, same_all[0], same_all[1], same_all[2])[
        :, :, 1:-1, 1:-1
    ]
    interior = basis_now[:, 1:-1, 1:-1]
    count_x = total_x // BLOCK_X
    count_y = total_y // BLOCK_Y
    count_z = layers // BLOCK_Z
    counts = (count_x, count_y, count_z)
    coarse_count = count_x * count_y * count_z
    zmatrix = segment_matrix(layers, count_z + 1)
    gram_local = jnp.einsum("apqz,cspqz->casz", interior, term_stack, precision=HIGHEST)
    gram_local = jnp.einsum("casz,zg->casg", gram_local, zmatrix, precision=HIGHEST)
    cell_x = anchor_x + jnp.arange(tile_x, dtype=jnp.int32)
    cell_y = anchor_y + jnp.arange(tile_y, dtype=jnp.int32)
    hit_x = (well_x[:, None] == cell_x[None, :]).astype(jnp.float32)
    hit_y = (well_y[:, None] == cell_y[None, :]).astype(jnp.float32)
    column = jnp.einsum("w,wx,wy->xy", well_rate, hit_x, hit_y, precision=HIGHEST)
    rhs_fine = source + column[:, :, None] / layers
    rhs_local = jnp.einsum("apqz,pqz->az", interior, rhs_fine, precision=HIGHEST)
    rhs_local = jnp.einsum("az,zg->ag", rhs_local, zmatrix, precision=HIGHEST)
    entry_ids, row_ids = tile_indices(anchor_x, anchor_y, counts)
    local_matrix = (
        jnp.zeros((coarse_count * coarse_count,), jnp.float32)
        .at[entry_ids.reshape(-1)]
        .add(gram_local.reshape(-1))
    )
    local_matrix = local_matrix.reshape(coarse_count, coarse_count)
    local_rhs = (
        jnp.zeros((coarse_count,), jnp.float32).at[row_ids.reshape(-1)].add(rhs_local.reshape(-1))
    )
    coarse, coarse_rhs = lax.psum((local_matrix, local_rhs), ("gx", "gy"))
    coarse_solution = solve_coarse(coarse, coarse_rhs)
    values_at = coarse_solution[row_ids]
    per_layer = jnp.einsum("ag,zg->az", values_at, zmatrix, precision=HIGHEST)
    prolonged = jnp.einsum("apqz,az->pqz", interior, per_layer, precision=HIGHEST)
    prolonged_ext = with_halo(prolonged, (("gx", 0), ("gy", 1)), 1)
    ones_all = (
        jnp.ones((tile_x + 1,), jnp.float32),
        jnp.ones((tile_y + 1,), jnp.float32),
        jnp.ones((layers - 1,), jnp.float32),
    )
    applied = cut_apply(prolonged_ext, storage, trans_all, ones_all)[1:-1, 1:-1]
    return prolonged + RELAX_WEIGHT * (rhs_fine - applied) / diagonal[1:-1, 1:-1]


MARGIN = SWEEPS + 1
AXES = ("gx", "gy")
VMEM_BYTES = 16 * 2**20


def swap_along(value, axis, first):
    sizes = {name_: lax.axis_size(name_) for name_ in AXES}
    other = AXES[1 - AXES.index(axis)]
    pairs = []
    for gx in range(sizes[AXES[0]]):
        for gy in range(sizes[AXES[1]]):
            place = {AXES[0]: gx, AXES[1]: gy}
            partner = dict(place)
            along = first + ((place[axis] - first) ^ 1) if place[axis] >= first else -1
            if 0 <= along < sizes[axis]:
                partner[axis] = along
            else:
                partner[other] = place[other] ^ 1
            if partner[other] < sizes[other]:
                pairs.append(tuple(p[AXES[0]] * sizes[AXES[1]] + p[AXES[1]] for p in (place, partner)))
    return lax.ppermute(value, AXES, pairs)


def pair_swaps(value, dim, axis, width):
    length = value.shape[dim]
    last = lax.slice_in_dim(value, length - width, length, axis=dim)
    first = lax.slice_in_dim(value, 0, width, axis=dim)
    even = lax.axis_index(axis) % 2 == 0
    far = swap_along(jnp.where(even, first, last), axis, 1)
    near = swap_along(jnp.where(even, last, first), axis, 0)
    return jnp.where(even, far, near), jnp.where(even, near, far)


def lane_iota(shape):
    return lax.broadcasted_iota(jnp.int32, shape, len(shape) - 1)


def face_ends(layer, parity):
    return lax.rem(layer + 1 + BLOCK_Z // 2 + BLOCK_Z * parity, 2 * BLOCK_Z) == 0


def in_grid(layer, parity, count):
    shifted = layer + BLOCK_Z // 2 + BLOCK_Z * parity
    node = 2 * (shifted // (2 * BLOCK_Z)) - parity
    return (node >= 0) & (node < count)


def up(value, axis):
    return pltpu.roll(value, value.shape[axis] - 1, axis)


def down(value, axis):
    return pltpu.roll(value, 1, axis)


def code_select(table, codes):
    result = jnp.broadcast_to(table[0], codes.shape)
    for code_id in range(1, len(table)):
        result = jnp.where(codes == code_id, table[code_id], result)
    return result


def plane_faces(resist, store, face_y):
    layer = lane_iota(resist.shape)
    y_face = jnp.where(face_y, 2.0 / (resist + up(resist, 0)), 0.0)
    z_face = jnp.where(layer == resist.shape[1] - 1, 0.0, 2.0 / (resist + up(resist, 1)))
    part = store + y_face + down(y_face, 0) + z_face + down(z_face, 1)
    z_faces = [jnp.where(face_ends(layer, parity), 0.0, z_face) for parity in (0, 1)]
    return y_face, z_faces[0], z_faces[1], part


def y_face_mask(shape, tile_y):
    row = lax.broadcasted_iota(jnp.int32, shape, 0)
    place = lax.axis_index("gy") * tile_y + jnp.where(row < tile_y + MARGIN, row, row - shape[0])
    inside = (place >= 0) & (place + 1 < lax.axis_size("gy") * tile_y)
    return inside & (row != tile_y + MARGIN - 1)


def sweep_planes(low, high, read, write, face_x, face_y, face_z, scale):
    if low >= high:
        return
    here = read(low)
    flux_before = face_x(low - 1) * (here - read(low - 1))
    for plane in range(low, high):
        beyond = read(plane + 1)
        flux = face_x(plane) * (beyond - here)
        flux_y = face_y(plane) * (up(here, 0) - here)
        above = up(here, 1)
        gain = above * (1.0 - here)
        loss = here * (1.0 - above)
        z0, z1 = face_z(plane)
        total = (flux - flux_before) + (flux_y - down(flux_y, 0))
        total = total + (z0 * gain - z1 * loss) + down(z0 * loss - z1 * gain, 1)
        write(plane, here + scale(plane) * total)
        here, flux_before = (beyond, flux)


def start_field(shape):
    return jnp.where(lax.rem(lane_iota(shape) // BLOCK_Z, 2) == 0, 1.0, 0.0)


def tile_kernel(
    rows_ref, source_ref, perm_ref, store_ref, well_x_ref, well_y_ref, well_rate_ref,
    table_ref, resist_ref, storage_ref, x_ref, y_ref, z0_ref, z1_ref, part_ref, scale_ref, rhs_ref,
    *field_refs,
):
    tile_x, rows, layers = rows_ref.shape
    tile_y = source_ref.shape[1]
    anchor_x = lax.axis_index("gx") * tile_x
    anchor_y = lax.axis_index("gy") * tile_y
    codes = perm_ref.shape[0]
    resists = [
        1.0 / jnp.full((1, layers), perm_ref[code], jnp.float32) for code in range(codes)
    ]
    stores = [jnp.full((1, layers), store_ref[code], jnp.float32) for code in range(codes)]
    for code in range(codes):
        table_ref[code : code + 1] = resists[code]
        table_ref[codes + code : codes + code + 1] = stores[code]
    face_y = y_face_mask((rows, layers), tile_y)
    hit_y = (
        lax.broadcasted_iota(jnp.int32, (tile_y, well_y_ref.shape[1]), 0) + anchor_y
        == well_y_ref[...]
    )
    before, x_before, part_before = (None, None, None)
    for plane in range(tile_x):
        resist = code_select(resists, rows_ref[plane])
        store = code_select(stores, rows_ref[plane])
        y_face, z0, z1, part = plane_faces(resist, store, face_y)
        resist_ref[plane] = resist
        storage_ref[plane] = store
        y_ref[plane] = y_face
        z0_ref[plane] = z0
        z1_ref[plane] = z1
        part_ref[plane] = part
        if plane:
            x_face = 2.0 / (before + resist)
            x_ref[plane - 1] = x_face
            if plane > 1:
                scale_ref[plane - 1] = RELAX_WEIGHT / (part_before + x_face + x_before)
            x_before = x_face
        before, part_before = (resist, part)
        hit = hit_y & (well_x_ref[...] == anchor_x + plane)
        column = jnp.sum(jnp.where(hit, well_rate_ref[...], 0.0), axis=1, keepdims=True)
        rhs_ref[plane] = source_ref[plane] + column / layers
    start = start_field((rows, layers))
    read = lambda plane: start
    for sweep_id, field in enumerate(field_refs):
        sweep_planes(
            1 + sweep_id,
            tile_x - 1 - sweep_id,
            read,
            field.__setitem__,
            x_ref.__getitem__,
            y_ref.__getitem__,
            lambda plane: (z0_ref[plane], z1_ref[plane]),
            scale_ref.__getitem__,
        )
        read = field.__getitem__


def basis_kernel(*refs):
    before_ref, after_ref, table_ref, resist_ref, storage_ref, x_ref, y_ref, z0_ref, z1_ref = refs[:9]
    part_ref, scale_ref, rhs_ref = refs[9:12]
    near_fields = refs[12 : 12 + SWEEPS]
    refs = refs[12 + SWEEPS :]
    packed_ref, basis_ref, side_ref, rhs_out_ref, store_out_ref, up_ref, down_ref = refs[:7]
    scale_far, x_far, y_far, z0_far, z1_far, sums_ref = refs[7:13]
    far_fields = refs[13:]
    tile_x, tile_y, layers = rhs_ref.shape
    rows = resist_ref.shape[1]
    planes = tile_x + 2 * MARGIN
    shape = (rows, layers)
    anchor_x = lax.axis_index("gx") * tile_x
    total_x = lax.axis_size("gx") * tile_x
    face_mask_y = y_face_mask(shape, tile_y)
    codes = table_ref.shape[0] // 2
    table = [table_ref[i : i + 1] for i in range(2 * codes)]

    def own(plane, depth=0):
        return MARGIN + depth <= plane < MARGIN + tile_x - depth

    def face_x(plane):
        inner = own(plane) and own(plane + 1)
        return x_ref[plane - MARGIN] if inner else x_far[plane]

    def near_or_far(near, far, depth=0):
        return lambda plane: near[plane - MARGIN] if own(plane, depth) else far[plane]

    face_y = near_or_far(y_ref, y_far)
    face_z0 = near_or_far(z0_ref, z0_far)
    face_z1 = near_or_far(z1_ref, z1_far)
    scale = near_or_far(scale_ref, scale_far, 1)
    resist_last, x_last, part_last = (None, None, None)
    for plane in range(planes):
        part = None
        if own(plane):
            resist = resist_ref[plane - MARGIN]
            part = part_ref[plane - MARGIN]
        else:
            strip = before_ref if plane < MARGIN else after_ref
            facies = strip[plane if plane < MARGIN else plane - MARGIN - tile_x]
            resist = code_select(table[:codes], facies)
            if 0 < plane < planes - 1:
                store = code_select(table[codes:], facies)
                y_far[plane], z0_far[plane], z1_far[plane], part = plane_faces(
                    resist, store, face_mask_y
                )
        if plane:
            if own(plane - 1) and own(plane):
                x_face = face_x(plane - 1)
            else:
                here = anchor_x + plane - 1 - MARGIN
                x_face = 2.0 / (resist_last + resist)
                x_face = jnp.where((here >= 0) & (here + 1 < total_x), x_face, 0.0)
                x_far[plane - 1] = x_face
            if plane > 1 and not own(plane - 1, 1):
                scale_far[plane - 1] = RELAX_WEIGHT / (part_last + x_face + x_last)
            x_last = x_face
        resist_last, part_last = (resist, part)

    start = start_field(shape)
    read = lambda plane: start
    for sweep_id in range(SWEEPS):
        depth = 1 + sweep_id
        first_end = min(MARGIN + depth, planes - depth)
        last_start = max(first_end, MARGIN + tile_x - depth)
        for low, high in ((depth, first_end), (last_start, planes - depth)):
            sweep_planes(
                low,
                high,
                read,
                far_fields[sweep_id].__setitem__,
                face_x,
                face_y,
                lambda plane: (face_z0(plane), face_z1(plane)),
                scale,
            )
        read = near_or_far(near_fields[sweep_id], far_fields[sweep_id], depth)

    tile = (tile_y, layers)
    cut_0 = face_ends(lane_iota(tile), 0)
    cut_any = cut_0 | face_ends(lane_iota(tile), 1)

    def inner(value):
        return value[:tile_y]

    sums = None
    for plane in range(tile_x):
        at = plane + MARGIN
        here_all = read(at)
        here = inner(here_all)
        step_y_all = up(here_all, 0) - here_all
        flux_y_all = y_ref[plane] * step_y_all
        flux_y = inner(flux_y_all)
        step_x = inner(read(at + 1)) - here
        flux_x = inner(face_x(at)) * step_x
        flux_before = inner(face_x(at - 1)) * (here - inner(read(at - 1)))
        z_face = jnp.maximum(inner(z0_ref[plane]), inner(z1_ref[plane]))
        above = up(here, 1)
        step_z = above - here
        energy_z = z_face * step_z * step_z
        other = 1.0 - here
        store = inner(storage_ref[plane])
        factor = inner(scale(at))
        rhs = rhs_ref[plane]
        below_end = jnp.where(cut_0, here, other)
        above_end = jnp.where(cut_0, above, 1.0 - above)
        z_cut = jnp.where(cut_any, z_face, 0.0)
        basis_ref[plane] = here
        side_ref[plane] = factor * (
            (flux_before - flux_x) + (inner(down(flux_y_all, 0)) - flux_y)
        )
        rhs_out_ref[plane] = factor * rhs
        store_out_ref[plane] = factor * store
        up_ref[plane] = factor * z_face
        down_ref[plane] = factor * down(z_face, 1)
        terms = (
            store * here * here,
            store * here * other,
            store * other * other,
            flux_x * step_x + flux_y * inner(step_y_all) + jnp.where(cut_any, 0.0, energy_z),
            jnp.where(cut_any, energy_z, 0.0),
            z_cut * below_end * below_end,
            z_cut * above_end * above_end,
            z_cut * below_end * above_end,
            here * rhs,
            other * rhs,
        )
        sums = terms if sums is None else [a + b for a, b in zip(sums, terms)]
    mass_00, mass_01, mass_11, energy, cut, low_2, high_2, low_high, rhs_0, rhs_1 = (
        jnp.sum(total, axis=0, keepdims=True) for total in sums
    )
    line = lane_iota((1, layers))
    count = layers // BLOCK_Z
    ends = (face_ends(line, 0), face_ends(line, 1))
    inside = (in_grid(line, 0, count), in_grid(line, 1, count))
    for parity, mass, right in ((0, mass_00, rhs_0), (1, mass_11, rhs_1)):
        own_end = jnp.where(ends[parity], low_2, cut)
        beyond_end = down(jnp.where(ends[parity], high_2, 0.0), 1)
        entry = mass + energy + own_end + beyond_end
        sums_ref[parity : parity + 1] = jnp.where(inside[parity], entry, 0.0)
        sums_ref[4 + parity : 5 + parity] = jnp.where(inside[parity], right, 0.0)
    sums_ref[2:3] = mass_01 - energy + (low_high - low_2) + down(low_high - high_2, 1)
    sums_ref[3:4] = -low_high
    sums_ref[6:8] = jnp.zeros((2, layers), jnp.float32)
    window = pltpu.roll(sums_ref[...], 0, 1, stride=1, stride_axis=0)
    width = 1
    while width < BLOCK_Z:
        window = window + pltpu.roll(window, width, 1)
        width *= 2
    row = lax.broadcasted_iota(jnp.int32, window.shape, 0)
    keep = lax.rem(lane_iota(window.shape) + layers - BLOCK_Z // 2 + 1 - row, BLOCK_Z) == 0
    packed = jnp.sum(jnp.where(keep, window, 0.0), axis=0, keepdims=True)
    packed_ref[...] = jnp.broadcast_to(packed, packed_ref.shape)


def solve_band(diagonal, first, second, right):
    count = len(diagonal)
    matrix = {(k, k): diagonal[k] for k in range(count)}
    for distance, band in ((1, first), (2, second)):
        for k in range(count - distance):
            matrix[k, k + distance] = band[k]
            matrix[k + distance, k] = band[k]
    left = list(range(count))
    steps = []
    while left:
        pivot = left.pop(0 if len(steps) % 2 == 0 else -1)
        inverse = 1.0 / matrix[pivot, pivot]
        linked = [k for k in left if (pivot, k) in matrix]
        lower = {k: matrix[pivot, k] * inverse for k in linked}
        for k in linked:
            right[k] = right[k] - lower[k] * right[pivot]
            for other in linked:
                if other >= k:
                    change = lower[k] * matrix[pivot, other]
                    entry = matrix[k, other] - change if (k, other) in matrix else -change
                    matrix[k, other] = entry
                    matrix[other, k] = entry
        steps.append((pivot, inverse, lower))
    values = [None] * count
    for pivot, inverse, lower in reversed(steps):
        value = right[pivot] * inverse
        for k, factor in lower.items():
            value = value - factor * values[k]
        values[pivot] = value
    return values


def pressure_kernel(
    rows_ref, basis_ref, side_ref, rhs_ref, store_ref, up_ref, down_ref, out_ref, entries
):
    tile_x, tile_y, layers = basis_ref.shape
    count = layers // BLOCK_Z
    half = BLOCK_Z // 2
    shape = (count, layers)
    node = lax.broadcasted_iota(jnp.int32, shape, 0)
    layer = lane_iota(shape)
    packed = jnp.sum(rows_ref[...], axis=0, keepdims=True)

    def held(segment, kind):
        return layer == lax.rem(segment * BLOCK_Z + half - 1 + kind, layers)

    parity = lax.rem(node, 2)
    own = held(node, parity) | held(node + 1, parity)
    right = held(node, parity + 4) | held(node + 1, parity + 4)
    masks = (own, held(node + 1, 2), held(node + 1, 3), right)
    for part_id, mask in enumerate(masks):
        part = jnp.where(mask, packed, 0.0)
        entries[part_id] = jnp.broadcast_to(jnp.sum(part, axis=1, keepdims=True), shape)
    values = solve_band(
        *([entries[part_id, k : k + 1] for k in range(count)] for part_id in range(4))
    )
    line = lane_iota((1, layers))
    fields = [jnp.zeros((1, layers), jnp.float32)] * 2
    for k in range(count):
        support = (line >= k * BLOCK_Z - half) & (line < k * BLOCK_Z + 3 * half)
        fields[k % 2] = jnp.where(support, values[k], fields[k % 2])
    value_0 = jnp.broadcast_to(fields[0], (tile_y, layers))
    value_1 = jnp.broadcast_to(fields[1], (tile_y, layers))
    apart = value_0 - value_1
    for plane in range(tile_x):
        here = basis_ref[plane]
        prolonged = here * value_0 + (1.0 - here) * value_1
        applied = (
            store_ref[plane] * prolonged
            + apart * side_ref[plane]
            + up_ref[plane] * (prolonged - up(prolonged, 1))
            + down_ref[plane] * (prolonged - down(prolonged, 1))
        )
        out_ref[plane] = prolonged + (rhs_ref[plane] - applied)


def column_step(facies, source, facies_perm, facies_store, well_x, well_y, well_rate):
    tile_x, tile_y, layers = facies.shape
    rows = tile_y + 2 * MARGIN
    planes = tile_x + 2 * MARGIN
    size = lax.axis_size(AXES)
    f32 = jnp.float32
    tile = jax.ShapeDtypeStruct(facies.shape, f32)
    wide = jax.ShapeDtypeStruct((tile_x, rows, layers), f32)
    vmem = pl.BlockSpec(memory_space=pltpu.VMEM)
    smem = pl.BlockSpec(memory_space=pltpu.SMEM)
    params = pltpu.CompilerParams(vmem_limit_bytes=VMEM_BYTES)

    before, after = pair_swaps(facies, 1, "gy", MARGIN)
    own = jnp.concatenate([facies, after, before], axis=1)
    before, after = pair_swaps(own, 0, "gx", MARGIN)
    near = pl.pallas_call(
        tile_kernel,
        out_shape=(jax.ShapeDtypeStruct((2 * facies_perm.shape[0], layers), f32),)
        + (wide,) * 8
        + (tile,)
        + (wide,) * SWEEPS,
        in_specs=[vmem, vmem, smem, smem, vmem, vmem, vmem],
        out_specs=(vmem,) * (10 + SWEEPS),
        compiler_params=params,
        cost_estimate=pl.CostEstimate(flops=3000000, bytes_accessed=1000000, transcendentals=0),
        name="tile",
    )(
        own,
        source,
        facies_perm,
        facies_store,
        well_x[None, :],
        well_y[None, :],
        well_rate[None, :],
    )
    copies, *fields = pl.pallas_call(
        basis_kernel,
        out_shape=(jax.ShapeDtypeStruct((size, layers), f32),) + (tile,) * 6,
        in_specs=[vmem] * (12 + SWEEPS),
        out_specs=(vmem,) * 7,
        scratch_shapes=[pltpu.VMEM((planes, rows, layers), f32)] * 5
        + [pltpu.VMEM((8, layers), f32)]
        + [pltpu.VMEM((planes, rows, layers), f32)] * SWEEPS,
        compiler_params=params,
        name="basis",
    )(before, after, *near)
    everyone = lax.all_to_all(copies, AXES, 0, 0, tiled=True)
    return pl.pallas_call(
        pressure_kernel,
        out_shape=tile,
        in_specs=[vmem] * 7,
        out_specs=vmem,
        scratch_shapes=[pltpu.VMEM((4, layers // BLOCK_Z, layers), f32)],
        compiler_params=params,
        name="pressure",
    )(everyone, *fields)


def solution(mesh):
    def per_device(facies, *others):
        tile_x, tile_y, layers = facies.shape
        total_x = tile_x * mesh.shape["gx"]
        total_y = tile_y * mesh.shape["gy"]
        one_column = total_x == BLOCK_X and total_y == BLOCK_Y
        fits = layers % 128 == 0 and tile_y % 8 == 0 and min(tile_x, tile_y) >= MARGIN
        step = column_step if one_column and fits else general_step
        return step(facies, *others)

    in_specs = (P("gx", "gy", None), P("gx", "gy", None), P(), P(), P(), P(), P())
    out_specs = P("gx", "gy", None)
    return jax.shard_map(
        per_device, mesh=mesh, in_specs=in_specs, out_specs=out_specs, check_vma=False
    )
```

```python
import jax
import jax.numpy as jnp
import numpy as np
from jax import lax
from jax.experimental import pallas as pl
from jax.experimental.pallas import tpu as pltpu
from jax.sharding import PartitionSpec as P

BLOCK_X = 64
BLOCK_Y = 64
BLOCK_Z = 16
SWEEPS = 3


RELAX_WEIGHT = 2.0 / 3.0
HIGHEST = lax.Precision.HIGHEST
first_bits = np.array([0, 0, 0, 0, 1, 1, 1, 1], dtype=np.int32)
second_bits = np.array([0, 0, 1, 1, 0, 0, 1, 1], dtype=np.int32)
third_bits = np.array([0, 1, 0, 1, 0, 1, 0, 1], dtype=np.int32)
shift_along_x = np.array([0, 2, -2, 0, 0, 0, 0], dtype=np.int32)
shift_along_y = np.array([0, 0, 0, 2, -2, 0, 0], dtype=np.int32)
shift_along_z = np.array([0, 0, 0, 0, 0, 2, -2], dtype=np.int32)


def with_halo(value, sides, width):
    for axis, dim in sides:
        size, length = (lax.axis_size(axis), value.shape[dim])
        up = [(i, (i + 1) % size) for i in range(size - 1)]
        down = [(j, i) for i, j in up]
        last = lax.slice_in_dim(value, length - width, length, axis=dim)
        initial = lax.slice_in_dim(value, 0, width, axis=dim)
        before = lax.ppermute(last, axis, up)
        after = lax.ppermute(initial, axis, down)
        value = jnp.concatenate([before, value, after], axis=dim)
    return value


def support_of(coords, block_size, parity):
    return parity + 2 * jnp.floor_divide(
        coords + block_size // 2 - block_size * parity, 2 * block_size
    )


def parity_nodes(coords, block_size):
    return jnp.stack([support_of(coords, block_size, 0), support_of(coords, block_size, 1)])


def parity_start(coords, block_size):
    node_ids = parity_nodes(coords, block_size)
    return (node_ids == jnp.floor_divide(coords, block_size)[None]).astype(jnp.float32)


def parity_same(coords, block_size):
    node_here = parity_nodes(coords[:-1], block_size)
    node_next = parity_nodes(coords[1:], block_size)
    return (node_here == node_next).astype(jnp.float32)


def harmonic(left_perm, right_perm):
    return 2.0 * left_perm * right_perm / (left_perm + right_perm)


def face_pad(values_in, dim_id, before):
    widths = [(0, 0), (0, 0), (0, 0)]
    widths[dim_id] = (1, 0) if before else (0, 1)
    return jnp.pad(values_in, widths)


def expand(line_in, dim_id):
    new_shape = [1, 1, 1]
    new_shape[dim_id] = line_in.shape[0]
    return line_in.reshape(new_shape)


def split_faces(values_in, dim_id):
    length = values_in.shape[dim_id]
    below_part = lax.slice_in_dim(values_in, 0, length - 1, axis=dim_id)
    above_part = lax.slice_in_dim(values_in, 1, length, axis=dim_id)
    return (below_part, above_part)


def cut_apply(values_in, storage, trans_all, same_all):
    result = storage * values_in
    for dim_id in range(3):
        trans_face = trans_all[dim_id]
        same_line = expand(same_all[dim_id], dim_id)
        below_part, above_part = split_faces(values_in, dim_id)
        result = result + face_pad(
            trans_face * (below_part - same_line * above_part), dim_id, False
        )
        result = result + face_pad(trans_face * (above_part - same_line * below_part), dim_id, True)
    return result


def rim_terms(values_in, trans_all, same_all):
    result = []
    for dim_id in range(3):
        trans_face = trans_all[dim_id]
        cross_mask = 1.0 - expand(same_all[dim_id], dim_id)
        below_part, above_part = split_faces(values_in, dim_id)
        result.append(face_pad(-trans_face * cross_mask * above_part, dim_id, False))
        result.append(face_pad(-trans_face * cross_mask * below_part, dim_id, True))
    return result


def diagonal_of(storage, trans_all):
    result = storage
    for dim_id in range(3):
        result = (
            result
            + face_pad(trans_all[dim_id], dim_id, False)
            + face_pad(trans_all[dim_id], dim_id, True)
        )
    return result


def lookup(facies, code_table):
    result = jnp.zeros(facies.shape, jnp.float32)
    for code_id in range(code_table.shape[0]):
        result = result + jnp.where(facies == code_id, code_table[code_id], 0.0)
    return result


def flatten_node(index_x, index_y, index_z, counts):
    count_x, count_y, count_z = counts
    flat_ids = (
        jnp.clip(index_x, 0, count_x - 1) * count_y + jnp.clip(index_y, 0, count_y - 1)
    ) * count_z
    return (flat_ids + jnp.clip(index_z, 0, count_z - 1)).astype(jnp.int32)


def tile_indices(anchor_x, anchor_y, counts):
    count_x, count_y, count_z = counts
    row_x = parity_nodes(jnp.reshape(anchor_x, (1,)), BLOCK_X)[first_bits][:, 0]
    row_y = parity_nodes(jnp.reshape(anchor_y, (1,)), BLOCK_Y)[second_bits][:, 0]
    seg_first = jnp.maximum(jnp.arange(count_z + 1, dtype=jnp.int32) * BLOCK_Z - BLOCK_Z // 2, 0)
    row_z = parity_nodes(seg_first, BLOCK_Z)[third_bits]
    row_ids = flatten_node(row_x[:, None], row_y[:, None], row_z, counts)
    col_ids = flatten_node(
        row_x[:, None, None] + jnp.asarray(shift_along_x)[None, :, None],
        row_y[:, None, None] + jnp.asarray(shift_along_y)[None, :, None],
        row_z[:, None, :] + jnp.asarray(shift_along_z)[None, :, None],
        counts,
    )
    entry_ids = row_ids[None, :, None, :] * (count_x * count_y * count_z) + col_ids[:, None, :, :]
    return (entry_ids, row_ids)


def segment_matrix(layers, segment_count):
    seg_of = (jnp.arange(layers, dtype=jnp.int32) + BLOCK_Z // 2) // BLOCK_Z
    return (seg_of[:, None] == jnp.arange(segment_count, dtype=jnp.int32)[None, :]).astype(
        jnp.float32
    )


def solve_coarse(coarse, coarse_rhs):
    factor = jnp.linalg.cholesky(coarse)
    middle = lax.linalg.triangular_solve(factor, coarse_rhs[:, None], left_side=True, lower=True)
    return lax.linalg.triangular_solve(
        factor, middle, left_side=True, lower=True, transpose_a=True
    )[:, 0]


def geometry(coeffs, margin, anchor_x, anchor_y, total_x, total_y):
    coord_x = anchor_x - margin + jnp.arange(coeffs.shape[1], dtype=jnp.int32)
    coord_y = anchor_y - margin + jnp.arange(coeffs.shape[2], dtype=jnp.int32)
    coord_z = jnp.arange(coeffs.shape[3], dtype=jnp.int32)
    inside_x = (coord_x >= 0) & (coord_x < total_x)
    inside_y = (coord_y >= 0) & (coord_y < total_y)
    inside = inside_x[:, None, None] & inside_y[None, :, None]
    perm_safe = jnp.where(inside, coeffs[0], 1.0)
    storage = jnp.where(inside, coeffs[1], 1.0)
    valid_x = (inside_x[:-1] & inside_x[1:]).astype(jnp.float32)
    valid_y = (inside_y[:-1] & inside_y[1:]).astype(jnp.float32)
    trans_x = harmonic(perm_safe[:-1], perm_safe[1:]) * valid_x[:, None, None]
    trans_y = harmonic(perm_safe[:, :-1], perm_safe[:, 1:]) * valid_y[None, :, None]
    trans_z = harmonic(perm_safe[:, :, :-1], perm_safe[:, :, 1:])
    trans_all = (trans_x, trans_y, trans_z)
    same_all = (
        parity_same(coord_x, BLOCK_X)[first_bits],
        parity_same(coord_y, BLOCK_Y)[second_bits],
        parity_same(coord_z, BLOCK_Z)[third_bits],
    )
    starts = (
        parity_start(coord_x, BLOCK_X)[first_bits],
        parity_start(coord_y, BLOCK_Y)[second_bits],
        parity_start(coord_z, BLOCK_Z)[third_bits],
    )
    return (storage, trans_all, diagonal_of(storage, trans_all), same_all, starts)


def initial(geo_set):
    start_x, start_y, start_z = geo_set[4]
    return start_x[:, :, None, None] * start_y[:, None, :, None] * start_z[:, None, None, :]


def smooth(basis_ext, geo_set):
    storage, trans_all, diagonal, same_all, _ = geo_set

    def change_of(values_in, same_x, same_y, same_z):
        return (
            -RELAX_WEIGHT
            * cut_apply(values_in, storage, trans_all, (same_x, same_y, same_z))
            / diagonal
        )

    changes = jax.vmap(change_of)(basis_ext, same_all[0], same_all[1], same_all[2])[:, 1:-1, 1:-1]
    interior = basis_ext[:, 1:-1, 1:-1]
    change_sum = jnp.sum(changes, axis=0)
    return interior + changes - interior * change_sum[None]


def basis_halo(basis_now):
    return with_halo(basis_now, (("gx", 1), ("gy", 2)), 1)


def general_step(facies, source, facies_perm, facies_store, well_x, well_y, well_rate):
    tile_x, tile_y, layers = facies.shape
    devs_x = lax.axis_size("gx")
    devs_y = lax.axis_size("gy")
    total_x = tile_x * devs_x
    total_y = tile_y * devs_y
    anchor_x = lax.axis_index("gx") * tile_x
    anchor_y = lax.axis_index("gy") * tile_y
    coeffs = jnp.stack([lookup(facies, facies_perm), lookup(facies, facies_store)])
    coeff_wide = with_halo(coeffs, (("gx", 1), ("gy", 2)), 1)
    geo_one = geometry(coeff_wide, 1, anchor_x, anchor_y, total_x, total_y)
    basis_now = initial(geo_one)[:, 1:-1, 1:-1]
    for _ in range(SWEEPS):
        basis_now = smooth(basis_halo(basis_now), geo_one)
    basis_now = basis_halo(basis_now)
    storage, trans_all, diagonal, same_all, _ = geo_one

    def terms_of(values_in, same_x, same_y, same_z):
        same_three = (same_x, same_y, same_z)
        return jnp.stack(
            [cut_apply(values_in, storage, trans_all, same_three)]
            + rim_terms(values_in, trans_all, same_three)
        )

    term_stack = jax.vmap(terms_of)(basis_now, same_all[0], same_all[1], same_all[2])[
        :, :, 1:-1, 1:-1
    ]
    interior = basis_now[:, 1:-1, 1:-1]
    count_x = total_x // BLOCK_X
    count_y = total_y // BLOCK_Y
    count_z = layers // BLOCK_Z
    counts = (count_x, count_y, count_z)
    coarse_count = count_x * count_y * count_z
    zmatrix = segment_matrix(layers, count_z + 1)
    gram_local = jnp.einsum("apqz,cspqz->casz", interior, term_stack, precision=HIGHEST)
    gram_local = jnp.einsum("casz,zg->casg", gram_local, zmatrix, precision=HIGHEST)
    cell_x = anchor_x + jnp.arange(tile_x, dtype=jnp.int32)
    cell_y = anchor_y + jnp.arange(tile_y, dtype=jnp.int32)
    hit_x = (well_x[:, None] == cell_x[None, :]).astype(jnp.float32)
    hit_y = (well_y[:, None] == cell_y[None, :]).astype(jnp.float32)
    column = jnp.einsum("w,wx,wy->xy", well_rate, hit_x, hit_y, precision=HIGHEST)
    rhs_fine = source + column[:, :, None] / layers
    rhs_local = jnp.einsum("apqz,pqz->az", interior, rhs_fine, precision=HIGHEST)
    rhs_local = jnp.einsum("az,zg->ag", rhs_local, zmatrix, precision=HIGHEST)
    entry_ids, row_ids = tile_indices(anchor_x, anchor_y, counts)
    local_matrix = (
        jnp.zeros((coarse_count * coarse_count,), jnp.float32)
        .at[entry_ids.reshape(-1)]
        .add(gram_local.reshape(-1))
    )
    local_matrix = local_matrix.reshape(coarse_count, coarse_count)
    local_rhs = (
        jnp.zeros((coarse_count,), jnp.float32).at[row_ids.reshape(-1)].add(rhs_local.reshape(-1))
    )
    coarse, coarse_rhs = lax.psum((local_matrix, local_rhs), ("gx", "gy"))
    coarse_solution = solve_coarse(coarse, coarse_rhs)
    values_at = coarse_solution[row_ids]
    per_layer = jnp.einsum("ag,zg->az", values_at, zmatrix, precision=HIGHEST)
    prolonged = jnp.einsum("apqz,az->pqz", interior, per_layer, precision=HIGHEST)
    prolonged_ext = with_halo(prolonged, (("gx", 0), ("gy", 1)), 1)
    ones_all = (
        jnp.ones((tile_x + 1,), jnp.float32),
        jnp.ones((tile_y + 1,), jnp.float32),
        jnp.ones((layers - 1,), jnp.float32),
    )
    applied = cut_apply(prolonged_ext, storage, trans_all, ones_all)[1:-1, 1:-1]
    return prolonged + RELAX_WEIGHT * (rhs_fine - applied) / diagonal[1:-1, 1:-1]


MARGIN = SWEEPS + 1
AXES = ("gx", "gy")
VMEM_BYTES = 16 * 2**20


def swap_along(value, axis, first):
    sizes = {name_: lax.axis_size(name_) for name_ in AXES}
    other = AXES[1 - AXES.index(axis)]
    pairs = []
    for gx in range(sizes[AXES[0]]):
        for gy in range(sizes[AXES[1]]):
            place = {AXES[0]: gx, AXES[1]: gy}
            partner = dict(place)
            along = first + ((place[axis] - first) ^ 1) if place[axis] >= first else -1
            if 0 <= along < sizes[axis]:
                partner[axis] = along
            else:
                partner[other] = place[other] ^ 1
            if partner[other] < sizes[other]:
                pairs.append(tuple(p[AXES[0]] * sizes[AXES[1]] + p[AXES[1]] for p in (place, partner)))
    return lax.ppermute(value, AXES, pairs)


def pair_swaps(value, dim, axis, width):
    length = value.shape[dim]
    last = lax.slice_in_dim(value, length - width, length, axis=dim)
    first = lax.slice_in_dim(value, 0, width, axis=dim)
    even = lax.axis_index(axis) % 2 == 0
    far = swap_along(jnp.where(even, first, last), axis, 1)
    near = swap_along(jnp.where(even, last, first), axis, 0)
    return jnp.where(even, far, near), jnp.where(even, near, far)


def lane_iota(shape):
    return lax.broadcasted_iota(jnp.int32, shape, len(shape) - 1)


def face_ends(layer, parity):
    return lax.rem(layer + 1 + BLOCK_Z // 2 + BLOCK_Z * parity, 2 * BLOCK_Z) == 0


def in_grid(layer, parity, count):
    shifted = layer + BLOCK_Z // 2 + BLOCK_Z * parity
    node = 2 * (shifted // (2 * BLOCK_Z)) - parity
    return (node >= 0) & (node < count)


def up(value, axis):
    return pltpu.roll(value, value.shape[axis] - 1, axis)


def down(value, axis):
    return pltpu.roll(value, 1, axis)


def code_select(table, codes):
    result = jnp.broadcast_to(table[0], codes.shape)
    for code_id in range(1, len(table)):
        result = jnp.where(codes == code_id, table[code_id], result)
    return result


def plane_faces(resist, store, face_y):
    layer = lane_iota(resist.shape)
    y_face = jnp.where(face_y, 2.0 / (resist + up(resist, 0)), 0.0)
    z_face = jnp.where(layer == resist.shape[1] - 1, 0.0, 2.0 / (resist + up(resist, 1)))
    part = store + y_face + down(y_face, 0) + z_face + down(z_face, 1)
    z_faces = [jnp.where(face_ends(layer, parity), 0.0, z_face) for parity in (0, 1)]
    return y_face, z_faces[0], z_faces[1], part


def y_face_mask(shape, tile_y):
    row = lax.broadcasted_iota(jnp.int32, shape, 0)
    place = lax.axis_index("gy") * tile_y + jnp.where(row < tile_y + MARGIN, row, row - shape[0])
    inside = (place >= 0) & (place + 1 < lax.axis_size("gy") * tile_y)
    return inside & (row != tile_y + MARGIN - 1)


def sweep_planes(low, high, read, write, face_x, face_y, face_z, scale):
    if low >= high:
        return
    here = read(low)
    flux_before = face_x(low - 1) * (here - read(low - 1))
    for plane in range(low, high):
        beyond = read(plane + 1)
        flux = face_x(plane) * (beyond - here)
        flux_y = face_y(plane) * (up(here, 0) - here)
        above = up(here, 1)
        gain = above * (1.0 - here)
        loss = here * (1.0 - above)
        z0, z1 = face_z(plane)
        total = (flux - flux_before) + (flux_y - down(flux_y, 0))
        total = total + (z0 * gain - z1 * loss) + down(z0 * loss - z1 * gain, 1)
        write(plane, here + scale(plane) * total)
        here, flux_before = (beyond, flux)


def start_field(shape):
    return jnp.where(lax.rem(lane_iota(shape) // BLOCK_Z, 2) == 0, 1.0, 0.0)


def tile_kernel(
    rows_ref, source_ref, perm_ref, store_ref, well_x_ref, well_y_ref, well_rate_ref,
    table_ref, resist_ref, storage_ref, x_ref, y_ref, z0_ref, z1_ref, part_ref, scale_ref, rhs_ref,
    *field_refs,
):
    tile_x, rows, layers = rows_ref.shape
    tile_y = source_ref.shape[1]
    anchor_x = lax.axis_index("gx") * tile_x
    anchor_y = lax.axis_index("gy") * tile_y
    codes = perm_ref.shape[0]
    resists = [
        1.0 / jnp.full((1, layers), perm_ref[code], jnp.float32) for code in range(codes)
    ]
    stores = [jnp.full((1, layers), store_ref[code], jnp.float32) for code in range(codes)]
    for code in range(codes):
        table_ref[code : code + 1] = resists[code]
        table_ref[codes + code : codes + code + 1] = stores[code]
    face_y = y_face_mask((rows, layers), tile_y)
    hit_y = (
        lax.broadcasted_iota(jnp.int32, (tile_y, well_y_ref.shape[1]), 0) + anchor_y
        == well_y_ref[...]
    )
    before, x_before, part_before = (None, None, None)
    for plane in range(tile_x):
        resist = code_select(resists, rows_ref[plane])
        store = code_select(stores, rows_ref[plane])
        y_face, z0, z1, part = plane_faces(resist, store, face_y)
        resist_ref[plane] = resist
        storage_ref[plane] = store
        y_ref[plane] = y_face
        z0_ref[plane] = z0
        z1_ref[plane] = z1
        part_ref[plane] = part
        if plane:
            x_face = 2.0 / (before + resist)
            x_ref[plane - 1] = x_face
            if plane > 1:
                scale_ref[plane - 1] = RELAX_WEIGHT / (part_before + x_face + x_before)
            x_before = x_face
        before, part_before = (resist, part)
        hit = hit_y & (well_x_ref[...] == anchor_x + plane)
        column = jnp.sum(jnp.where(hit, well_rate_ref[...], 0.0), axis=1, keepdims=True)
        rhs_ref[plane] = source_ref[plane] + column / layers
    start = start_field((rows, layers))
    read = lambda plane: start
    for sweep_id, field in enumerate(field_refs):
        sweep_planes(
            1 + sweep_id,
            tile_x - 1 - sweep_id,
            read,
            field.__setitem__,
            x_ref.__getitem__,
            y_ref.__getitem__,
            lambda plane: (z0_ref[plane], z1_ref[plane]),
            scale_ref.__getitem__,
        )
        read = field.__getitem__


def basis_kernel(*refs):
    before_ref, after_ref, table_ref, resist_ref, storage_ref, x_ref, y_ref, z0_ref, z1_ref = refs[:9]
    part_ref, scale_ref, rhs_ref = refs[9:12]
    near_fields = refs[12 : 12 + SWEEPS]
    refs = refs[12 + SWEEPS :]
    packed_ref, basis_ref, side_ref, rhs_out_ref, store_out_ref, up_ref, down_ref = refs[:7]
    scale_far, x_far, y_far, z0_far, z1_far, sums_ref = refs[7:13]
    far_fields = refs[13:]
    tile_x, tile_y, layers = rhs_ref.shape
    rows = resist_ref.shape[1]
    planes = tile_x + 2 * MARGIN
    shape = (rows, layers)
    anchor_x = lax.axis_index("gx") * tile_x
    total_x = lax.axis_size("gx") * tile_x
    face_mask_y = y_face_mask(shape, tile_y)
    codes = table_ref.shape[0] // 2
    table = [table_ref[i : i + 1] for i in range(2 * codes)]

    def own(plane, depth=0):
        return MARGIN + depth <= plane < MARGIN + tile_x - depth

    def face_x(plane):
        inner = own(plane) and own(plane + 1)
        return x_ref[plane - MARGIN] if inner else x_far[plane]

    def near_or_far(near, far, depth=0):
        return lambda plane: near[plane - MARGIN] if own(plane, depth) else far[plane]

    face_y = near_or_far(y_ref, y_far)
    face_z0 = near_or_far(z0_ref, z0_far)
    face_z1 = near_or_far(z1_ref, z1_far)
    scale = near_or_far(scale_ref, scale_far, 1)
    resist_last, x_last, part_last = (None, None, None)
    for plane in range(planes):
        part = None
        if own(plane):
            resist = resist_ref[plane - MARGIN]
            part = part_ref[plane - MARGIN]
        else:
            strip = before_ref if plane < MARGIN else after_ref
            facies = strip[plane if plane < MARGIN else plane - MARGIN - tile_x]
            resist = code_select(table[:codes], facies)
            if 0 < plane < planes - 1:
                store = code_select(table[codes:], facies)
                y_far[plane], z0_far[plane], z1_far[plane], part = plane_faces(
                    resist, store, face_mask_y
                )
        if plane:
            if own(plane - 1) and own(plane):
                x_face = face_x(plane - 1)
            else:
                here = anchor_x + plane - 1 - MARGIN
                x_face = 2.0 / (resist_last + resist)
                x_face = jnp.where((here >= 0) & (here + 1 < total_x), x_face, 0.0)
                x_far[plane - 1] = x_face
            if plane > 1 and not own(plane - 1, 1):
                scale_far[plane - 1] = RELAX_WEIGHT / (part_last + x_face + x_last)
            x_last = x_face
        resist_last, part_last = (resist, part)

    start = start_field(shape)
    read = lambda plane: start
    for sweep_id in range(SWEEPS):
        depth = 1 + sweep_id
        first_end = min(MARGIN + depth, planes - depth)
        last_start = max(first_end, MARGIN + tile_x - depth)
        for low, high in ((depth, first_end), (last_start, planes - depth)):
            sweep_planes(
                low,
                high,
                read,
                far_fields[sweep_id].__setitem__,
                face_x,
                face_y,
                lambda plane: (face_z0(plane), face_z1(plane)),
                scale,
            )
        read = near_or_far(near_fields[sweep_id], far_fields[sweep_id], depth)

    tile = (tile_y, layers)
    cut_0 = face_ends(lane_iota(tile), 0)
    cut_any = cut_0 | face_ends(lane_iota(tile), 1)

    def inner(value):
        return value[:tile_y]

    sums = None
    for plane in range(tile_x):
        at = plane + MARGIN
        here_all = read(at)
        here = inner(here_all)
        step_y_all = up(here_all, 0) - here_all
        flux_y_all = y_ref[plane] * step_y_all
        flux_y = inner(flux_y_all)
        step_x = inner(read(at + 1)) - here
        flux_x = inner(face_x(at)) * step_x
        flux_before = inner(face_x(at - 1)) * (here - inner(read(at - 1)))
        z_face = jnp.maximum(inner(z0_ref[plane]), inner(z1_ref[plane]))
        above = up(here, 1)
        step_z = above - here
        energy_z = z_face * step_z * step_z
        other = 1.0 - here
        store = inner(storage_ref[plane])
        factor = inner(scale(at))
        rhs = rhs_ref[plane]
        below_end = jnp.where(cut_0, here, other)
        above_end = jnp.where(cut_0, above, 1.0 - above)
        z_cut = jnp.where(cut_any, z_face, 0.0)
        basis_ref[plane] = here
        side_ref[plane] = factor * (
            (flux_before - flux_x) + (inner(down(flux_y_all, 0)) - flux_y)
        )
        rhs_out_ref[plane] = factor * rhs
        store_out_ref[plane] = factor * store
        up_ref[plane] = factor * z_face
        down_ref[plane] = factor * down(z_face, 1)
        terms = (
            store * here * here,
            store * here * other,
            store * other * other,
            flux_x * step_x + flux_y * inner(step_y_all) + jnp.where(cut_any, 0.0, energy_z),
            jnp.where(cut_any, energy_z, 0.0),
            z_cut * below_end * below_end,
            z_cut * above_end * above_end,
            z_cut * below_end * above_end,
            here * rhs,
            other * rhs,
        )
        sums = terms if sums is None else [a + b for a, b in zip(sums, terms)]
    mass_00, mass_01, mass_11, energy, cut, low_2, high_2, low_high, rhs_0, rhs_1 = (
        jnp.sum(total, axis=0, keepdims=True) for total in sums
    )
    line = lane_iota((1, layers))
    count = layers // BLOCK_Z
    ends = (face_ends(line, 0), face_ends(line, 1))
    inside = (in_grid(line, 0, count), in_grid(line, 1, count))
    for parity, mass, right in ((0, mass_00, rhs_0), (1, mass_11, rhs_1)):
        own_end = jnp.where(ends[parity], low_2, cut)
        beyond_end = down(jnp.where(ends[parity], high_2, 0.0), 1)
        entry = mass + energy + own_end + beyond_end
        sums_ref[parity : parity + 1] = jnp.where(inside[parity], entry, 0.0)
        sums_ref[4 + parity : 5 + parity] = jnp.where(inside[parity], right, 0.0)
    sums_ref[2:3] = mass_01 - energy + (low_high - low_2) + down(low_high - high_2, 1)
    sums_ref[3:4] = -low_high
    sums_ref[6:8] = jnp.zeros((2, layers), jnp.float32)
    window = pltpu.roll(sums_ref[...], 0, 1, stride=1, stride_axis=0)
    width = 1
    while width < BLOCK_Z:
        window = window + pltpu.roll(window, width, 1)
        width *= 2
    row = lax.broadcasted_iota(jnp.int32, window.shape, 0)
    keep = lax.rem(lane_iota(window.shape) + layers - BLOCK_Z // 2 + 1 - row, BLOCK_Z) == 0
    packed = jnp.sum(jnp.where(keep, window, 0.0), axis=0, keepdims=True)
    packed_ref[...] = jnp.broadcast_to(packed, packed_ref.shape)


def solve_band(diagonal, first, second, right):
    count = len(diagonal)
    matrix = {(k, k): diagonal[k] for k in range(count)}
    for distance, band in ((1, first), (2, second)):
        for k in range(count - distance):
            matrix[k, k + distance] = band[k]
            matrix[k + distance, k] = band[k]
    left = list(range(count))
    steps = []
    while left:
        pivot = left.pop(0 if len(steps) % 2 == 0 else -1)
        inverse = 1.0 / matrix[pivot, pivot]
        linked = [k for k in left if (pivot, k) in matrix]
        lower = {k: matrix[pivot, k] * inverse for k in linked}
        for k in linked:
            right[k] = right[k] - lower[k] * right[pivot]
            for other in linked:
                if other >= k:
                    change = lower[k] * matrix[pivot, other]
                    entry = matrix[k, other] - change if (k, other) in matrix else -change
                    matrix[k, other] = entry
                    matrix[other, k] = entry
        steps.append((pivot, inverse, lower))
    values = [None] * count
    for pivot, inverse, lower in reversed(steps):
        value = right[pivot] * inverse
        for k, factor in lower.items():
            value = value - factor * values[k]
        values[pivot] = value
    return values


def pressure_kernel(
    rows_ref, basis_ref, side_ref, rhs_ref, store_ref, up_ref, down_ref, out_ref, entries
):
    tile_x, tile_y, layers = basis_ref.shape
    count = layers // BLOCK_Z
    half = BLOCK_Z // 2
    shape = (count, layers)
    node = lax.broadcasted_iota(jnp.int32, shape, 0)
    layer = lane_iota(shape)
    packed = jnp.sum(rows_ref[...], axis=0, keepdims=True)

    def held(segment, kind):
        return layer == lax.rem(segment * BLOCK_Z + half - 1 + kind, layers)

    parity = lax.rem(node, 2)
    own = held(node, parity) | held(node + 1, parity)
    right = held(node, parity + 4) | held(node + 1, parity + 4)
    masks = (own, held(node + 1, 2), held(node + 1, 3), right)
    for part_id, mask in enumerate(masks):
        part = jnp.where(mask, packed, 0.0)
        entries[part_id] = jnp.broadcast_to(jnp.sum(part, axis=1, keepdims=True), shape)
    values = solve_band(
        *([entries[part_id, k : k + 1] for k in range(count)] for part_id in range(4))
    )
    line = lane_iota((1, layers))
    fields = [jnp.zeros((1, layers), jnp.float32)] * 2
    for k in range(count):
        support = (line >= k * BLOCK_Z - half) & (line < k * BLOCK_Z + 3 * half)
        fields[k % 2] = jnp.where(support, values[k], fields[k % 2])
    value_0 = jnp.broadcast_to(fields[0], (tile_y, layers))
    value_1 = jnp.broadcast_to(fields[1], (tile_y, layers))
    apart = value_0 - value_1
    for plane in range(tile_x):
        here = basis_ref[plane]
        prolonged = here * value_0 + (1.0 - here) * value_1
        applied = (
            store_ref[plane] * prolonged
            + apart * side_ref[plane]
            + up_ref[plane] * (prolonged - up(prolonged, 1))
            + down_ref[plane] * (prolonged - down(prolonged, 1))
        )
        out_ref[plane] = prolonged + (rhs_ref[plane] - applied)


def column_step(facies, source, facies_perm, facies_store, well_x, well_y, well_rate):
    tile_x, tile_y, layers = facies.shape
    rows = tile_y + 2 * MARGIN
    planes = tile_x + 2 * MARGIN
    size = lax.axis_size(AXES)
    f32 = jnp.float32
    tile = jax.ShapeDtypeStruct(facies.shape, f32)
    wide = jax.ShapeDtypeStruct((tile_x, rows, layers), f32)
    vmem = pl.BlockSpec(memory_space=pltpu.VMEM)
    smem = pl.BlockSpec(memory_space=pltpu.SMEM)
    params = pltpu.CompilerParams(vmem_limit_bytes=VMEM_BYTES)

    far = swap_along(facies, "gy", 1)
    near = swap_along(facies, "gy", 0)
    even = lax.axis_index("gy") % 2 == 0
    before = jnp.where(even, far[:, -MARGIN:], near[:, -MARGIN:])
    after = jnp.where(even, near[:, :MARGIN], far[:, :MARGIN])
    own = jnp.concatenate([facies, after, before], axis=1)
    before, after = pair_swaps(own, 0, "gx", MARGIN)
    near = pl.pallas_call(
        tile_kernel,
        out_shape=(jax.ShapeDtypeStruct((2 * facies_perm.shape[0], layers), f32),)
        + (wide,) * 8
        + (tile,)
        + (wide,) * SWEEPS,
        in_specs=[vmem, vmem, smem, smem, vmem, vmem, vmem],
        out_specs=(vmem,) * (10 + SWEEPS),
        compiler_params=params,
        cost_estimate=pl.CostEstimate(flops=3000000, bytes_accessed=1000000, transcendentals=0),
        name="tile",
    )(
        own,
        source,
        facies_perm,
        facies_store,
        well_x[None, :],
        well_y[None, :],
        well_rate[None, :],
    )
    copies, *fields = pl.pallas_call(
        basis_kernel,
        out_shape=(jax.ShapeDtypeStruct((size, layers), f32),) + (tile,) * 6,
        in_specs=[vmem] * (12 + SWEEPS),
        out_specs=(vmem,) * 7,
        scratch_shapes=[pltpu.VMEM((planes, rows, layers), f32)] * 5
        + [pltpu.VMEM((8, layers), f32)]
        + [pltpu.VMEM((planes, rows, layers), f32)] * SWEEPS,
        compiler_params=params,
        name="basis",
    )(before, after, *near)
    everyone = lax.all_to_all(copies, AXES, 0, 0, tiled=True)
    return pl.pallas_call(
        pressure_kernel,
        out_shape=tile,
        in_specs=[vmem] * 7,
        out_specs=vmem,
        scratch_shapes=[pltpu.VMEM((4, layers // BLOCK_Z, layers), f32)],
        compiler_params=params,
        name="pressure",
    )(everyone, *fields)


def solution(mesh):
    def per_device(facies, *others):
        tile_x, tile_y, layers = facies.shape
        total_x = tile_x * mesh.shape["gx"]
        total_y = tile_y * mesh.shape["gy"]
        one_column = total_x == BLOCK_X and total_y == BLOCK_Y
        fits = layers % 128 == 0 and tile_y % 8 == 0 and min(tile_x, tile_y) >= MARGIN
        step = column_step if one_column and fits else general_step
        return step(facies, *others)

    in_specs = (P("gx", "gy", None), P("gx", "gy", None), P(), P(), P(), P(), P())
    out_specs = P("gx", "gy", None)
    return jax.shard_map(
        per_device, mesh=mesh, in_specs=in_specs, out_specs=out_specs, check_vma=False
    )
```

```python
import jax
import jax.numpy as jnp
import numpy as np
from jax import lax
from jax.experimental import pallas as pl
from jax.experimental.pallas import tpu as pltpu
from jax.sharding import PartitionSpec as P

BLOCK_X = 64
BLOCK_Y = 64
BLOCK_Z = 16
SWEEPS = 3


RELAX_WEIGHT = 2.0 / 3.0
HIGHEST = lax.Precision.HIGHEST
first_bits = np.array([0, 0, 0, 0, 1, 1, 1, 1], dtype=np.int32)
second_bits = np.array([0, 0, 1, 1, 0, 0, 1, 1], dtype=np.int32)
third_bits = np.array([0, 1, 0, 1, 0, 1, 0, 1], dtype=np.int32)
shift_along_x = np.array([0, 2, -2, 0, 0, 0, 0], dtype=np.int32)
shift_along_y = np.array([0, 0, 0, 2, -2, 0, 0], dtype=np.int32)
shift_along_z = np.array([0, 0, 0, 0, 0, 2, -2], dtype=np.int32)


def with_halo(value, sides, width):
    for axis, dim in sides:
        size, length = (lax.axis_size(axis), value.shape[dim])
        up = [(i, (i + 1) % size) for i in range(size - 1)]
        down = [(j, i) for i, j in up]
        last = lax.slice_in_dim(value, length - width, length, axis=dim)
        initial = lax.slice_in_dim(value, 0, width, axis=dim)
        before = lax.ppermute(last, axis, up)
        after = lax.ppermute(initial, axis, down)
        value = jnp.concatenate([before, value, after], axis=dim)
    return value


def support_of(coords, block_size, parity):
    return parity + 2 * jnp.floor_divide(
        coords + block_size // 2 - block_size * parity, 2 * block_size
    )


def parity_nodes(coords, block_size):
    return jnp.stack([support_of(coords, block_size, 0), support_of(coords, block_size, 1)])


def parity_start(coords, block_size):
    node_ids = parity_nodes(coords, block_size)
    return (node_ids == jnp.floor_divide(coords, block_size)[None]).astype(jnp.float32)


def parity_same(coords, block_size):
    node_here = parity_nodes(coords[:-1], block_size)
    node_next = parity_nodes(coords[1:], block_size)
    return (node_here == node_next).astype(jnp.float32)


def harmonic(left_perm, right_perm):
    return 2.0 * left_perm * right_perm / (left_perm + right_perm)


def face_pad(values_in, dim_id, before):
    widths = [(0, 0), (0, 0), (0, 0)]
    widths[dim_id] = (1, 0) if before else (0, 1)
    return jnp.pad(values_in, widths)


def expand(line_in, dim_id):
    new_shape = [1, 1, 1]
    new_shape[dim_id] = line_in.shape[0]
    return line_in.reshape(new_shape)


def split_faces(values_in, dim_id):
    length = values_in.shape[dim_id]
    below_part = lax.slice_in_dim(values_in, 0, length - 1, axis=dim_id)
    above_part = lax.slice_in_dim(values_in, 1, length, axis=dim_id)
    return (below_part, above_part)


def cut_apply(values_in, storage, trans_all, same_all):
    result = storage * values_in
    for dim_id in range(3):
        trans_face = trans_all[dim_id]
        same_line = expand(same_all[dim_id], dim_id)
        below_part, above_part = split_faces(values_in, dim_id)
        result = result + face_pad(
            trans_face * (below_part - same_line * above_part), dim_id, False
        )
        result = result + face_pad(trans_face * (above_part - same_line * below_part), dim_id, True)
    return result


def rim_terms(values_in, trans_all, same_all):
    result = []
    for dim_id in range(3):
        trans_face = trans_all[dim_id]
        cross_mask = 1.0 - expand(same_all[dim_id], dim_id)
        below_part, above_part = split_faces(values_in, dim_id)
        result.append(face_pad(-trans_face * cross_mask * above_part, dim_id, False))
        result.append(face_pad(-trans_face * cross_mask * below_part, dim_id, True))
    return result


def diagonal_of(storage, trans_all):
    result = storage
    for dim_id in range(3):
        result = (
            result
            + face_pad(trans_all[dim_id], dim_id, False)
            + face_pad(trans_all[dim_id], dim_id, True)
        )
    return result


def lookup(facies, code_table):
    result = jnp.zeros(facies.shape, jnp.float32)
    for code_id in range(code_table.shape[0]):
        result = result + jnp.where(facies == code_id, code_table[code_id], 0.0)
    return result


def flatten_node(index_x, index_y, index_z, counts):
    count_x, count_y, count_z = counts
    flat_ids = (
        jnp.clip(index_x, 0, count_x - 1) * count_y + jnp.clip(index_y, 0, count_y - 1)
    ) * count_z
    return (flat_ids + jnp.clip(index_z, 0, count_z - 1)).astype(jnp.int32)


def tile_indices(anchor_x, anchor_y, counts):
    count_x, count_y, count_z = counts
    row_x = parity_nodes(jnp.reshape(anchor_x, (1,)), BLOCK_X)[first_bits][:, 0]
    row_y = parity_nodes(jnp.reshape(anchor_y, (1,)), BLOCK_Y)[second_bits][:, 0]
    seg_first = jnp.maximum(jnp.arange(count_z + 1, dtype=jnp.int32) * BLOCK_Z - BLOCK_Z // 2, 0)
    row_z = parity_nodes(seg_first, BLOCK_Z)[third_bits]
    row_ids = flatten_node(row_x[:, None], row_y[:, None], row_z, counts)
    col_ids = flatten_node(
        row_x[:, None, None] + jnp.asarray(shift_along_x)[None, :, None],
        row_y[:, None, None] + jnp.asarray(shift_along_y)[None, :, None],
        row_z[:, None, :] + jnp.asarray(shift_along_z)[None, :, None],
        counts,
    )
    entry_ids = row_ids[None, :, None, :] * (count_x * count_y * count_z) + col_ids[:, None, :, :]
    return (entry_ids, row_ids)


def segment_matrix(layers, segment_count):
    seg_of = (jnp.arange(layers, dtype=jnp.int32) + BLOCK_Z // 2) // BLOCK_Z
    return (seg_of[:, None] == jnp.arange(segment_count, dtype=jnp.int32)[None, :]).astype(
        jnp.float32
    )


def solve_coarse(coarse, coarse_rhs):
    factor = jnp.linalg.cholesky(coarse)
    middle = lax.linalg.triangular_solve(factor, coarse_rhs[:, None], left_side=True, lower=True)
    return lax.linalg.triangular_solve(
        factor, middle, left_side=True, lower=True, transpose_a=True
    )[:, 0]


def geometry(coeffs, margin, anchor_x, anchor_y, total_x, total_y):
    coord_x = anchor_x - margin + jnp.arange(coeffs.shape[1], dtype=jnp.int32)
    coord_y = anchor_y - margin + jnp.arange(coeffs.shape[2], dtype=jnp.int32)
    coord_z = jnp.arange(coeffs.shape[3], dtype=jnp.int32)
    inside_x = (coord_x >= 0) & (coord_x < total_x)
    inside_y = (coord_y >= 0) & (coord_y < total_y)
    inside = inside_x[:, None, None] & inside_y[None, :, None]
    perm_safe = jnp.where(inside, coeffs[0], 1.0)
    storage = jnp.where(inside, coeffs[1], 1.0)
    valid_x = (inside_x[:-1] & inside_x[1:]).astype(jnp.float32)
    valid_y = (inside_y[:-1] & inside_y[1:]).astype(jnp.float32)
    trans_x = harmonic(perm_safe[:-1], perm_safe[1:]) * valid_x[:, None, None]
    trans_y = harmonic(perm_safe[:, :-1], perm_safe[:, 1:]) * valid_y[None, :, None]
    trans_z = harmonic(perm_safe[:, :, :-1], perm_safe[:, :, 1:])
    trans_all = (trans_x, trans_y, trans_z)
    same_all = (
        parity_same(coord_x, BLOCK_X)[first_bits],
        parity_same(coord_y, BLOCK_Y)[second_bits],
        parity_same(coord_z, BLOCK_Z)[third_bits],
    )
    starts = (
        parity_start(coord_x, BLOCK_X)[first_bits],
        parity_start(coord_y, BLOCK_Y)[second_bits],
        parity_start(coord_z, BLOCK_Z)[third_bits],
    )
    return (storage, trans_all, diagonal_of(storage, trans_all), same_all, starts)


def initial(geo_set):
    start_x, start_y, start_z = geo_set[4]
    return start_x[:, :, None, None] * start_y[:, None, :, None] * start_z[:, None, None, :]


def smooth(basis_ext, geo_set):
    storage, trans_all, diagonal, same_all, _ = geo_set

    def change_of(values_in, same_x, same_y, same_z):
        return (
            -RELAX_WEIGHT
            * cut_apply(values_in, storage, trans_all, (same_x, same_y, same_z))
            / diagonal
        )

    changes = jax.vmap(change_of)(basis_ext, same_all[0], same_all[1], same_all[2])[:, 1:-1, 1:-1]
    interior = basis_ext[:, 1:-1, 1:-1]
    change_sum = jnp.sum(changes, axis=0)
    return interior + changes - interior * change_sum[None]


def basis_halo(basis_now):
    return with_halo(basis_now, (("gx", 1), ("gy", 2)), 1)


def general_step(facies, source, facies_perm, facies_store, well_x, well_y, well_rate):
    tile_x, tile_y, layers = facies.shape
    devs_x = lax.axis_size("gx")
    devs_y = lax.axis_size("gy")
    total_x = tile_x * devs_x
    total_y = tile_y * devs_y
    anchor_x = lax.axis_index("gx") * tile_x
    anchor_y = lax.axis_index("gy") * tile_y
    coeffs = jnp.stack([lookup(facies, facies_perm), lookup(facies, facies_store)])
    coeff_wide = with_halo(coeffs, (("gx", 1), ("gy", 2)), 1)
    geo_one = geometry(coeff_wide, 1, anchor_x, anchor_y, total_x, total_y)
    basis_now = initial(geo_one)[:, 1:-1, 1:-1]
    for _ in range(SWEEPS):
        basis_now = smooth(basis_halo(basis_now), geo_one)
    basis_now = basis_halo(basis_now)
    storage, trans_all, diagonal, same_all, _ = geo_one

    def terms_of(values_in, same_x, same_y, same_z):
        same_three = (same_x, same_y, same_z)
        return jnp.stack(
            [cut_apply(values_in, storage, trans_all, same_three)]
            + rim_terms(values_in, trans_all, same_three)
        )

    term_stack = jax.vmap(terms_of)(basis_now, same_all[0], same_all[1], same_all[2])[
        :, :, 1:-1, 1:-1
    ]
    interior = basis_now[:, 1:-1, 1:-1]
    count_x = total_x // BLOCK_X
    count_y = total_y // BLOCK_Y
    count_z = layers // BLOCK_Z
    counts = (count_x, count_y, count_z)
    coarse_count = count_x * count_y * count_z
    zmatrix = segment_matrix(layers, count_z + 1)
    gram_local = jnp.einsum("apqz,cspqz->casz", interior, term_stack, precision=HIGHEST)
    gram_local = jnp.einsum("casz,zg->casg", gram_local, zmatrix, precision=HIGHEST)
    cell_x = anchor_x + jnp.arange(tile_x, dtype=jnp.int32)
    cell_y = anchor_y + jnp.arange(tile_y, dtype=jnp.int32)
    hit_x = (well_x[:, None] == cell_x[None, :]).astype(jnp.float32)
    hit_y = (well_y[:, None] == cell_y[None, :]).astype(jnp.float32)
    column = jnp.einsum("w,wx,wy->xy", well_rate, hit_x, hit_y, precision=HIGHEST)
    rhs_fine = source + column[:, :, None] / layers
    rhs_local = jnp.einsum("apqz,pqz->az", interior, rhs_fine, precision=HIGHEST)
    rhs_local = jnp.einsum("az,zg->ag", rhs_local, zmatrix, precision=HIGHEST)
    entry_ids, row_ids = tile_indices(anchor_x, anchor_y, counts)
    local_matrix = (
        jnp.zeros((coarse_count * coarse_count,), jnp.float32)
        .at[entry_ids.reshape(-1)]
        .add(gram_local.reshape(-1))
    )
    local_matrix = local_matrix.reshape(coarse_count, coarse_count)
    local_rhs = (
        jnp.zeros((coarse_count,), jnp.float32).at[row_ids.reshape(-1)].add(rhs_local.reshape(-1))
    )
    coarse, coarse_rhs = lax.psum((local_matrix, local_rhs), ("gx", "gy"))
    coarse_solution = solve_coarse(coarse, coarse_rhs)
    values_at = coarse_solution[row_ids]
    per_layer = jnp.einsum("ag,zg->az", values_at, zmatrix, precision=HIGHEST)
    prolonged = jnp.einsum("apqz,az->pqz", interior, per_layer, precision=HIGHEST)
    prolonged_ext = with_halo(prolonged, (("gx", 0), ("gy", 1)), 1)
    ones_all = (
        jnp.ones((tile_x + 1,), jnp.float32),
        jnp.ones((tile_y + 1,), jnp.float32),
        jnp.ones((layers - 1,), jnp.float32),
    )
    applied = cut_apply(prolonged_ext, storage, trans_all, ones_all)[1:-1, 1:-1]
    return prolonged + RELAX_WEIGHT * (rhs_fine - applied) / diagonal[1:-1, 1:-1]


MARGIN = SWEEPS + 1
AXES = ("gx", "gy")
VMEM_BYTES = 16 * 2**20


def swap_along(value, axis, first):
    sizes = {name_: lax.axis_size(name_) for name_ in AXES}
    other = AXES[1 - AXES.index(axis)]
    pairs = []
    for gx in range(sizes[AXES[0]]):
        for gy in range(sizes[AXES[1]]):
            place = {AXES[0]: gx, AXES[1]: gy}
            partner = dict(place)
            along = first + ((place[axis] - first) ^ 1) if place[axis] >= first else -1
            if 0 <= along < sizes[axis]:
                partner[axis] = along
            else:
                partner[other] = place[other] ^ 1
            if partner[other] < sizes[other]:
                pairs.append(tuple(p[AXES[0]] * sizes[AXES[1]] + p[AXES[1]] for p in (place, partner)))
    return lax.ppermute(value, AXES, pairs)


def wide_tile(facies):
    count = facies.shape[0]
    even_x, even_y = (lax.axis_index(axis) % 2 == 0 for axis in AXES)

    def end_planes(value, at_first):
        return jnp.where(at_first, value[:MARGIN], value[count - MARGIN :])

    far = swap_along(facies, "gy", 1)
    near = swap_along(facies, "gy", 0)
    beside = swap_along(end_planes(facies, ~even_x), "gx", 0)
    before = jnp.where(even_y, far[:, -MARGIN:], near[:, -MARGIN:])
    after = jnp.where(even_y, near[:, :MARGIN], far[:, :MARGIN])
    rest = jnp.concatenate([after, before], axis=1)
    own = jnp.concatenate([facies, rest], axis=1)
    far = swap_along(end_planes(own, even_x), "gx", 1)
    corners = swap_along(end_planes(rest, ~even_x), "gx", 0)
    near = jnp.concatenate([beside, corners], axis=1)
    return own, jnp.where(even_x, far, near), jnp.where(even_x, near, far)


def lane_iota(shape):
    return lax.broadcasted_iota(jnp.int32, shape, len(shape) - 1)


def face_ends(layer, parity):
    return lax.rem(layer + 1 + BLOCK_Z // 2 + BLOCK_Z * parity, 2 * BLOCK_Z) == 0


def in_grid(layer, parity, count):
    shifted = layer + BLOCK_Z // 2 + BLOCK_Z * parity
    node = 2 * (shifted // (2 * BLOCK_Z)) - parity
    return (node >= 0) & (node < count)


def up(value, axis):
    return pltpu.roll(value, value.shape[axis] - 1, axis)


def down(value, axis):
    return pltpu.roll(value, 1, axis)


def code_select(table, codes):
    result = jnp.broadcast_to(table[0], codes.shape)
    for code_id in range(1, len(table)):
        result = jnp.where(codes == code_id, table[code_id], result)
    return result


def plane_faces(resist, store, face_y):
    layer = lane_iota(resist.shape)
    y_face = jnp.where(face_y, 2.0 / (resist + up(resist, 0)), 0.0)
    z_face = jnp.where(layer == resist.shape[1] - 1, 0.0, 2.0 / (resist + up(resist, 1)))
    part = store + y_face + down(y_face, 0) + z_face + down(z_face, 1)
    z_faces = [jnp.where(face_ends(layer, parity), 0.0, z_face) for parity in (0, 1)]
    return y_face, z_faces[0], z_faces[1], part


def y_face_mask(shape, tile_y):
    row = lax.broadcasted_iota(jnp.int32, shape, 0)
    place = lax.axis_index("gy") * tile_y + jnp.where(row < tile_y + MARGIN, row, row - shape[0])
    inside = (place >= 0) & (place + 1 < lax.axis_size("gy") * tile_y)
    return inside & (row != tile_y + MARGIN - 1)


def sweep_planes(low, high, read, write, face_x, face_y, face_z, scale):
    if low >= high:
        return
    here = read(low)
    flux_before = face_x(low - 1) * (here - read(low - 1))
    for plane in range(low, high):
        beyond = read(plane + 1)
        flux = face_x(plane) * (beyond - here)
        flux_y = face_y(plane) * (up(here, 0) - here)
        above = up(here, 1)
        gain = above * (1.0 - here)
        loss = here * (1.0 - above)
        z0, z1 = face_z(plane)
        total = (flux - flux_before) + (flux_y - down(flux_y, 0))
        total = total + (z0 * gain - z1 * loss) + down(z0 * loss - z1 * gain, 1)
        write(plane, here + scale(plane) * total)
        here, flux_before = (beyond, flux)


def start_field(shape):
    return jnp.where(lax.rem(lane_iota(shape) // BLOCK_Z, 2) == 0, 1.0, 0.0)


def tile_kernel(
    rows_ref, source_ref, perm_ref, store_ref, well_x_ref, well_y_ref, well_rate_ref,
    table_ref, resist_ref, storage_ref, x_ref, y_ref, z0_ref, z1_ref, part_ref, scale_ref, rhs_ref,
    *field_refs,
):
    tile_x, rows, layers = rows_ref.shape
    tile_y = source_ref.shape[1]
    anchor_x = lax.axis_index("gx") * tile_x
    anchor_y = lax.axis_index("gy") * tile_y
    codes = perm_ref.shape[0]
    resists = [
        1.0 / jnp.full((1, layers), perm_ref[code], jnp.float32) for code in range(codes)
    ]
    stores = [jnp.full((1, layers), store_ref[code], jnp.float32) for code in range(codes)]
    for code in range(codes):
        table_ref[code : code + 1] = resists[code]
        table_ref[codes + code : codes + code + 1] = stores[code]
    face_y = y_face_mask((rows, layers), tile_y)
    hit_y = (
        lax.broadcasted_iota(jnp.int32, (tile_y, well_y_ref.shape[1]), 0) + anchor_y
        == well_y_ref[...]
    )
    before, x_before, part_before = (None, None, None)
    for plane in range(tile_x):
        resist = code_select(resists, rows_ref[plane])
        store = code_select(stores, rows_ref[plane])
        y_face, z0, z1, part = plane_faces(resist, store, face_y)
        resist_ref[plane] = resist
        storage_ref[plane] = store
        y_ref[plane] = y_face
        z0_ref[plane] = z0
        z1_ref[plane] = z1
        part_ref[plane] = part
        if plane:
            x_face = 2.0 / (before + resist)
            x_ref[plane - 1] = x_face
            if plane > 1:
                scale_ref[plane - 1] = RELAX_WEIGHT / (part_before + x_face + x_before)
            x_before = x_face
        before, part_before = (resist, part)
        hit = hit_y & (well_x_ref[...] == anchor_x + plane)
        column = jnp.sum(jnp.where(hit, well_rate_ref[...], 0.0), axis=1, keepdims=True)
        rhs_ref[plane] = source_ref[plane] + column / layers
    start = start_field((rows, layers))
    read = lambda plane: start
    for sweep_id, field in enumerate(field_refs):
        sweep_planes(
            1 + sweep_id,
            tile_x - 1 - sweep_id,
            read,
            field.__setitem__,
            x_ref.__getitem__,
            y_ref.__getitem__,
            lambda plane: (z0_ref[plane], z1_ref[plane]),
            scale_ref.__getitem__,
        )
        read = field.__getitem__


def basis_kernel(*refs):
    before_ref, after_ref, table_ref, resist_ref, storage_ref, x_ref, y_ref, z0_ref, z1_ref = refs[:9]
    part_ref, scale_ref, rhs_ref = refs[9:12]
    near_fields = refs[12 : 12 + SWEEPS]
    refs = refs[12 + SWEEPS :]
    packed_ref, basis_ref, side_ref, rhs_out_ref, store_out_ref, up_ref, down_ref = refs[:7]
    scale_far, x_far, y_far, z0_far, z1_far, sums_ref = refs[7:13]
    far_fields = refs[13:]
    tile_x, tile_y, layers = rhs_ref.shape
    rows = resist_ref.shape[1]
    planes = tile_x + 2 * MARGIN
    shape = (rows, layers)
    anchor_x = lax.axis_index("gx") * tile_x
    total_x = lax.axis_size("gx") * tile_x
    face_mask_y = y_face_mask(shape, tile_y)
    codes = table_ref.shape[0] // 2
    table = [table_ref[i : i + 1] for i in range(2 * codes)]

    def own(plane, depth=0):
        return MARGIN + depth <= plane < MARGIN + tile_x - depth

    def face_x(plane):
        inner = own(plane) and own(plane + 1)
        return x_ref[plane - MARGIN] if inner else x_far[plane]

    def near_or_far(near, far, depth=0):
        return lambda plane: near[plane - MARGIN] if own(plane, depth) else far[plane]

    face_y = near_or_far(y_ref, y_far)
    face_z0 = near_or_far(z0_ref, z0_far)
    face_z1 = near_or_far(z1_ref, z1_far)
    scale = near_or_far(scale_ref, scale_far, 1)
    resist_last, x_last, part_last = (None, None, None)
    for plane in range(planes):
        part = None
        if own(plane):
            resist = resist_ref[plane - MARGIN]
            part = part_ref[plane - MARGIN]
        else:
            strip = before_ref if plane < MARGIN else after_ref
            facies = strip[plane if plane < MARGIN else plane - MARGIN - tile_x]
            resist = code_select(table[:codes], facies)
            if 0 < plane < planes - 1:
                store = code_select(table[codes:], facies)
                y_far[plane], z0_far[plane], z1_far[plane], part = plane_faces(
                    resist, store, face_mask_y
                )
        if plane:
            if own(plane - 1) and own(plane):
                x_face = face_x(plane - 1)
            else:
                here = anchor_x + plane - 1 - MARGIN
                x_face = 2.0 / (resist_last + resist)
                x_face = jnp.where((here >= 0) & (here + 1 < total_x), x_face, 0.0)
                x_far[plane - 1] = x_face
            if plane > 1 and not own(plane - 1, 1):
                scale_far[plane - 1] = RELAX_WEIGHT / (part_last + x_face + x_last)
            x_last = x_face
        resist_last, part_last = (resist, part)

    start = start_field(shape)
    read = lambda plane: start
    for sweep_id in range(SWEEPS):
        depth = 1 + sweep_id
        first_end = min(MARGIN + depth, planes - depth)
        last_start = max(first_end, MARGIN + tile_x - depth)
        for low, high in ((depth, first_end), (last_start, planes - depth)):
            sweep_planes(
                low,
                high,
                read,
                far_fields[sweep_id].__setitem__,
                face_x,
                face_y,
                lambda plane: (face_z0(plane), face_z1(plane)),
                scale,
            )
        read = near_or_far(near_fields[sweep_id], far_fields[sweep_id], depth)

    tile = (tile_y, layers)
    cut_0 = face_ends(lane_iota(tile), 0)
    cut_any = cut_0 | face_ends(lane_iota(tile), 1)

    def inner(value):
        return value[:tile_y]

    sums = None
    for plane in range(tile_x):
        at = plane + MARGIN
        here_all = read(at)
        here = inner(here_all)
        step_y_all = up(here_all, 0) - here_all
        flux_y_all = y_ref[plane] * step_y_all
        flux_y = inner(flux_y_all)
        step_x = inner(read(at + 1)) - here
        flux_x = inner(face_x(at)) * step_x
        flux_before = inner(face_x(at - 1)) * (here - inner(read(at - 1)))
        z_face = jnp.maximum(inner(z0_ref[plane]), inner(z1_ref[plane]))
        above = up(here, 1)
        step_z = above - here
        energy_z = z_face * step_z * step_z
        other = 1.0 - here
        store = inner(storage_ref[plane])
        factor = inner(scale(at))
        rhs = rhs_ref[plane]
        below_end = jnp.where(cut_0, here, other)
        above_end = jnp.where(cut_0, above, 1.0 - above)
        z_cut = jnp.where(cut_any, z_face, 0.0)
        basis_ref[plane] = here
        side_ref[plane] = factor * (
            (flux_before - flux_x) + (inner(down(flux_y_all, 0)) - flux_y)
        )
        rhs_out_ref[plane] = factor * rhs
        store_out_ref[plane] = factor * store
        up_ref[plane] = factor * z_face
        down_ref[plane] = factor * down(z_face, 1)
        terms = (
            store * here * here,
            store * here * other,
            store * other * other,
            flux_x * step_x + flux_y * inner(step_y_all) + jnp.where(cut_any, 0.0, energy_z),
            jnp.where(cut_any, energy_z, 0.0),
            z_cut * below_end * below_end,
            z_cut * above_end * above_end,
            z_cut * below_end * above_end,
            here * rhs,
            other * rhs,
        )
        sums = terms if sums is None else [a + b for a, b in zip(sums, terms)]
    mass_00, mass_01, mass_11, energy, cut, low_2, high_2, low_high, rhs_0, rhs_1 = (
        jnp.sum(total, axis=0, keepdims=True) for total in sums
    )
    line = lane_iota((1, layers))
    count = layers // BLOCK_Z
    ends = (face_ends(line, 0), face_ends(line, 1))
    inside = (in_grid(line, 0, count), in_grid(line, 1, count))
    for parity, mass, right in ((0, mass_00, rhs_0), (1, mass_11, rhs_1)):
        own_end = jnp.where(ends[parity], low_2, cut)
        beyond_end = down(jnp.where(ends[parity], high_2, 0.0), 1)
        entry = mass + energy + own_end + beyond_end
        sums_ref[parity : parity + 1] = jnp.where(inside[parity], entry, 0.0)
        sums_ref[4 + parity : 5 + parity] = jnp.where(inside[parity], right, 0.0)
    sums_ref[2:3] = mass_01 - energy + (low_high - low_2) + down(low_high - high_2, 1)
    sums_ref[3:4] = -low_high
    sums_ref[6:8] = jnp.zeros((2, layers), jnp.float32)
    window = pltpu.roll(sums_ref[...], 0, 1, stride=1, stride_axis=0)
    width = 1
    while width < BLOCK_Z:
        window = window + pltpu.roll(window, width, 1)
        width *= 2
    row = lax.broadcasted_iota(jnp.int32, window.shape, 0)
    keep = lax.rem(lane_iota(window.shape) + layers - BLOCK_Z // 2 + 1 - row, BLOCK_Z) == 0
    packed = jnp.sum(jnp.where(keep, window, 0.0), axis=0, keepdims=True)
    packed_ref[...] = jnp.broadcast_to(packed, packed_ref.shape)


def solve_band(diagonal, first, second, right):
    count = len(diagonal)
    matrix = {(k, k): diagonal[k] for k in range(count)}
    for distance, band in ((1, first), (2, second)):
        for k in range(count - distance):
            matrix[k, k + distance] = band[k]
            matrix[k + distance, k] = band[k]
    left = list(range(count))
    steps = []
    while left:
        pivot = left.pop(0 if len(steps) % 2 == 0 else -1)
        inverse = 1.0 / matrix[pivot, pivot]
        linked = [k for k in left if (pivot, k) in matrix]
        lower = {k: matrix[pivot, k] * inverse for k in linked}
        for k in linked:
            right[k] = right[k] - lower[k] * right[pivot]
            for other in linked:
                if other >= k:
                    change = lower[k] * matrix[pivot, other]
                    entry = matrix[k, other] - change if (k, other) in matrix else -change
                    matrix[k, other] = entry
                    matrix[other, k] = entry
        steps.append((pivot, inverse, lower))
    values = [None] * count
    for pivot, inverse, lower in reversed(steps):
        value = right[pivot] * inverse
        for k, factor in lower.items():
            value = value - factor * values[k]
        values[pivot] = value
    return values


def pressure_kernel(
    rows_ref, basis_ref, side_ref, rhs_ref, store_ref, up_ref, down_ref, out_ref, entries
):
    tile_x, tile_y, layers = basis_ref.shape
    count = layers // BLOCK_Z
    half = BLOCK_Z // 2
    shape = (count, layers)
    node = lax.broadcasted_iota(jnp.int32, shape, 0)
    layer = lane_iota(shape)
    packed = jnp.sum(rows_ref[...], axis=0, keepdims=True)

    def held(segment, kind):
        return layer == lax.rem(segment * BLOCK_Z + half - 1 + kind, layers)

    parity = lax.rem(node, 2)
    own = held(node, parity) | held(node + 1, parity)
    right = held(node, parity + 4) | held(node + 1, parity + 4)
    masks = (own, held(node + 1, 2), held(node + 1, 3), right)
    for part_id, mask in enumerate(masks):
        part = jnp.where(mask, packed, 0.0)
        entries[part_id] = jnp.broadcast_to(jnp.sum(part, axis=1, keepdims=True), shape)
    values = solve_band(
        *([entries[part_id, k : k + 1] for k in range(count)] for part_id in range(4))
    )
    line = lane_iota((1, layers))
    fields = [jnp.zeros((1, layers), jnp.float32)] * 2
    for k in range(count):
        support = (line >= k * BLOCK_Z - half) & (line < k * BLOCK_Z + 3 * half)
        fields[k % 2] = jnp.where(support, values[k], fields[k % 2])
    value_0 = jnp.broadcast_to(fields[0], (tile_y, layers))
    value_1 = jnp.broadcast_to(fields[1], (tile_y, layers))
    apart = value_0 - value_1
    for plane in range(tile_x):
        here = basis_ref[plane]
        prolonged = here * value_0 + (1.0 - here) * value_1
        applied = (
            store_ref[plane] * prolonged
            + apart * side_ref[plane]
            + up_ref[plane] * (prolonged - up(prolonged, 1))
            + down_ref[plane] * (prolonged - down(prolonged, 1))
        )
        out_ref[plane] = prolonged + (rhs_ref[plane] - applied)


def column_step(facies, source, facies_perm, facies_store, well_x, well_y, well_rate):
    tile_x, tile_y, layers = facies.shape
    rows = tile_y + 2 * MARGIN
    planes = tile_x + 2 * MARGIN
    size = lax.axis_size(AXES)
    f32 = jnp.float32
    tile = jax.ShapeDtypeStruct(facies.shape, f32)
    wide = jax.ShapeDtypeStruct((tile_x, rows, layers), f32)
    vmem = pl.BlockSpec(memory_space=pltpu.VMEM)
    smem = pl.BlockSpec(memory_space=pltpu.SMEM)
    params = pltpu.CompilerParams(vmem_limit_bytes=VMEM_BYTES)

    own, before, after = wide_tile(facies)
    near = pl.pallas_call(
        tile_kernel,
        out_shape=(jax.ShapeDtypeStruct((2 * facies_perm.shape[0], layers), f32),)
        + (wide,) * 8
        + (tile,)
        + (wide,) * SWEEPS,
        in_specs=[vmem, vmem, smem, smem, vmem, vmem, vmem],
        out_specs=(vmem,) * (10 + SWEEPS),
        compiler_params=params,
        cost_estimate=pl.CostEstimate(flops=3000000, bytes_accessed=1000000, transcendentals=0),
        name="tile",
    )(
        own,
        source,
        facies_perm,
        facies_store,
        well_x[None, :],
        well_y[None, :],
        well_rate[None, :],
    )
    copies, *fields = pl.pallas_call(
        basis_kernel,
        out_shape=(jax.ShapeDtypeStruct((size, layers), f32),) + (tile,) * 6,
        in_specs=[vmem] * (12 + SWEEPS),
        out_specs=(vmem,) * 7,
        scratch_shapes=[pltpu.VMEM((planes, rows, layers), f32)] * 5
        + [pltpu.VMEM((8, layers), f32)]
        + [pltpu.VMEM((planes, rows, layers), f32)] * SWEEPS,
        compiler_params=params,
        name="basis",
    )(before, after, *near)
    everyone = lax.all_to_all(copies, AXES, 0, 0, tiled=True)
    return pl.pallas_call(
        pressure_kernel,
        out_shape=tile,
        in_specs=[vmem] * 7,
        out_specs=vmem,
        scratch_shapes=[pltpu.VMEM((4, layers // BLOCK_Z, layers), f32)],
        compiler_params=params,
        name="pressure",
    )(everyone, *fields)


def solution(mesh):
    def per_device(facies, *others):
        tile_x, tile_y, layers = facies.shape
        total_x = tile_x * mesh.shape["gx"]
        total_y = tile_y * mesh.shape["gy"]
        one_column = total_x == BLOCK_X and total_y == BLOCK_Y
        fits = layers % 128 == 0 and tile_y % 8 == 0 and min(tile_x, tile_y) >= MARGIN
        step = column_step if one_column and fits else general_step
        return step(facies, *others)

    in_specs = (P("gx", "gy", None), P("gx", "gy", None), P(), P(), P(), P(), P())
    out_specs = P("gx", "gy", None)
    return jax.shard_map(
        per_device, mesh=mesh, in_specs=in_specs, out_specs=out_specs, check_vma=False
    )
```

```python
import jax
import jax.numpy as jnp
import numpy as np
from jax import lax
from jax.experimental import pallas as pl
from jax.experimental.pallas import tpu as pltpu
from jax.sharding import PartitionSpec as P

BLOCK_X = 64
BLOCK_Y = 64
BLOCK_Z = 16
SWEEPS = 3


RELAX_WEIGHT = 2.0 / 3.0
HIGHEST = lax.Precision.HIGHEST
first_bits = np.array([0, 0, 0, 0, 1, 1, 1, 1], dtype=np.int32)
second_bits = np.array([0, 0, 1, 1, 0, 0, 1, 1], dtype=np.int32)
third_bits = np.array([0, 1, 0, 1, 0, 1, 0, 1], dtype=np.int32)
shift_along_x = np.array([0, 2, -2, 0, 0, 0, 0], dtype=np.int32)
shift_along_y = np.array([0, 0, 0, 2, -2, 0, 0], dtype=np.int32)
shift_along_z = np.array([0, 0, 0, 0, 0, 2, -2], dtype=np.int32)


def with_halo(value, sides, width):
    for axis, dim in sides:
        size, length = (lax.axis_size(axis), value.shape[dim])
        up = [(i, (i + 1) % size) for i in range(size - 1)]
        down = [(j, i) for i, j in up]
        last = lax.slice_in_dim(value, length - width, length, axis=dim)
        initial = lax.slice_in_dim(value, 0, width, axis=dim)
        before = lax.ppermute(last, axis, up)
        after = lax.ppermute(initial, axis, down)
        value = jnp.concatenate([before, value, after], axis=dim)
    return value


def support_of(coords, block_size, parity):
    return parity + 2 * jnp.floor_divide(
        coords + block_size // 2 - block_size * parity, 2 * block_size
    )


def parity_nodes(coords, block_size):
    return jnp.stack([support_of(coords, block_size, 0), support_of(coords, block_size, 1)])


def parity_start(coords, block_size):
    node_ids = parity_nodes(coords, block_size)
    return (node_ids == jnp.floor_divide(coords, block_size)[None]).astype(jnp.float32)


def parity_same(coords, block_size):
    node_here = parity_nodes(coords[:-1], block_size)
    node_next = parity_nodes(coords[1:], block_size)
    return (node_here == node_next).astype(jnp.float32)


def harmonic(left_perm, right_perm):
    return 2.0 * left_perm * right_perm / (left_perm + right_perm)


def face_pad(values_in, dim_id, before):
    widths = [(0, 0), (0, 0), (0, 0)]
    widths[dim_id] = (1, 0) if before else (0, 1)
    return jnp.pad(values_in, widths)


def expand(line_in, dim_id):
    new_shape = [1, 1, 1]
    new_shape[dim_id] = line_in.shape[0]
    return line_in.reshape(new_shape)


def split_faces(values_in, dim_id):
    length = values_in.shape[dim_id]
    below_part = lax.slice_in_dim(values_in, 0, length - 1, axis=dim_id)
    above_part = lax.slice_in_dim(values_in, 1, length, axis=dim_id)
    return (below_part, above_part)


def cut_apply(values_in, storage, trans_all, same_all):
    result = storage * values_in
    for dim_id in range(3):
        trans_face = trans_all[dim_id]
        same_line = expand(same_all[dim_id], dim_id)
        below_part, above_part = split_faces(values_in, dim_id)
        result = result + face_pad(
            trans_face * (below_part - same_line * above_part), dim_id, False
        )
        result = result + face_pad(trans_face * (above_part - same_line * below_part), dim_id, True)
    return result


def rim_terms(values_in, trans_all, same_all):
    result = []
    for dim_id in range(3):
        trans_face = trans_all[dim_id]
        cross_mask = 1.0 - expand(same_all[dim_id], dim_id)
        below_part, above_part = split_faces(values_in, dim_id)
        result.append(face_pad(-trans_face * cross_mask * above_part, dim_id, False))
        result.append(face_pad(-trans_face * cross_mask * below_part, dim_id, True))
    return result


def diagonal_of(storage, trans_all):
    result = storage
    for dim_id in range(3):
        result = (
            result
            + face_pad(trans_all[dim_id], dim_id, False)
            + face_pad(trans_all[dim_id], dim_id, True)
        )
    return result


def lookup(facies, code_table):
    result = jnp.zeros(facies.shape, jnp.float32)
    for code_id in range(code_table.shape[0]):
        result = result + jnp.where(facies == code_id, code_table[code_id], 0.0)
    return result


def flatten_node(index_x, index_y, index_z, counts):
    count_x, count_y, count_z = counts
    flat_ids = (
        jnp.clip(index_x, 0, count_x - 1) * count_y + jnp.clip(index_y, 0, count_y - 1)
    ) * count_z
    return (flat_ids + jnp.clip(index_z, 0, count_z - 1)).astype(jnp.int32)


def tile_indices(anchor_x, anchor_y, counts):
    count_x, count_y, count_z = counts
    row_x = parity_nodes(jnp.reshape(anchor_x, (1,)), BLOCK_X)[first_bits][:, 0]
    row_y = parity_nodes(jnp.reshape(anchor_y, (1,)), BLOCK_Y)[second_bits][:, 0]
    seg_first = jnp.maximum(jnp.arange(count_z + 1, dtype=jnp.int32) * BLOCK_Z - BLOCK_Z // 2, 0)
    row_z = parity_nodes(seg_first, BLOCK_Z)[third_bits]
    row_ids = flatten_node(row_x[:, None], row_y[:, None], row_z, counts)
    col_ids = flatten_node(
        row_x[:, None, None] + jnp.asarray(shift_along_x)[None, :, None],
        row_y[:, None, None] + jnp.asarray(shift_along_y)[None, :, None],
        row_z[:, None, :] + jnp.asarray(shift_along_z)[None, :, None],
        counts,
    )
    entry_ids = row_ids[None, :, None, :] * (count_x * count_y * count_z) + col_ids[:, None, :, :]
    return (entry_ids, row_ids)


def segment_matrix(layers, segment_count):
    seg_of = (jnp.arange(layers, dtype=jnp.int32) + BLOCK_Z // 2) // BLOCK_Z
    return (seg_of[:, None] == jnp.arange(segment_count, dtype=jnp.int32)[None, :]).astype(
        jnp.float32
    )


def solve_coarse(coarse, coarse_rhs):
    factor = jnp.linalg.cholesky(coarse)
    middle = lax.linalg.triangular_solve(factor, coarse_rhs[:, None], left_side=True, lower=True)
    return lax.linalg.triangular_solve(
        factor, middle, left_side=True, lower=True, transpose_a=True
    )[:, 0]


def geometry(coeffs, margin, anchor_x, anchor_y, total_x, total_y):
    coord_x = anchor_x - margin + jnp.arange(coeffs.shape[1], dtype=jnp.int32)
    coord_y = anchor_y - margin + jnp.arange(coeffs.shape[2], dtype=jnp.int32)
    coord_z = jnp.arange(coeffs.shape[3], dtype=jnp.int32)
    inside_x = (coord_x >= 0) & (coord_x < total_x)
    inside_y = (coord_y >= 0) & (coord_y < total_y)
    inside = inside_x[:, None, None] & inside_y[None, :, None]
    perm_safe = jnp.where(inside, coeffs[0], 1.0)
    storage = jnp.where(inside, coeffs[1], 1.0)
    valid_x = (inside_x[:-1] & inside_x[1:]).astype(jnp.float32)
    valid_y = (inside_y[:-1] & inside_y[1:]).astype(jnp.float32)
    trans_x = harmonic(perm_safe[:-1], perm_safe[1:]) * valid_x[:, None, None]
    trans_y = harmonic(perm_safe[:, :-1], perm_safe[:, 1:]) * valid_y[None, :, None]
    trans_z = harmonic(perm_safe[:, :, :-1], perm_safe[:, :, 1:])
    trans_all = (trans_x, trans_y, trans_z)
    same_all = (
        parity_same(coord_x, BLOCK_X)[first_bits],
        parity_same(coord_y, BLOCK_Y)[second_bits],
        parity_same(coord_z, BLOCK_Z)[third_bits],
    )
    starts = (
        parity_start(coord_x, BLOCK_X)[first_bits],
        parity_start(coord_y, BLOCK_Y)[second_bits],
        parity_start(coord_z, BLOCK_Z)[third_bits],
    )
    return (storage, trans_all, diagonal_of(storage, trans_all), same_all, starts)


def initial(geo_set):
    start_x, start_y, start_z = geo_set[4]
    return start_x[:, :, None, None] * start_y[:, None, :, None] * start_z[:, None, None, :]


def smooth(basis_ext, geo_set):
    storage, trans_all, diagonal, same_all, _ = geo_set

    def change_of(values_in, same_x, same_y, same_z):
        return (
            -RELAX_WEIGHT
            * cut_apply(values_in, storage, trans_all, (same_x, same_y, same_z))
            / diagonal
        )

    changes = jax.vmap(change_of)(basis_ext, same_all[0], same_all[1], same_all[2])[:, 1:-1, 1:-1]
    interior = basis_ext[:, 1:-1, 1:-1]
    change_sum = jnp.sum(changes, axis=0)
    return interior + changes - interior * change_sum[None]


def basis_halo(basis_now):
    return with_halo(basis_now, (("gx", 1), ("gy", 2)), 1)


def general_step(facies, source, facies_perm, facies_store, well_x, well_y, well_rate):
    tile_x, tile_y, layers = facies.shape
    devs_x = lax.axis_size("gx")
    devs_y = lax.axis_size("gy")
    total_x = tile_x * devs_x
    total_y = tile_y * devs_y
    anchor_x = lax.axis_index("gx") * tile_x
    anchor_y = lax.axis_index("gy") * tile_y
    coeffs = jnp.stack([lookup(facies, facies_perm), lookup(facies, facies_store)])
    coeff_wide = with_halo(coeffs, (("gx", 1), ("gy", 2)), 1)
    geo_one = geometry(coeff_wide, 1, anchor_x, anchor_y, total_x, total_y)
    basis_now = initial(geo_one)[:, 1:-1, 1:-1]
    for _ in range(SWEEPS):
        basis_now = smooth(basis_halo(basis_now), geo_one)
    basis_now = basis_halo(basis_now)
    storage, trans_all, diagonal, same_all, _ = geo_one

    def terms_of(values_in, same_x, same_y, same_z):
        same_three = (same_x, same_y, same_z)
        return jnp.stack(
            [cut_apply(values_in, storage, trans_all, same_three)]
            + rim_terms(values_in, trans_all, same_three)
        )

    term_stack = jax.vmap(terms_of)(basis_now, same_all[0], same_all[1], same_all[2])[
        :, :, 1:-1, 1:-1
    ]
    interior = basis_now[:, 1:-1, 1:-1]
    count_x = total_x // BLOCK_X
    count_y = total_y // BLOCK_Y
    count_z = layers // BLOCK_Z
    counts = (count_x, count_y, count_z)
    coarse_count = count_x * count_y * count_z
    zmatrix = segment_matrix(layers, count_z + 1)
    gram_local = jnp.einsum("apqz,cspqz->casz", interior, term_stack, precision=HIGHEST)
    gram_local = jnp.einsum("casz,zg->casg", gram_local, zmatrix, precision=HIGHEST)
    cell_x = anchor_x + jnp.arange(tile_x, dtype=jnp.int32)
    cell_y = anchor_y + jnp.arange(tile_y, dtype=jnp.int32)
    hit_x = (well_x[:, None] == cell_x[None, :]).astype(jnp.float32)
    hit_y = (well_y[:, None] == cell_y[None, :]).astype(jnp.float32)
    column = jnp.einsum("w,wx,wy->xy", well_rate, hit_x, hit_y, precision=HIGHEST)
    rhs_fine = source + column[:, :, None] / layers
    rhs_local = jnp.einsum("apqz,pqz->az", interior, rhs_fine, precision=HIGHEST)
    rhs_local = jnp.einsum("az,zg->ag", rhs_local, zmatrix, precision=HIGHEST)
    entry_ids, row_ids = tile_indices(anchor_x, anchor_y, counts)
    local_matrix = (
        jnp.zeros((coarse_count * coarse_count,), jnp.float32)
        .at[entry_ids.reshape(-1)]
        .add(gram_local.reshape(-1))
    )
    local_matrix = local_matrix.reshape(coarse_count, coarse_count)
    local_rhs = (
        jnp.zeros((coarse_count,), jnp.float32).at[row_ids.reshape(-1)].add(rhs_local.reshape(-1))
    )
    coarse, coarse_rhs = lax.psum((local_matrix, local_rhs), ("gx", "gy"))
    coarse_solution = solve_coarse(coarse, coarse_rhs)
    values_at = coarse_solution[row_ids]
    per_layer = jnp.einsum("ag,zg->az", values_at, zmatrix, precision=HIGHEST)
    prolonged = jnp.einsum("apqz,az->pqz", interior, per_layer, precision=HIGHEST)
    prolonged_ext = with_halo(prolonged, (("gx", 0), ("gy", 1)), 1)
    ones_all = (
        jnp.ones((tile_x + 1,), jnp.float32),
        jnp.ones((tile_y + 1,), jnp.float32),
        jnp.ones((layers - 1,), jnp.float32),
    )
    applied = cut_apply(prolonged_ext, storage, trans_all, ones_all)[1:-1, 1:-1]
    return prolonged + RELAX_WEIGHT * (rhs_fine - applied) / diagonal[1:-1, 1:-1]


MARGIN = SWEEPS + 1
AXES = ("gx", "gy")
VMEM_BYTES = 16 * 2**20


def swap_along(value, axis, first):
    sizes = {name_: lax.axis_size(name_) for name_ in AXES}
    other = AXES[1 - AXES.index(axis)]
    pairs = []
    for gx in range(sizes[AXES[0]]):
        for gy in range(sizes[AXES[1]]):
            place = {AXES[0]: gx, AXES[1]: gy}
            partner = dict(place)
            along = first + ((place[axis] - first) ^ 1) if place[axis] >= first else -1
            if 0 <= along < sizes[axis]:
                partner[axis] = along
            else:
                partner[other] = place[other] ^ 1
            if partner[other] < sizes[other]:
                pairs.append(tuple(p[AXES[0]] * sizes[AXES[1]] + p[AXES[1]] for p in (place, partner)))
    return lax.ppermute(value, AXES, pairs)


def wide_tile(facies):
    count = facies.shape[0]
    even_x, even_y = (lax.axis_index(axis) % 2 == 0 for axis in AXES)

    def end_planes(value, at_first):
        return jnp.where(at_first, value[:MARGIN], value[count - MARGIN :])

    far = swap_along(facies, "gy", 1)
    near = swap_along(facies, "gy", 0)
    beside = swap_along(end_planes(facies, ~even_x), "gx", 0)
    before = jnp.where(even_y, far[:, -MARGIN:], near[:, -MARGIN:])
    after = jnp.where(even_y, near[:, :MARGIN], far[:, :MARGIN])
    rest = jnp.concatenate([after, before], axis=1)
    own = jnp.concatenate([facies, rest], axis=1)
    far = swap_along(end_planes(own, even_x), "gx", 1)
    corners = swap_along(end_planes(rest, ~even_x), "gx", 0)
    near = jnp.concatenate([beside, corners], axis=1)
    return own, jnp.where(even_x, far, near), jnp.where(even_x, near, far)


def lane_iota(shape):
    return lax.broadcasted_iota(jnp.int32, shape, len(shape) - 1)


def face_ends(layer, parity):
    return lax.rem(layer + 1 + BLOCK_Z // 2 + BLOCK_Z * parity, 2 * BLOCK_Z) == 0


def in_grid(layer, parity, count):
    shifted = layer + BLOCK_Z // 2 + BLOCK_Z * parity
    node = 2 * (shifted // (2 * BLOCK_Z)) - parity
    return (node >= 0) & (node < count)


def up(value, axis):
    return pltpu.roll(value, value.shape[axis] - 1, axis)


def down(value, axis):
    return pltpu.roll(value, 1, axis)


def code_select(table, codes):
    result = jnp.broadcast_to(table[0], codes.shape)
    for code_id in range(1, len(table)):
        result = jnp.where(codes == code_id, table[code_id], result)
    return result


def plane_faces(resist, store, face_y):
    layer = lane_iota(resist.shape)
    y_face = jnp.where(face_y, 2.0 / (resist + up(resist, 0)), 0.0)
    z_face = jnp.where(layer == resist.shape[1] - 1, 0.0, 2.0 / (resist + up(resist, 1)))
    part = store + y_face + down(y_face, 0) + z_face + down(z_face, 1)
    z_faces = [jnp.where(face_ends(layer, parity), 0.0, z_face) for parity in (0, 1)]
    return y_face, z_faces[0], z_faces[1], part


def y_face_mask(shape, tile_y):
    row = lax.broadcasted_iota(jnp.int32, shape, 0)
    place = lax.axis_index("gy") * tile_y + jnp.where(row < tile_y + MARGIN, row, row - shape[0])
    inside = (place >= 0) & (place + 1 < lax.axis_size("gy") * tile_y)
    return inside & (row != tile_y + MARGIN - 1)


def sweep_planes(low, high, read, write, face_x, face_y, face_z, scale):
    if low >= high:
        return
    here = read(low)
    flux_before = face_x(low - 1) * (here - read(low - 1))
    for plane in range(low, high):
        beyond = read(plane + 1)
        flux = face_x(plane) * (beyond - here)
        flux_y = face_y(plane) * (up(here, 0) - here)
        above = up(here, 1)
        gain = above * (1.0 - here)
        loss = here * (1.0 - above)
        z0, z1 = face_z(plane)
        total = (flux - flux_before) + (flux_y - down(flux_y, 0))
        total = total + (z0 * gain - z1 * loss) + down(z0 * loss - z1 * gain, 1)
        write(plane, here + scale(plane) * total)
        here, flux_before = (beyond, flux)


def start_field(shape):
    return jnp.where(lax.rem(lane_iota(shape) // BLOCK_Z, 2) == 0, 1.0, 0.0)


def tile_kernel(
    rows_ref, source_ref, perm_ref, store_ref, well_x_ref, well_y_ref, well_rate_ref,
    table_ref, resist_ref, storage_ref, x_ref, y_ref, z0_ref, z1_ref, part_ref, scale_ref, rhs_ref,
    *field_refs,
):
    tile_x, rows, layers = rows_ref.shape
    tile_y = source_ref.shape[1]
    anchor_x = lax.axis_index("gx") * tile_x
    anchor_y = lax.axis_index("gy") * tile_y
    codes = perm_ref.shape[0]
    resists = [
        1.0 / jnp.full((1, layers), perm_ref[code], jnp.float32) for code in range(codes)
    ]
    stores = [jnp.full((1, layers), store_ref[code], jnp.float32) for code in range(codes)]
    for code in range(codes):
        table_ref[code : code + 1] = resists[code]
        table_ref[codes + code : codes + code + 1] = stores[code]
    face_y = y_face_mask((rows, layers), tile_y)
    hit_y = (
        lax.broadcasted_iota(jnp.int32, (tile_y, well_y_ref.shape[1]), 0) + anchor_y
        == well_y_ref[...]
    )
    before, x_before, part_before = (None, None, None)
    for plane in range(tile_x):
        resist = code_select(resists, rows_ref[plane])
        store = code_select(stores, rows_ref[plane])
        y_face, z0, z1, part = plane_faces(resist, store, face_y)
        resist_ref[plane] = resist
        storage_ref[plane] = store
        y_ref[plane] = y_face
        z0_ref[plane] = z0
        z1_ref[plane] = z1
        part_ref[plane] = part
        if plane:
            x_face = 2.0 / (before + resist)
            x_ref[plane - 1] = x_face
            if plane > 1:
                scale_ref[plane - 1] = RELAX_WEIGHT / (part_before + x_face + x_before)
            x_before = x_face
        before, part_before = (resist, part)
        hit = hit_y & (well_x_ref[...] == anchor_x + plane)
        column = jnp.sum(jnp.where(hit, well_rate_ref[...], 0.0), axis=1, keepdims=True)
        rhs_ref[plane] = source_ref[plane] + column / layers
    start = start_field((rows, layers))
    read = lambda plane: start
    for sweep_id, field in enumerate(field_refs):
        sweep_planes(
            1 + sweep_id,
            tile_x - 1 - sweep_id,
            read,
            field.__setitem__,
            x_ref.__getitem__,
            y_ref.__getitem__,
            lambda plane: (z0_ref[plane], z1_ref[plane]),
            scale_ref.__getitem__,
        )
        read = field.__getitem__


def basis_kernel(*refs):
    before_ref, after_ref, table_ref, resist_ref, storage_ref, x_ref, y_ref, z0_ref, z1_ref = refs[:9]
    part_ref, scale_ref, rhs_ref = refs[9:12]
    near_fields = refs[12 : 12 + SWEEPS]
    refs = refs[12 + SWEEPS :]
    packed_ref, basis_ref, side_ref, rhs_out_ref, store_out_ref, up_ref, down_ref = refs[:7]
    scale_far, x_far, y_far, z0_far, z1_far, sums_ref = refs[7:13]
    far_fields = refs[13:]
    tile_x, tile_y, layers = rhs_ref.shape
    rows = resist_ref.shape[1]
    planes = tile_x + 2 * MARGIN
    shape = (rows, layers)
    anchor_x = lax.axis_index("gx") * tile_x
    total_x = lax.axis_size("gx") * tile_x
    face_mask_y = y_face_mask(shape, tile_y)
    codes = table_ref.shape[0] // 2
    table = [table_ref[i : i + 1] for i in range(2 * codes)]

    def own(plane, depth=0):
        return MARGIN + depth <= plane < MARGIN + tile_x - depth

    def face_x(plane):
        inner = own(plane) and own(plane + 1)
        return x_ref[plane - MARGIN] if inner else x_far[plane]

    def near_or_far(near, far, depth=0):
        return lambda plane: near[plane - MARGIN] if own(plane, depth) else far[plane]

    face_y = near_or_far(y_ref, y_far)
    face_z0 = near_or_far(z0_ref, z0_far)
    face_z1 = near_or_far(z1_ref, z1_far)
    scale = near_or_far(scale_ref, scale_far, 1)
    resist_last, x_last, part_last = (None, None, None)
    for plane in range(planes):
        part = None
        if own(plane):
            resist = resist_ref[plane - MARGIN]
            part = part_ref[plane - MARGIN]
        else:
            strip = before_ref if plane < MARGIN else after_ref
            facies = strip[plane if plane < MARGIN else plane - MARGIN - tile_x]
            resist = code_select(table[:codes], facies)
            if 0 < plane < planes - 1:
                store = code_select(table[codes:], facies)
                y_far[plane], z0_far[plane], z1_far[plane], part = plane_faces(
                    resist, store, face_mask_y
                )
        if plane:
            if own(plane - 1) and own(plane):
                x_face = face_x(plane - 1)
            else:
                here = anchor_x + plane - 1 - MARGIN
                x_face = 2.0 / (resist_last + resist)
                x_face = jnp.where((here >= 0) & (here + 1 < total_x), x_face, 0.0)
                x_far[plane - 1] = x_face
            if plane > 1 and not own(plane - 1, 1):
                scale_far[plane - 1] = RELAX_WEIGHT / (part_last + x_face + x_last)
            x_last = x_face
        resist_last, part_last = (resist, part)

    start = start_field(shape)
    read = lambda plane: start
    for sweep_id in range(SWEEPS):
        depth = 1 + sweep_id
        first_end = min(MARGIN + depth, planes - depth)
        last_start = max(first_end, MARGIN + tile_x - depth)
        for low, high in ((depth, first_end), (last_start, planes - depth)):
            sweep_planes(
                low,
                high,
                read,
                far_fields[sweep_id].__setitem__,
                face_x,
                face_y,
                lambda plane: (face_z0(plane), face_z1(plane)),
                scale,
            )
        read = near_or_far(near_fields[sweep_id], far_fields[sweep_id], depth)

    tile = (tile_y, layers)
    cut_0 = face_ends(lane_iota(tile), 0)
    cut_any = cut_0 | face_ends(lane_iota(tile), 1)

    def inner(value):
        return value[:tile_y]

    sums = None
    for plane in range(tile_x):
        at = plane + MARGIN
        here_all = read(at)
        here = inner(here_all)
        step_y_all = up(here_all, 0) - here_all
        flux_y_all = y_ref[plane] * step_y_all
        flux_y = inner(flux_y_all)
        step_x = inner(read(at + 1)) - here
        flux_x = inner(face_x(at)) * step_x
        flux_before = inner(face_x(at - 1)) * (here - inner(read(at - 1)))
        z_face = jnp.maximum(inner(z0_ref[plane]), inner(z1_ref[plane]))
        above = up(here, 1)
        step_z = above - here
        energy_z = z_face * step_z * step_z
        other = 1.0 - here
        store = inner(storage_ref[plane])
        factor = inner(scale(at))
        rhs = rhs_ref[plane]
        below_end = jnp.where(cut_0, here, other)
        above_end = jnp.where(cut_0, above, 1.0 - above)
        z_cut = jnp.where(cut_any, z_face, 0.0)
        basis_ref[plane] = here
        side_ref[plane] = factor * (
            (flux_before - flux_x) + (inner(down(flux_y_all, 0)) - flux_y)
        )
        rhs_out_ref[plane] = factor * rhs
        store_out_ref[plane] = factor * store
        up_ref[plane] = factor * z_face
        down_ref[plane] = factor * down(z_face, 1)
        terms = (
            store * here * here,
            store * here * other,
            store * other * other,
            flux_x * step_x + flux_y * inner(step_y_all) + jnp.where(cut_any, 0.0, energy_z),
            jnp.where(cut_any, energy_z, 0.0),
            z_cut * below_end * below_end,
            z_cut * above_end * above_end,
            z_cut * below_end * above_end,
            here * rhs,
            other * rhs,
        )
        sums = terms if sums is None else [a + b for a, b in zip(sums, terms)]
    mass_00, mass_01, mass_11, energy, cut, low_2, high_2, low_high, rhs_0, rhs_1 = (
        jnp.sum(total, axis=0, keepdims=True) for total in sums
    )
    line = lane_iota((1, layers))
    count = layers // BLOCK_Z
    ends = (face_ends(line, 0), face_ends(line, 1))
    inside = (in_grid(line, 0, count), in_grid(line, 1, count))
    for parity, mass, right in ((0, mass_00, rhs_0), (1, mass_11, rhs_1)):
        own_end = jnp.where(ends[parity], low_2, cut)
        beyond_end = down(jnp.where(ends[parity], high_2, 0.0), 1)
        entry = mass + energy + own_end + beyond_end
        sums_ref[parity : parity + 1] = jnp.where(inside[parity], entry, 0.0)
        sums_ref[4 + parity : 5 + parity] = jnp.where(inside[parity], right, 0.0)
    sums_ref[2:3] = mass_01 - energy + (low_high - low_2) + down(low_high - high_2, 1)
    sums_ref[3:4] = -low_high
    sums_ref[6:8] = jnp.zeros((2, layers), jnp.float32)
    line = lax.broadcasted_iota(jnp.int32, (layers, layers), 0)
    lane = lane_iota((layers, layers))
    segment = lambda at: lax.rem(at + BLOCK_Z // 2, layers) // BLOCK_Z
    same = jnp.where(segment(line) == segment(lane), 1.0, 0.0)
    window = jnp.dot(sums_ref[...], same, precision=HIGHEST, preferred_element_type=jnp.float32)
    row = lax.broadcasted_iota(jnp.int32, window.shape, 0)
    keep = lax.rem(lane_iota(window.shape), BLOCK_Z) == row
    packed = jnp.sum(jnp.where(keep, window, 0.0), axis=0, keepdims=True)
    packed_ref[...] = jnp.broadcast_to(packed, packed_ref.shape)


def solve_band(diagonal, first, second, right):
    count = len(diagonal)
    matrix = {(k, k): diagonal[k] for k in range(count)}
    for distance, band in ((1, first), (2, second)):
        for k in range(count - distance):
            matrix[k, k + distance] = band[k]
            matrix[k + distance, k] = band[k]
    left = list(range(count))
    steps = []
    while left:
        pivot = left.pop(0 if len(steps) % 2 == 0 else -1)
        inverse = 1.0 / matrix[pivot, pivot]
        linked = [k for k in left if (pivot, k) in matrix]
        lower = {k: matrix[pivot, k] * inverse for k in linked}
        for k in linked:
            right[k] = right[k] - lower[k] * right[pivot]
            for other in linked:
                if other >= k:
                    change = lower[k] * matrix[pivot, other]
                    entry = matrix[k, other] - change if (k, other) in matrix else -change
                    matrix[k, other] = entry
                    matrix[other, k] = entry
        steps.append((pivot, inverse, lower))
    values = [None] * count
    for pivot, inverse, lower in reversed(steps):
        value = right[pivot] * inverse
        for k, factor in lower.items():
            value = value - factor * values[k]
        values[pivot] = value
    return values


def pressure_kernel(
    rows_ref, basis_ref, side_ref, rhs_ref, store_ref, up_ref, down_ref, out_ref, entries
):
    tile_x, tile_y, layers = basis_ref.shape
    count = layers // BLOCK_Z
    half = BLOCK_Z // 2
    shape = (count, layers)
    node = lax.broadcasted_iota(jnp.int32, shape, 0)
    layer = lane_iota(shape)
    packed = jnp.sum(rows_ref[...], axis=0, keepdims=True)

    def held(segment, kind):
        return layer == lax.rem(segment * BLOCK_Z + kind, layers)

    parity = lax.rem(node, 2)
    own = held(node, parity) | held(node + 1, parity)
    right = held(node, parity + 4) | held(node + 1, parity + 4)
    masks = (own, held(node + 1, 2), held(node + 1, 3), right)
    for part_id, mask in enumerate(masks):
        part = jnp.where(mask, packed, 0.0)
        entries[part_id] = jnp.broadcast_to(jnp.sum(part, axis=1, keepdims=True), shape)
    values = solve_band(
        *([entries[part_id, k : k + 1] for k in range(count)] for part_id in range(4))
    )
    line = lane_iota((1, layers))
    fields = [jnp.zeros((1, layers), jnp.float32)] * 2
    for k in range(count):
        support = (line >= k * BLOCK_Z - half) & (line < k * BLOCK_Z + 3 * half)
        fields[k % 2] = jnp.where(support, values[k], fields[k % 2])
    value_0 = jnp.broadcast_to(fields[0], (tile_y, layers))
    value_1 = jnp.broadcast_to(fields[1], (tile_y, layers))
    apart = value_0 - value_1
    for plane in range(tile_x):
        here = basis_ref[plane]
        prolonged = here * value_0 + (1.0 - here) * value_1
        applied = (
            store_ref[plane] * prolonged
            + apart * side_ref[plane]
            + up_ref[plane] * (prolonged - up(prolonged, 1))
            + down_ref[plane] * (prolonged - down(prolonged, 1))
        )
        out_ref[plane] = prolonged + (rhs_ref[plane] - applied)


def column_step(facies, source, facies_perm, facies_store, well_x, well_y, well_rate):
    tile_x, tile_y, layers = facies.shape
    rows = tile_y + 2 * MARGIN
    planes = tile_x + 2 * MARGIN
    size = lax.axis_size(AXES)
    f32 = jnp.float32
    tile = jax.ShapeDtypeStruct(facies.shape, f32)
    wide = jax.ShapeDtypeStruct((tile_x, rows, layers), f32)
    vmem = pl.BlockSpec(memory_space=pltpu.VMEM)
    smem = pl.BlockSpec(memory_space=pltpu.SMEM)
    params = pltpu.CompilerParams(vmem_limit_bytes=VMEM_BYTES)

    own, before, after = wide_tile(facies)
    near = pl.pallas_call(
        tile_kernel,
        out_shape=(jax.ShapeDtypeStruct((2 * facies_perm.shape[0], layers), f32),)
        + (wide,) * 8
        + (tile,)
        + (wide,) * SWEEPS,
        in_specs=[vmem, vmem, smem, smem, vmem, vmem, vmem],
        out_specs=(vmem,) * (10 + SWEEPS),
        compiler_params=params,
        cost_estimate=pl.CostEstimate(flops=3000000, bytes_accessed=1000000, transcendentals=0),
        name="tile",
    )(
        own,
        source,
        facies_perm,
        facies_store,
        well_x[None, :],
        well_y[None, :],
        well_rate[None, :],
    )
    copies, *fields = pl.pallas_call(
        basis_kernel,
        out_shape=(jax.ShapeDtypeStruct((size, layers), f32),) + (tile,) * 6,
        in_specs=[vmem] * (12 + SWEEPS),
        out_specs=(vmem,) * 7,
        scratch_shapes=[pltpu.VMEM((planes, rows, layers), f32)] * 5
        + [pltpu.VMEM((8, layers), f32)]
        + [pltpu.VMEM((planes, rows, layers), f32)] * SWEEPS,
        compiler_params=params,
        name="basis",
    )(before, after, *near)
    everyone = lax.all_to_all(copies, AXES, 0, 0, tiled=True)
    return pl.pallas_call(
        pressure_kernel,
        out_shape=tile,
        in_specs=[vmem] * 7,
        out_specs=vmem,
        scratch_shapes=[pltpu.VMEM((4, layers // BLOCK_Z, layers), f32)],
        compiler_params=params,
        name="pressure",
    )(everyone, *fields)


def solution(mesh):
    def per_device(facies, *others):
        tile_x, tile_y, layers = facies.shape
        total_x = tile_x * mesh.shape["gx"]
        total_y = tile_y * mesh.shape["gy"]
        one_column = total_x == BLOCK_X and total_y == BLOCK_Y
        fits = layers % 128 == 0 and tile_y % 8 == 0 and min(tile_x, tile_y) >= MARGIN
        step = column_step if one_column and fits else general_step
        return step(facies, *others)

    in_specs = (P("gx", "gy", None), P("gx", "gy", None), P(), P(), P(), P(), P())
    out_specs = P("gx", "gy", None)
    return jax.shard_map(
        per_device, mesh=mesh, in_specs=in_specs, out_specs=out_specs, check_vma=False
    )
```

```python
import jax
import jax.numpy as jnp
import numpy as np
from jax import lax
from jax.experimental import pallas as pl
from jax.experimental.pallas import tpu as pltpu
from jax.sharding import PartitionSpec as P

BLOCK_X = 64
BLOCK_Y = 64
BLOCK_Z = 16
SWEEPS = 3


RELAX_WEIGHT = 2.0 / 3.0
HIGHEST = lax.Precision.HIGHEST
first_bits = np.array([0, 0, 0, 0, 1, 1, 1, 1], dtype=np.int32)
second_bits = np.array([0, 0, 1, 1, 0, 0, 1, 1], dtype=np.int32)
third_bits = np.array([0, 1, 0, 1, 0, 1, 0, 1], dtype=np.int32)
shift_along_x = np.array([0, 2, -2, 0, 0, 0, 0], dtype=np.int32)
shift_along_y = np.array([0, 0, 0, 2, -2, 0, 0], dtype=np.int32)
shift_along_z = np.array([0, 0, 0, 0, 0, 2, -2], dtype=np.int32)


def with_halo(value, sides, width):
    for axis, dim in sides:
        size, length = (lax.axis_size(axis), value.shape[dim])
        up = [(i, (i + 1) % size) for i in range(size - 1)]
        down = [(j, i) for i, j in up]
        last = lax.slice_in_dim(value, length - width, length, axis=dim)
        initial = lax.slice_in_dim(value, 0, width, axis=dim)
        before = lax.ppermute(last, axis, up)
        after = lax.ppermute(initial, axis, down)
        value = jnp.concatenate([before, value, after], axis=dim)
    return value


def support_of(coords, block_size, parity):
    return parity + 2 * jnp.floor_divide(
        coords + block_size // 2 - block_size * parity, 2 * block_size
    )


def parity_nodes(coords, block_size):
    return jnp.stack([support_of(coords, block_size, 0), support_of(coords, block_size, 1)])


def parity_start(coords, block_size):
    node_ids = parity_nodes(coords, block_size)
    return (node_ids == jnp.floor_divide(coords, block_size)[None]).astype(jnp.float32)


def parity_same(coords, block_size):
    node_here = parity_nodes(coords[:-1], block_size)
    node_next = parity_nodes(coords[1:], block_size)
    return (node_here == node_next).astype(jnp.float32)


def harmonic(left_perm, right_perm):
    return 2.0 * left_perm * right_perm / (left_perm + right_perm)


def face_pad(values_in, dim_id, before):
    widths = [(0, 0), (0, 0), (0, 0)]
    widths[dim_id] = (1, 0) if before else (0, 1)
    return jnp.pad(values_in, widths)


def expand(line_in, dim_id):
    new_shape = [1, 1, 1]
    new_shape[dim_id] = line_in.shape[0]
    return line_in.reshape(new_shape)


def split_faces(values_in, dim_id):
    length = values_in.shape[dim_id]
    below_part = lax.slice_in_dim(values_in, 0, length - 1, axis=dim_id)
    above_part = lax.slice_in_dim(values_in, 1, length, axis=dim_id)
    return (below_part, above_part)


def cut_apply(values_in, storage, trans_all, same_all):
    result = storage * values_in
    for dim_id in range(3):
        trans_face = trans_all[dim_id]
        same_line = expand(same_all[dim_id], dim_id)
        below_part, above_part = split_faces(values_in, dim_id)
        result = result + face_pad(
            trans_face * (below_part - same_line * above_part), dim_id, False
        )
        result = result + face_pad(trans_face * (above_part - same_line * below_part), dim_id, True)
    return result


def rim_terms(values_in, trans_all, same_all):
    result = []
    for dim_id in range(3):
        trans_face = trans_all[dim_id]
        cross_mask = 1.0 - expand(same_all[dim_id], dim_id)
        below_part, above_part = split_faces(values_in, dim_id)
        result.append(face_pad(-trans_face * cross_mask * above_part, dim_id, False))
        result.append(face_pad(-trans_face * cross_mask * below_part, dim_id, True))
    return result


def diagonal_of(storage, trans_all):
    result = storage
    for dim_id in range(3):
        result = (
            result
            + face_pad(trans_all[dim_id], dim_id, False)
            + face_pad(trans_all[dim_id], dim_id, True)
        )
    return result


def lookup(facies, code_table):
    result = jnp.zeros(facies.shape, jnp.float32)
    for code_id in range(code_table.shape[0]):
        result = result + jnp.where(facies == code_id, code_table[code_id], 0.0)
    return result


def flatten_node(index_x, index_y, index_z, counts):
    count_x, count_y, count_z = counts
    flat_ids = (
        jnp.clip(index_x, 0, count_x - 1) * count_y + jnp.clip(index_y, 0, count_y - 1)
    ) * count_z
    return (flat_ids + jnp.clip(index_z, 0, count_z - 1)).astype(jnp.int32)


def tile_indices(anchor_x, anchor_y, counts):
    count_x, count_y, count_z = counts
    row_x = parity_nodes(jnp.reshape(anchor_x, (1,)), BLOCK_X)[first_bits][:, 0]
    row_y = parity_nodes(jnp.reshape(anchor_y, (1,)), BLOCK_Y)[second_bits][:, 0]
    seg_first = jnp.maximum(jnp.arange(count_z + 1, dtype=jnp.int32) * BLOCK_Z - BLOCK_Z // 2, 0)
    row_z = parity_nodes(seg_first, BLOCK_Z)[third_bits]
    row_ids = flatten_node(row_x[:, None], row_y[:, None], row_z, counts)
    col_ids = flatten_node(
        row_x[:, None, None] + jnp.asarray(shift_along_x)[None, :, None],
        row_y[:, None, None] + jnp.asarray(shift_along_y)[None, :, None],
        row_z[:, None, :] + jnp.asarray(shift_along_z)[None, :, None],
        counts,
    )
    entry_ids = row_ids[None, :, None, :] * (count_x * count_y * count_z) + col_ids[:, None, :, :]
    return (entry_ids, row_ids)


def segment_matrix(layers, segment_count):
    seg_of = (jnp.arange(layers, dtype=jnp.int32) + BLOCK_Z // 2) // BLOCK_Z
    return (seg_of[:, None] == jnp.arange(segment_count, dtype=jnp.int32)[None, :]).astype(
        jnp.float32
    )


def solve_coarse(coarse, coarse_rhs):
    factor = jnp.linalg.cholesky(coarse)
    middle = lax.linalg.triangular_solve(factor, coarse_rhs[:, None], left_side=True, lower=True)
    return lax.linalg.triangular_solve(
        factor, middle, left_side=True, lower=True, transpose_a=True
    )[:, 0]


def geometry(coeffs, margin, anchor_x, anchor_y, total_x, total_y):
    coord_x = anchor_x - margin + jnp.arange(coeffs.shape[1], dtype=jnp.int32)
    coord_y = anchor_y - margin + jnp.arange(coeffs.shape[2], dtype=jnp.int32)
    coord_z = jnp.arange(coeffs.shape[3], dtype=jnp.int32)
    inside_x = (coord_x >= 0) & (coord_x < total_x)
    inside_y = (coord_y >= 0) & (coord_y < total_y)
    inside = inside_x[:, None, None] & inside_y[None, :, None]
    perm_safe = jnp.where(inside, coeffs[0], 1.0)
    storage = jnp.where(inside, coeffs[1], 1.0)
    valid_x = (inside_x[:-1] & inside_x[1:]).astype(jnp.float32)
    valid_y = (inside_y[:-1] & inside_y[1:]).astype(jnp.float32)
    trans_x = harmonic(perm_safe[:-1], perm_safe[1:]) * valid_x[:, None, None]
    trans_y = harmonic(perm_safe[:, :-1], perm_safe[:, 1:]) * valid_y[None, :, None]
    trans_z = harmonic(perm_safe[:, :, :-1], perm_safe[:, :, 1:])
    trans_all = (trans_x, trans_y, trans_z)
    same_all = (
        parity_same(coord_x, BLOCK_X)[first_bits],
        parity_same(coord_y, BLOCK_Y)[second_bits],
        parity_same(coord_z, BLOCK_Z)[third_bits],
    )
    starts = (
        parity_start(coord_x, BLOCK_X)[first_bits],
        parity_start(coord_y, BLOCK_Y)[second_bits],
        parity_start(coord_z, BLOCK_Z)[third_bits],
    )
    return (storage, trans_all, diagonal_of(storage, trans_all), same_all, starts)


def initial(geo_set):
    start_x, start_y, start_z = geo_set[4]
    return start_x[:, :, None, None] * start_y[:, None, :, None] * start_z[:, None, None, :]


def smooth(basis_ext, geo_set):
    storage, trans_all, diagonal, same_all, _ = geo_set

    def change_of(values_in, same_x, same_y, same_z):
        return (
            -RELAX_WEIGHT
            * cut_apply(values_in, storage, trans_all, (same_x, same_y, same_z))
            / diagonal
        )

    changes = jax.vmap(change_of)(basis_ext, same_all[0], same_all[1], same_all[2])[:, 1:-1, 1:-1]
    interior = basis_ext[:, 1:-1, 1:-1]
    change_sum = jnp.sum(changes, axis=0)
    return interior + changes - interior * change_sum[None]


def basis_halo(basis_now):
    return with_halo(basis_now, (("gx", 1), ("gy", 2)), 1)


def general_step(facies, source, facies_perm, facies_store, well_x, well_y, well_rate):
    tile_x, tile_y, layers = facies.shape
    devs_x = lax.axis_size("gx")
    devs_y = lax.axis_size("gy")
    total_x = tile_x * devs_x
    total_y = tile_y * devs_y
    anchor_x = lax.axis_index("gx") * tile_x
    anchor_y = lax.axis_index("gy") * tile_y
    coeffs = jnp.stack([lookup(facies, facies_perm), lookup(facies, facies_store)])
    coeff_wide = with_halo(coeffs, (("gx", 1), ("gy", 2)), 1)
    geo_one = geometry(coeff_wide, 1, anchor_x, anchor_y, total_x, total_y)
    basis_now = initial(geo_one)[:, 1:-1, 1:-1]
    for _ in range(SWEEPS):
        basis_now = smooth(basis_halo(basis_now), geo_one)
    basis_now = basis_halo(basis_now)
    storage, trans_all, diagonal, same_all, _ = geo_one

    def terms_of(values_in, same_x, same_y, same_z):
        same_three = (same_x, same_y, same_z)
        return jnp.stack(
            [cut_apply(values_in, storage, trans_all, same_three)]
            + rim_terms(values_in, trans_all, same_three)
        )

    term_stack = jax.vmap(terms_of)(basis_now, same_all[0], same_all[1], same_all[2])[
        :, :, 1:-1, 1:-1
    ]
    interior = basis_now[:, 1:-1, 1:-1]
    count_x = total_x // BLOCK_X
    count_y = total_y // BLOCK_Y
    count_z = layers // BLOCK_Z
    counts = (count_x, count_y, count_z)
    coarse_count = count_x * count_y * count_z
    zmatrix = segment_matrix(layers, count_z + 1)
    gram_local = jnp.einsum("apqz,cspqz->casz", interior, term_stack, precision=HIGHEST)
    gram_local = jnp.einsum("casz,zg->casg", gram_local, zmatrix, precision=HIGHEST)
    cell_x = anchor_x + jnp.arange(tile_x, dtype=jnp.int32)
    cell_y = anchor_y + jnp.arange(tile_y, dtype=jnp.int32)
    hit_x = (well_x[:, None] == cell_x[None, :]).astype(jnp.float32)
    hit_y = (well_y[:, None] == cell_y[None, :]).astype(jnp.float32)
    column = jnp.einsum("w,wx,wy->xy", well_rate, hit_x, hit_y, precision=HIGHEST)
    rhs_fine = source + column[:, :, None] / layers
    rhs_local = jnp.einsum("apqz,pqz->az", interior, rhs_fine, precision=HIGHEST)
    rhs_local = jnp.einsum("az,zg->ag", rhs_local, zmatrix, precision=HIGHEST)
    entry_ids, row_ids = tile_indices(anchor_x, anchor_y, counts)
    local_matrix = (
        jnp.zeros((coarse_count * coarse_count,), jnp.float32)
        .at[entry_ids.reshape(-1)]
        .add(gram_local.reshape(-1))
    )
    local_matrix = local_matrix.reshape(coarse_count, coarse_count)
    local_rhs = (
        jnp.zeros((coarse_count,), jnp.float32).at[row_ids.reshape(-1)].add(rhs_local.reshape(-1))
    )
    coarse, coarse_rhs = lax.psum((local_matrix, local_rhs), ("gx", "gy"))
    coarse_solution = solve_coarse(coarse, coarse_rhs)
    values_at = coarse_solution[row_ids]
    per_layer = jnp.einsum("ag,zg->az", values_at, zmatrix, precision=HIGHEST)
    prolonged = jnp.einsum("apqz,az->pqz", interior, per_layer, precision=HIGHEST)
    prolonged_ext = with_halo(prolonged, (("gx", 0), ("gy", 1)), 1)
    ones_all = (
        jnp.ones((tile_x + 1,), jnp.float32),
        jnp.ones((tile_y + 1,), jnp.float32),
        jnp.ones((layers - 1,), jnp.float32),
    )
    applied = cut_apply(prolonged_ext, storage, trans_all, ones_all)[1:-1, 1:-1]
    return prolonged + RELAX_WEIGHT * (rhs_fine - applied) / diagonal[1:-1, 1:-1]


MARGIN = SWEEPS + 1
FACES = 6
AXES = ("gx", "gy")
VMEM_BYTES = 16 * 2**20


def swap_along(value, axis, first):
    sizes = {name_: lax.axis_size(name_) for name_ in AXES}
    other = AXES[1 - AXES.index(axis)]
    pairs = []
    for gx in range(sizes[AXES[0]]):
        for gy in range(sizes[AXES[1]]):
            place = {AXES[0]: gx, AXES[1]: gy}
            partner = dict(place)
            along = first + ((place[axis] - first) ^ 1) if place[axis] >= first else -1
            if 0 <= along < sizes[axis]:
                partner[axis] = along
            else:
                partner[other] = place[other] ^ 1
            if partner[other] < sizes[other]:
                pairs.append(tuple(p[AXES[0]] * sizes[AXES[1]] + p[AXES[1]] for p in (place, partner)))
    return lax.ppermute(value, AXES, pairs)


def wide_tile(facies):
    count = facies.shape[0]
    even_x, even_y = (lax.axis_index(axis) % 2 == 0 for axis in AXES)

    def end_planes(value, at_first):
        return jnp.where(at_first, value[:MARGIN], value[count - MARGIN :])

    far = swap_along(facies, "gy", 1)
    near = swap_along(facies, "gy", 0)
    beside = swap_along(end_planes(facies, ~even_x), "gx", 0)
    before = jnp.where(even_y, far[:, -MARGIN:], near[:, -MARGIN:])
    after = jnp.where(even_y, near[:, :MARGIN], far[:, :MARGIN])
    rest = jnp.concatenate([after, before], axis=1)
    own = jnp.concatenate([facies, rest], axis=1)
    far = swap_along(end_planes(own, even_x), "gx", 1)
    corners = swap_along(end_planes(rest, ~even_x), "gx", 0)
    near = jnp.concatenate([beside, corners], axis=1)
    return own, jnp.where(even_x, far, near), jnp.where(even_x, near, far)


def lane_iota(shape):
    return lax.broadcasted_iota(jnp.int32, shape, len(shape) - 1)


def face_ends(layer, parity):
    return lax.rem(layer + 1 + BLOCK_Z // 2 + BLOCK_Z * parity, 2 * BLOCK_Z) == 0


def in_grid(layer, parity, count):
    shifted = layer + BLOCK_Z // 2 + BLOCK_Z * parity
    node = 2 * (shifted // (2 * BLOCK_Z)) - parity
    return (node >= 0) & (node < count)


def up(value, axis):
    return pltpu.roll(value, value.shape[axis] - 1, axis)


def down(value, axis):
    return pltpu.roll(value, 1, axis)


def code_select(table, codes):
    result = jnp.broadcast_to(table[0], codes.shape)
    for code_id in range(1, len(table)):
        result = jnp.where(codes == code_id, table[code_id], result)
    return result


def plane_faces(resist, store, face_y):
    layer = lane_iota(resist.shape)
    y_face = jnp.where(face_y, 2.0 / (resist + up(resist, 0)), 0.0)
    z_face = jnp.where(layer == resist.shape[1] - 1, 0.0, 2.0 / (resist + up(resist, 1)))
    z_faces = [jnp.where(face_ends(layer, parity), 0.0, z_face) for parity in (0, 1)]
    faces = (y_face, *z_faces)
    before = (down(y_face, 0), *(down(value, 1) for value in z_faces))
    part = store + y_face + before[0] + z_face + jnp.maximum(before[1], before[2])
    return faces + before, part


def y_face_mask(shape, tile_y):
    row = lax.broadcasted_iota(jnp.int32, shape, 0)
    place = lax.axis_index("gy") * tile_y + jnp.where(row < tile_y + MARGIN, row, row - shape[0])
    inside = (place >= 0) & (place + 1 < lax.axis_size("gy") * tile_y)
    return inside & (row != tile_y + MARGIN - 1)


def sweep_planes(low, high, read, write, face_x, faces_of, scale):
    if low >= high:
        return
    here = read(low)
    flux_before = face_x(low - 1) * (here - read(low - 1))
    for plane in range(low, high):
        beyond = read(plane + 1)
        flux = face_x(plane) * (beyond - here)
        y_after, z0_after, z1_after, y_before, z0_before, z1_before = faces_of(plane)
        above, below = (up(here, 1), down(here, 1))
        other = 1.0 - here
        total = flux - flux_before
        total = total + (y_after * (up(here, 0) - here) + y_before * (down(here, 0) - here))
        total = total + (z0_after * (above * other) - z1_after * (here * (1.0 - above)))
        total = total + (z0_before * (below * other) - z1_before * (here * (1.0 - below)))
        write(plane, here + scale(plane) * total)
        here, flux_before = (beyond, flux)


def start_field(shape):
    return jnp.where(lax.rem(lane_iota(shape) // BLOCK_Z, 2) == 0, 1.0, 0.0)


def tile_kernel(
    rows_ref, source_ref, perm_ref, store_ref, well_x_ref, well_y_ref, well_rate_ref,
    table_ref, rhs_ref, resist_ref, storage_ref, x_ref, part_ref, scale_ref, *more_refs,
):
    tile_x, rows, layers = rows_ref.shape
    tile_y = source_ref.shape[1]
    anchor_x = lax.axis_index("gx") * tile_x
    anchor_y = lax.axis_index("gy") * tile_y
    codes = perm_ref.shape[0]
    resists = [
        1.0 / jnp.full((1, layers), perm_ref[code], jnp.float32) for code in range(codes)
    ]
    stores = [jnp.full((1, layers), store_ref[code], jnp.float32) for code in range(codes)]
    for code in range(codes):
        table_ref[code : code + 1] = resists[code]
        table_ref[codes + code : codes + code + 1] = stores[code]
    face_refs, field_refs = (more_refs[:FACES], more_refs[FACES:])
    face_y = y_face_mask((rows, layers), tile_y)
    hit_y = (
        lax.broadcasted_iota(jnp.int32, (tile_y, well_y_ref.shape[1]), 0) + anchor_y
        == well_y_ref[...]
    )
    before, x_before, part_before = (None, None, None)
    for plane in range(tile_x):
        resist = code_select(resists, rows_ref[plane])
        store = code_select(stores, rows_ref[plane])
        faces, part = plane_faces(resist, store, face_y)
        resist_ref[plane] = resist
        storage_ref[plane] = store
        for ref, face in zip(face_refs, faces):
            ref[plane] = face
        part_ref[plane] = part
        if plane:
            x_face = 2.0 / (before + resist)
            x_ref[plane - 1] = x_face
            if plane > 1:
                scale_ref[plane - 1] = RELAX_WEIGHT / (part_before + x_face + x_before)
            x_before = x_face
        before, part_before = (resist, part)
        hit = hit_y & (well_x_ref[...] == anchor_x + plane)
        column = jnp.sum(jnp.where(hit, well_rate_ref[...], 0.0), axis=1, keepdims=True)
        rhs_ref[plane] = source_ref[plane] + column / layers
    start = start_field((rows, layers))
    read = lambda plane: start
    for sweep_id, field in enumerate(field_refs):
        sweep_planes(
            1 + sweep_id,
            tile_x - 1 - sweep_id,
            read,
            field.__setitem__,
            x_ref.__getitem__,
            lambda plane: [ref[plane] for ref in face_refs],
            scale_ref.__getitem__,
        )
        read = field.__getitem__


def basis_kernel(*refs):
    before_ref, after_ref, table_ref, rhs_ref, resist_ref, storage_ref, x_ref, part_ref, scale_ref = refs[:9]
    refs = refs[9:]
    near_faces, near_fields, refs = (refs[:FACES], refs[FACES : FACES + SWEEPS], refs[FACES + SWEEPS :])
    packed_ref, basis_ref, side_ref, rhs_out_ref, store_out_ref, up_ref, down_ref, sums_ref = refs[:8]
    scale_far, x_far = refs[8:10]
    far_faces, far_fields = (refs[10 : 10 + FACES], refs[10 + FACES :])
    tile_x, tile_y, layers = rhs_ref.shape
    rows = resist_ref.shape[1]
    planes = tile_x + 2 * MARGIN
    shape = (rows, layers)
    anchor_x = lax.axis_index("gx") * tile_x
    total_x = lax.axis_size("gx") * tile_x
    face_mask_y = y_face_mask(shape, tile_y)
    codes = table_ref.shape[0] // 2
    table = [table_ref[i : i + 1] for i in range(2 * codes)]

    def own(plane, depth=0):
        return MARGIN + depth <= plane < MARGIN + tile_x - depth

    def face_x(plane):
        inner = own(plane) and own(plane + 1)
        return x_ref[plane - MARGIN] if inner else x_far[plane]

    def near_or_far(near, far, depth=0):
        return lambda plane: near[plane - MARGIN] if own(plane, depth) else far[plane]

    def faces_of(plane):
        return [near_or_far(near, far)(plane) for near, far in zip(near_faces, far_faces)]

    scale = near_or_far(scale_ref, scale_far, 1)
    resist_last, x_last, part_last = (None, None, None)
    for plane in range(planes):
        part = None
        if own(plane):
            resist = resist_ref[plane - MARGIN]
            part = part_ref[plane - MARGIN]
        else:
            strip = before_ref if plane < MARGIN else after_ref
            facies = strip[plane if plane < MARGIN else plane - MARGIN - tile_x]
            resist = code_select(table[:codes], facies)
            if 0 < plane < planes - 1:
                store = code_select(table[codes:], facies)
                faces, part = plane_faces(resist, store, face_mask_y)
                for ref, face in zip(far_faces, faces):
                    ref[plane] = face
        if plane:
            if own(plane - 1) and own(plane):
                x_face = face_x(plane - 1)
            else:
                here = anchor_x + plane - 1 - MARGIN
                x_face = 2.0 / (resist_last + resist)
                x_face = jnp.where((here >= 0) & (here + 1 < total_x), x_face, 0.0)
                x_far[plane - 1] = x_face
            if plane > 1 and not own(plane - 1, 1):
                scale_far[plane - 1] = RELAX_WEIGHT / (part_last + x_face + x_last)
            x_last = x_face
        resist_last, part_last = (resist, part)

    start = start_field(shape)
    read = lambda plane: start
    for sweep_id in range(SWEEPS):
        depth = 1 + sweep_id
        first_end = min(MARGIN + depth, planes - depth)
        last_start = max(first_end, MARGIN + tile_x - depth)
        for low, high in ((depth, first_end), (last_start, planes - depth)):
            sweep_planes(
                low,
                high,
                read,
                far_fields[sweep_id].__setitem__,
                face_x,
                faces_of,
                scale,
            )
        read = near_or_far(near_fields[sweep_id], far_fields[sweep_id], depth)

    tile = (tile_y, layers)
    cut_0 = face_ends(lane_iota(tile), 0)
    cut_any = cut_0 | face_ends(lane_iota(tile), 1)

    def inner(value):
        return value[:tile_y]

    sums = None
    for plane in range(tile_x):
        at = plane + MARGIN
        here_all = read(at)
        here = inner(here_all)
        step_y_all = up(here_all, 0) - here_all
        y_after, z0_after, z1_after, y_before, z0_before, z1_before = faces_of(at)
        flux_y = inner(y_after * step_y_all)
        flux_y_before = inner(y_before * (here_all - down(here_all, 0)))
        step_x = inner(read(at + 1)) - here
        flux_x = inner(face_x(at)) * step_x
        flux_before = inner(face_x(at - 1)) * (here - inner(read(at - 1)))
        z_face = inner(jnp.maximum(z0_after, z1_after))
        above = up(here, 1)
        step_z = above - here
        energy_z = z_face * step_z * step_z
        other = 1.0 - here
        store = inner(storage_ref[plane])
        factor = inner(scale(at))
        rhs = rhs_ref[plane]
        below_end = jnp.where(cut_0, here, other)
        above_end = jnp.where(cut_0, above, 1.0 - above)
        z_cut = jnp.where(cut_any, z_face, 0.0)
        basis_ref[plane] = here
        side_ref[plane] = factor * (
            (flux_before - flux_x) + (flux_y_before - flux_y)
        )
        rhs_out_ref[plane] = factor * rhs
        store_out_ref[plane] = factor * store
        up_ref[plane] = factor * z_face
        down_ref[plane] = factor * inner(jnp.maximum(z0_before, z1_before))
        terms = (
            store * here * here,
            store * here * other,
            store * other * other,
            flux_x * step_x + flux_y * inner(step_y_all) + jnp.where(cut_any, 0.0, energy_z),
            jnp.where(cut_any, energy_z, 0.0),
            z_cut * below_end * below_end,
            z_cut * above_end * above_end,
            z_cut * below_end * above_end,
            here * rhs,
            other * rhs,
        )
        sums = terms if sums is None else [a + b for a, b in zip(sums, terms)]
    mass_00, mass_01, mass_11, energy, cut, low_2, high_2, low_high, rhs_0, rhs_1 = (
        jnp.sum(total, axis=0, keepdims=True) for total in sums
    )
    line = lane_iota((1, layers))
    count = layers // BLOCK_Z
    ends = (face_ends(line, 0), face_ends(line, 1))
    inside = (in_grid(line, 0, count), in_grid(line, 1, count))
    for parity, mass, right in ((0, mass_00, rhs_0), (1, mass_11, rhs_1)):
        own_end = jnp.where(ends[parity], low_2, cut)
        beyond_end = down(jnp.where(ends[parity], high_2, 0.0), 1)
        entry = mass + energy + own_end + beyond_end
        sums_ref[parity : parity + 1] = jnp.where(inside[parity], entry, 0.0)
        sums_ref[4 + parity : 5 + parity] = jnp.where(inside[parity], right, 0.0)
    sums_ref[2:3] = mass_01 - energy + (low_high - low_2) + down(low_high - high_2, 1)
    sums_ref[3:4] = -low_high
    sums_ref[6:8] = jnp.zeros((2, layers), jnp.float32)
    line = lax.broadcasted_iota(jnp.int32, (layers, layers), 0)
    lane = lane_iota((layers, layers))
    segment = lambda at: lax.rem(at + BLOCK_Z // 2, layers) // BLOCK_Z
    same = jnp.where(segment(line) == segment(lane), 1.0, 0.0)
    window = jnp.dot(sums_ref[...], same, precision=HIGHEST, preferred_element_type=jnp.float32)
    row = lax.broadcasted_iota(jnp.int32, window.shape, 0)
    keep = lax.rem(lane_iota(window.shape), BLOCK_Z) == row
    packed = jnp.sum(jnp.where(keep, window, 0.0), axis=0, keepdims=True)
    packed_ref[...] = jnp.broadcast_to(packed, packed_ref.shape)


def solve_band(diagonal, first, second, right):
    count = len(diagonal)
    matrix = {(k, k): diagonal[k] for k in range(count)}
    for distance, band in ((1, first), (2, second)):
        for k in range(count - distance):
            matrix[k, k + distance] = band[k]
            matrix[k + distance, k] = band[k]
    left = list(range(count))
    steps = []
    while left:
        pivot = left.pop(0 if len(steps) % 2 == 0 else -1)
        inverse = 1.0 / matrix[pivot, pivot]
        linked = [k for k in left if (pivot, k) in matrix]
        lower = {k: matrix[pivot, k] * inverse for k in linked}
        for k in linked:
            right[k] = right[k] - lower[k] * right[pivot]
            for other in linked:
                if other >= k:
                    change = lower[k] * matrix[pivot, other]
                    entry = matrix[k, other] - change if (k, other) in matrix else -change
                    matrix[k, other] = entry
                    matrix[other, k] = entry
        steps.append((pivot, inverse, lower))
    values = [None] * count
    for pivot, inverse, lower in reversed(steps):
        value = right[pivot] * inverse
        for k, factor in lower.items():
            value = value - factor * values[k]
        values[pivot] = value
    return values


def pressure_kernel(
    rows_ref, basis_ref, side_ref, rhs_ref, store_ref, up_ref, down_ref, out_ref, entries
):
    tile_x, tile_y, layers = basis_ref.shape
    count = layers // BLOCK_Z
    half = BLOCK_Z // 2
    shape = (count, layers)
    node = lax.broadcasted_iota(jnp.int32, shape, 0)
    layer = lane_iota(shape)
    packed = jnp.sum(rows_ref[...], axis=0, keepdims=True)

    def held(segment, kind):
        return layer == lax.rem(segment * BLOCK_Z + kind, layers)

    parity = lax.rem(node, 2)
    own = held(node, parity) | held(node + 1, parity)
    right = held(node, parity + 4) | held(node + 1, parity + 4)
    masks = (own, held(node + 1, 2), held(node + 1, 3), right)
    for part_id, mask in enumerate(masks):
        part = jnp.where(mask, packed, 0.0)
        entries[part_id] = jnp.broadcast_to(jnp.sum(part, axis=1, keepdims=True), shape)
    values = solve_band(
        *([entries[part_id, k : k + 1] for k in range(count)] for part_id in range(4))
    )
    line = lane_iota((1, layers))
    fields = [jnp.zeros((1, layers), jnp.float32)] * 2
    for k in range(count):
        support = (line >= k * BLOCK_Z - half) & (line < k * BLOCK_Z + 3 * half)
        fields[k % 2] = jnp.where(support, values[k], fields[k % 2])
    value_0 = jnp.broadcast_to(fields[0], (tile_y, layers))
    value_1 = jnp.broadcast_to(fields[1], (tile_y, layers))
    apart = value_0 - value_1
    for plane in range(tile_x):
        here = basis_ref[plane]
        prolonged = here * value_0 + (1.0 - here) * value_1
        applied = (
            store_ref[plane] * prolonged
            + apart * side_ref[plane]
            + up_ref[plane] * (prolonged - up(prolonged, 1))
            + down_ref[plane] * (prolonged - down(prolonged, 1))
        )
        out_ref[plane] = prolonged + (rhs_ref[plane] - applied)


def column_step(facies, source, facies_perm, facies_store, well_x, well_y, well_rate):
    tile_x, tile_y, layers = facies.shape
    rows = tile_y + 2 * MARGIN
    planes = tile_x + 2 * MARGIN
    size = lax.axis_size(AXES)
    f32 = jnp.float32
    tile = jax.ShapeDtypeStruct(facies.shape, f32)
    wide = jax.ShapeDtypeStruct((tile_x, rows, layers), f32)
    vmem = pl.BlockSpec(memory_space=pltpu.VMEM)
    smem = pl.BlockSpec(memory_space=pltpu.SMEM)
    params = pltpu.CompilerParams(vmem_limit_bytes=VMEM_BYTES)

    own, before, after = wide_tile(facies)
    near = pl.pallas_call(
        tile_kernel,
        out_shape=(jax.ShapeDtypeStruct((2 * facies_perm.shape[0], layers), f32),)
        + (tile,)
        + (wide,) * (5 + FACES + SWEEPS),
        in_specs=[vmem, vmem, smem, smem, vmem, vmem, vmem],
        out_specs=(vmem,) * (7 + FACES + SWEEPS),
        compiler_params=params,
        cost_estimate=pl.CostEstimate(flops=3000000, bytes_accessed=1000000, transcendentals=0),
        name="tile",
    )(
        own,
        source,
        facies_perm,
        facies_store,
        well_x[None, :],
        well_y[None, :],
        well_rate[None, :],
    )
    copies, *fields = pl.pallas_call(
        basis_kernel,
        out_shape=(jax.ShapeDtypeStruct((size, layers), f32),) + (tile,) * 6,
        in_specs=[vmem] * (9 + FACES + SWEEPS),
        out_specs=(vmem,) * 7,
        scratch_shapes=[pltpu.VMEM((8, layers), f32)]
        + [pltpu.VMEM((planes, rows, layers), f32)] * (2 + FACES + SWEEPS),
        compiler_params=params,
        name="basis",
    )(before, after, *near)
    everyone = lax.all_to_all(copies, AXES, 0, 0, tiled=True)
    return pl.pallas_call(
        pressure_kernel,
        out_shape=tile,
        in_specs=[vmem] * 7,
        out_specs=vmem,
        scratch_shapes=[pltpu.VMEM((4, layers // BLOCK_Z, layers), f32)],
        compiler_params=params,
        name="pressure",
    )(everyone, *fields)


def solution(mesh):
    def per_device(facies, *others):
        tile_x, tile_y, layers = facies.shape
        total_x = tile_x * mesh.shape["gx"]
        total_y = tile_y * mesh.shape["gy"]
        one_column = total_x == BLOCK_X and total_y == BLOCK_Y
        fits = layers % 128 == 0 and tile_y % 8 == 0 and min(tile_x, tile_y) >= MARGIN
        step = column_step if one_column and fits else general_step
        return step(facies, *others)

    in_specs = (P("gx", "gy", None), P("gx", "gy", None), P(), P(), P(), P(), P())
    out_specs = P("gx", "gy", None)
    return jax.shard_map(
        per_device, mesh=mesh, in_specs=in_specs, out_specs=out_specs, check_vma=False
    )
```

```python
import jax
import jax.numpy as jnp
import numpy as np
from jax import lax
from jax.experimental import pallas as pl
from jax.experimental.pallas import tpu as pltpu
from jax.sharding import PartitionSpec as P

BLOCK_X = 64
BLOCK_Y = 64
BLOCK_Z = 16
SWEEPS = 3


RELAX_WEIGHT = 2.0 / 3.0
HIGHEST = lax.Precision.HIGHEST
first_bits = np.array([0, 0, 0, 0, 1, 1, 1, 1], dtype=np.int32)
second_bits = np.array([0, 0, 1, 1, 0, 0, 1, 1], dtype=np.int32)
third_bits = np.array([0, 1, 0, 1, 0, 1, 0, 1], dtype=np.int32)
shift_along_x = np.array([0, 2, -2, 0, 0, 0, 0], dtype=np.int32)
shift_along_y = np.array([0, 0, 0, 2, -2, 0, 0], dtype=np.int32)
shift_along_z = np.array([0, 0, 0, 0, 0, 2, -2], dtype=np.int32)


def with_halo(value, sides, width):
    for axis, dim in sides:
        size, length = (lax.axis_size(axis), value.shape[dim])
        up = [(i, (i + 1) % size) for i in range(size - 1)]
        down = [(j, i) for i, j in up]
        last = lax.slice_in_dim(value, length - width, length, axis=dim)
        initial = lax.slice_in_dim(value, 0, width, axis=dim)
        before = lax.ppermute(last, axis, up)
        after = lax.ppermute(initial, axis, down)
        value = jnp.concatenate([before, value, after], axis=dim)
    return value


def support_of(coords, block_size, parity):
    return parity + 2 * jnp.floor_divide(
        coords + block_size // 2 - block_size * parity, 2 * block_size
    )


def parity_nodes(coords, block_size):
    return jnp.stack([support_of(coords, block_size, 0), support_of(coords, block_size, 1)])


def parity_start(coords, block_size):
    node_ids = parity_nodes(coords, block_size)
    return (node_ids == jnp.floor_divide(coords, block_size)[None]).astype(jnp.float32)


def parity_same(coords, block_size):
    node_here = parity_nodes(coords[:-1], block_size)
    node_next = parity_nodes(coords[1:], block_size)
    return (node_here == node_next).astype(jnp.float32)


def harmonic(left_perm, right_perm):
    return 2.0 * left_perm * right_perm / (left_perm + right_perm)


def face_pad(values_in, dim_id, before):
    widths = [(0, 0), (0, 0), (0, 0)]
    widths[dim_id] = (1, 0) if before else (0, 1)
    return jnp.pad(values_in, widths)


def expand(line_in, dim_id):
    new_shape = [1, 1, 1]
    new_shape[dim_id] = line_in.shape[0]
    return line_in.reshape(new_shape)


def split_faces(values_in, dim_id):
    length = values_in.shape[dim_id]
    below_part = lax.slice_in_dim(values_in, 0, length - 1, axis=dim_id)
    above_part = lax.slice_in_dim(values_in, 1, length, axis=dim_id)
    return (below_part, above_part)


def cut_apply(values_in, storage, trans_all, same_all):
    result = storage * values_in
    for dim_id in range(3):
        trans_face = trans_all[dim_id]
        same_line = expand(same_all[dim_id], dim_id)
        below_part, above_part = split_faces(values_in, dim_id)
        result = result + face_pad(
            trans_face * (below_part - same_line * above_part), dim_id, False
        )
        result = result + face_pad(trans_face * (above_part - same_line * below_part), dim_id, True)
    return result


def rim_terms(values_in, trans_all, same_all):
    result = []
    for dim_id in range(3):
        trans_face = trans_all[dim_id]
        cross_mask = 1.0 - expand(same_all[dim_id], dim_id)
        below_part, above_part = split_faces(values_in, dim_id)
        result.append(face_pad(-trans_face * cross_mask * above_part, dim_id, False))
        result.append(face_pad(-trans_face * cross_mask * below_part, dim_id, True))
    return result


def diagonal_of(storage, trans_all):
    result = storage
    for dim_id in range(3):
        result = (
            result
            + face_pad(trans_all[dim_id], dim_id, False)
            + face_pad(trans_all[dim_id], dim_id, True)
        )
    return result


def lookup(facies, code_table):
    result = jnp.zeros(facies.shape, jnp.float32)
    for code_id in range(code_table.shape[0]):
        result = result + jnp.where(facies == code_id, code_table[code_id], 0.0)
    return result


def flatten_node(index_x, index_y, index_z, counts):
    count_x, count_y, count_z = counts
    flat_ids = (
        jnp.clip(index_x, 0, count_x - 1) * count_y + jnp.clip(index_y, 0, count_y - 1)
    ) * count_z
    return (flat_ids + jnp.clip(index_z, 0, count_z - 1)).astype(jnp.int32)


def tile_indices(anchor_x, anchor_y, counts):
    count_x, count_y, count_z = counts
    row_x = parity_nodes(jnp.reshape(anchor_x, (1,)), BLOCK_X)[first_bits][:, 0]
    row_y = parity_nodes(jnp.reshape(anchor_y, (1,)), BLOCK_Y)[second_bits][:, 0]
    seg_first = jnp.maximum(jnp.arange(count_z + 1, dtype=jnp.int32) * BLOCK_Z - BLOCK_Z // 2, 0)
    row_z = parity_nodes(seg_first, BLOCK_Z)[third_bits]
    row_ids = flatten_node(row_x[:, None], row_y[:, None], row_z, counts)
    col_ids = flatten_node(
        row_x[:, None, None] + jnp.asarray(shift_along_x)[None, :, None],
        row_y[:, None, None] + jnp.asarray(shift_along_y)[None, :, None],
        row_z[:, None, :] + jnp.asarray(shift_along_z)[None, :, None],
        counts,
    )
    entry_ids = row_ids[None, :, None, :] * (count_x * count_y * count_z) + col_ids[:, None, :, :]
    return (entry_ids, row_ids)


def segment_matrix(layers, segment_count):
    seg_of = (jnp.arange(layers, dtype=jnp.int32) + BLOCK_Z // 2) // BLOCK_Z
    return (seg_of[:, None] == jnp.arange(segment_count, dtype=jnp.int32)[None, :]).astype(
        jnp.float32
    )


def solve_coarse(coarse, coarse_rhs):
    factor = jnp.linalg.cholesky(coarse)
    middle = lax.linalg.triangular_solve(factor, coarse_rhs[:, None], left_side=True, lower=True)
    return lax.linalg.triangular_solve(
        factor, middle, left_side=True, lower=True, transpose_a=True
    )[:, 0]


def geometry(coeffs, margin, anchor_x, anchor_y, total_x, total_y):
    coord_x = anchor_x - margin + jnp.arange(coeffs.shape[1], dtype=jnp.int32)
    coord_y = anchor_y - margin + jnp.arange(coeffs.shape[2], dtype=jnp.int32)
    coord_z = jnp.arange(coeffs.shape[3], dtype=jnp.int32)
    inside_x = (coord_x >= 0) & (coord_x < total_x)
    inside_y = (coord_y >= 0) & (coord_y < total_y)
    inside = inside_x[:, None, None] & inside_y[None, :, None]
    perm_safe = jnp.where(inside, coeffs[0], 1.0)
    storage = jnp.where(inside, coeffs[1], 1.0)
    valid_x = (inside_x[:-1] & inside_x[1:]).astype(jnp.float32)
    valid_y = (inside_y[:-1] & inside_y[1:]).astype(jnp.float32)
    trans_x = harmonic(perm_safe[:-1], perm_safe[1:]) * valid_x[:, None, None]
    trans_y = harmonic(perm_safe[:, :-1], perm_safe[:, 1:]) * valid_y[None, :, None]
    trans_z = harmonic(perm_safe[:, :, :-1], perm_safe[:, :, 1:])
    trans_all = (trans_x, trans_y, trans_z)
    same_all = (
        parity_same(coord_x, BLOCK_X)[first_bits],
        parity_same(coord_y, BLOCK_Y)[second_bits],
        parity_same(coord_z, BLOCK_Z)[third_bits],
    )
    starts = (
        parity_start(coord_x, BLOCK_X)[first_bits],
        parity_start(coord_y, BLOCK_Y)[second_bits],
        parity_start(coord_z, BLOCK_Z)[third_bits],
    )
    return (storage, trans_all, diagonal_of(storage, trans_all), same_all, starts)


def initial(geo_set):
    start_x, start_y, start_z = geo_set[4]
    return start_x[:, :, None, None] * start_y[:, None, :, None] * start_z[:, None, None, :]


def smooth(basis_ext, geo_set):
    storage, trans_all, diagonal, same_all, _ = geo_set

    def change_of(values_in, same_x, same_y, same_z):
        return (
            -RELAX_WEIGHT
            * cut_apply(values_in, storage, trans_all, (same_x, same_y, same_z))
            / diagonal
        )

    changes = jax.vmap(change_of)(basis_ext, same_all[0], same_all[1], same_all[2])[:, 1:-1, 1:-1]
    interior = basis_ext[:, 1:-1, 1:-1]
    change_sum = jnp.sum(changes, axis=0)
    return interior + changes - interior * change_sum[None]


def basis_halo(basis_now):
    return with_halo(basis_now, (("gx", 1), ("gy", 2)), 1)


def general_step(facies, source, facies_perm, facies_store, well_x, well_y, well_rate):
    tile_x, tile_y, layers = facies.shape
    devs_x = lax.axis_size("gx")
    devs_y = lax.axis_size("gy")
    total_x = tile_x * devs_x
    total_y = tile_y * devs_y
    anchor_x = lax.axis_index("gx") * tile_x
    anchor_y = lax.axis_index("gy") * tile_y
    coeffs = jnp.stack([lookup(facies, facies_perm), lookup(facies, facies_store)])
    coeff_wide = with_halo(coeffs, (("gx", 1), ("gy", 2)), 1)
    geo_one = geometry(coeff_wide, 1, anchor_x, anchor_y, total_x, total_y)
    basis_now = initial(geo_one)[:, 1:-1, 1:-1]
    for _ in range(SWEEPS):
        basis_now = smooth(basis_halo(basis_now), geo_one)
    basis_now = basis_halo(basis_now)
    storage, trans_all, diagonal, same_all, _ = geo_one

    def terms_of(values_in, same_x, same_y, same_z):
        same_three = (same_x, same_y, same_z)
        return jnp.stack(
            [cut_apply(values_in, storage, trans_all, same_three)]
            + rim_terms(values_in, trans_all, same_three)
        )

    term_stack = jax.vmap(terms_of)(basis_now, same_all[0], same_all[1], same_all[2])[
        :, :, 1:-1, 1:-1
    ]
    interior = basis_now[:, 1:-1, 1:-1]
    count_x = total_x // BLOCK_X
    count_y = total_y // BLOCK_Y
    count_z = layers // BLOCK_Z
    counts = (count_x, count_y, count_z)
    coarse_count = count_x * count_y * count_z
    zmatrix = segment_matrix(layers, count_z + 1)
    gram_local = jnp.einsum("apqz,cspqz->casz", interior, term_stack, precision=HIGHEST)
    gram_local = jnp.einsum("casz,zg->casg", gram_local, zmatrix, precision=HIGHEST)
    cell_x = anchor_x + jnp.arange(tile_x, dtype=jnp.int32)
    cell_y = anchor_y + jnp.arange(tile_y, dtype=jnp.int32)
    hit_x = (well_x[:, None] == cell_x[None, :]).astype(jnp.float32)
    hit_y = (well_y[:, None] == cell_y[None, :]).astype(jnp.float32)
    column = jnp.einsum("w,wx,wy->xy", well_rate, hit_x, hit_y, precision=HIGHEST)
    rhs_fine = source + column[:, :, None] / layers
    rhs_local = jnp.einsum("apqz,pqz->az", interior, rhs_fine, precision=HIGHEST)
    rhs_local = jnp.einsum("az,zg->ag", rhs_local, zmatrix, precision=HIGHEST)
    entry_ids, row_ids = tile_indices(anchor_x, anchor_y, counts)
    local_matrix = (
        jnp.zeros((coarse_count * coarse_count,), jnp.float32)
        .at[entry_ids.reshape(-1)]
        .add(gram_local.reshape(-1))
    )
    local_matrix = local_matrix.reshape(coarse_count, coarse_count)
    local_rhs = (
        jnp.zeros((coarse_count,), jnp.float32).at[row_ids.reshape(-1)].add(rhs_local.reshape(-1))
    )
    coarse, coarse_rhs = lax.psum((local_matrix, local_rhs), ("gx", "gy"))
    coarse_solution = solve_coarse(coarse, coarse_rhs)
    values_at = coarse_solution[row_ids]
    per_layer = jnp.einsum("ag,zg->az", values_at, zmatrix, precision=HIGHEST)
    prolonged = jnp.einsum("apqz,az->pqz", interior, per_layer, precision=HIGHEST)
    prolonged_ext = with_halo(prolonged, (("gx", 0), ("gy", 1)), 1)
    ones_all = (
        jnp.ones((tile_x + 1,), jnp.float32),
        jnp.ones((tile_y + 1,), jnp.float32),
        jnp.ones((layers - 1,), jnp.float32),
    )
    applied = cut_apply(prolonged_ext, storage, trans_all, ones_all)[1:-1, 1:-1]
    return prolonged + RELAX_WEIGHT * (rhs_fine - applied) / diagonal[1:-1, 1:-1]


MARGIN = SWEEPS + 1
FACES = 6
AXES = ("gx", "gy")
VMEM_BYTES = 16 * 2**20


def neighbour(index, size, first):
    partner = first + ((index - first) ^ 1) if index >= first else -1
    return partner if 0 <= partner < size else None


def swap(value, first_x, first_y):
    size_x, size_y = (lax.axis_size(axis) for axis in AXES)
    pairs = []
    for x in range(size_x):
        for y in range(size_y):
            to_x = x if first_x is None else neighbour(x, size_x, first_x)
            to_y = y if first_y is None else neighbour(y, size_y, first_y)
            if to_x is None:
                to_x, to_y = (x, neighbour(y, size_y, 0))
            elif to_y is None:
                to_x, to_y = (neighbour(x, size_x, 0), y)
            if to_x is not None and to_y is not None:
                pairs.append((x * size_y + y, to_x * size_y + to_y))
    return lax.ppermute(value, AXES, pairs)


def wide_tile(facies):
    even_x, even_y = (lax.axis_index(axis) % 2 == 0 for axis in AXES)

    def planes(value, at_first):
        return jnp.where(at_first, value[:MARGIN], value[-MARGIN:])

    def rows(value, at_first):
        return jnp.where(at_first, value[:, :MARGIN], value[:, -MARGIN:])

    def sides(far, near):
        return jnp.concatenate([jnp.where(even_y, near, far), jnp.where(even_y, far, near)], axis=1)

    near_end = planes(facies, ~even_x)
    far_y = swap(facies, None, 1)
    near_y = swap(facies, None, 0)
    near_x = swap(near_end, 0, None)
    own = jnp.concatenate([facies, sides(rows(far_y, ~even_y), rows(near_y, even_y))], axis=1)
    far_x = swap(planes(own, even_x), 1, None)
    beside = (rows(near_x, even_y), rows(near_x, ~even_y))
    corner_far = swap(beside[0], None, 1)
    corner_near = swap(beside[1], None, 0)
    near_x = jnp.concatenate([near_x, sides(corner_far, corner_near)], axis=1)
    return own, jnp.where(even_x, far_x, near_x), jnp.where(even_x, near_x, far_x)


def lane_iota(shape):
    return lax.broadcasted_iota(jnp.int32, shape, len(shape) - 1)


def face_ends(layer, parity):
    return lax.rem(layer + 1 + BLOCK_Z // 2 + BLOCK_Z * parity, 2 * BLOCK_Z) == 0


def in_grid(layer, parity, count):
    shifted = layer + BLOCK_Z // 2 + BLOCK_Z * parity
    node = 2 * (shifted // (2 * BLOCK_Z)) - parity
    return (node >= 0) & (node < count)


def up(value, axis):
    return pltpu.roll(value, value.shape[axis] - 1, axis)


def down(value, axis):
    return pltpu.roll(value, 1, axis)


def code_select(table, codes):
    result = jnp.broadcast_to(table[0], codes.shape)
    for code_id in range(1, len(table)):
        result = jnp.where(codes == code_id, table[code_id], result)
    return result


def plane_faces(resist, store, face_y):
    layer = lane_iota(resist.shape)
    y_face = jnp.where(face_y, 2.0 / (resist + up(resist, 0)), 0.0)
    z_face = jnp.where(layer == resist.shape[1] - 1, 0.0, 2.0 / (resist + up(resist, 1)))
    z_faces = [jnp.where(face_ends(layer, parity), 0.0, z_face) for parity in (0, 1)]
    faces = (y_face, *z_faces)
    before = (down(y_face, 0), *(down(value, 1) for value in z_faces))
    part = store + y_face + before[0] + z_face + jnp.maximum(before[1], before[2])
    return faces + before, part


def y_face_mask(shape, tile_y):
    row = lax.broadcasted_iota(jnp.int32, shape, 0)
    place = lax.axis_index("gy") * tile_y + jnp.where(row < tile_y + MARGIN, row, row - shape[0])
    inside = (place >= 0) & (place + 1 < lax.axis_size("gy") * tile_y)
    return inside & (row != tile_y + MARGIN - 1)


def sweep_planes(low, high, read, write, face_x, faces_of, scale):
    if low >= high:
        return
    here = read(low)
    flux_before = face_x(low - 1) * (here - read(low - 1))
    for plane in range(low, high):
        beyond = read(plane + 1)
        flux = face_x(plane) * (beyond - here)
        y_after, z0_after, z1_after, y_before, z0_before, z1_before = faces_of(plane)
        above, below = (up(here, 1), down(here, 1))
        other = 1.0 - here
        total = flux - flux_before
        total = total + (y_after * (up(here, 0) - here) + y_before * (down(here, 0) - here))
        total = total + (z0_after * (above * other) - z1_after * (here * (1.0 - above)))
        total = total + (z0_before * (below * other) - z1_before * (here * (1.0 - below)))
        write(plane, here + scale(plane) * total)
        here, flux_before = (beyond, flux)


def start_field(shape):
    return jnp.where(lax.rem(lane_iota(shape) // BLOCK_Z, 2) == 0, 1.0, 0.0)


def tile_kernel(
    rows_ref, source_ref, perm_ref, store_ref, well_x_ref, well_y_ref, well_rate_ref,
    table_ref, rhs_ref, resist_ref, storage_ref, x_ref, part_ref, scale_ref, *more_refs,
):
    tile_x, rows, layers = rows_ref.shape
    tile_y = source_ref.shape[1]
    anchor_x = lax.axis_index("gx") * tile_x
    anchor_y = lax.axis_index("gy") * tile_y
    codes = perm_ref.shape[0]
    resists = [
        1.0 / jnp.full((1, layers), perm_ref[code], jnp.float32) for code in range(codes)
    ]
    stores = [jnp.full((1, layers), store_ref[code], jnp.float32) for code in range(codes)]
    for code in range(codes):
        table_ref[code : code + 1] = resists[code]
        table_ref[codes + code : codes + code + 1] = stores[code]
    face_refs, field_refs = (more_refs[:FACES], more_refs[FACES:])
    face_y = y_face_mask((rows, layers), tile_y)
    hit_y = (
        lax.broadcasted_iota(jnp.int32, (tile_y, well_y_ref.shape[1]), 0) + anchor_y
        == well_y_ref[...]
    )
    ones = jnp.ones((well_rate_ref.shape[1], layers), jnp.float32)
    before, x_before, part_before = (None, None, None)
    for plane in range(tile_x):
        resist = code_select(resists, rows_ref[plane])
        store = code_select(stores, rows_ref[plane])
        faces, part = plane_faces(resist, store, face_y)
        resist_ref[plane] = resist
        storage_ref[plane] = store
        for ref, face in zip(face_refs, faces):
            ref[plane] = face
        part_ref[plane] = part
        if plane:
            x_face = 2.0 / (before + resist)
            x_ref[plane - 1] = x_face
            if plane > 1:
                scale_ref[plane - 1] = RELAX_WEIGHT / (part_before + x_face + x_before)
            x_before = x_face
        before, part_before = (resist, part)
        hit = hit_y & (well_x_ref[...] == anchor_x + plane)
        rates = jnp.where(hit, well_rate_ref[...], 0.0)
        column = jnp.dot(rates, ones, precision=HIGHEST, preferred_element_type=jnp.float32)
        rhs_ref[plane] = source_ref[plane] + column / layers
    start = start_field((rows, layers))
    read = lambda plane: start
    for sweep_id, field in enumerate(field_refs):
        sweep_planes(
            1 + sweep_id,
            tile_x - 1 - sweep_id,
            read,
            field.__setitem__,
            x_ref.__getitem__,
            lambda plane: [ref[plane] for ref in face_refs],
            scale_ref.__getitem__,
        )
        read = field.__getitem__


def basis_kernel(*refs):
    before_ref, after_ref, table_ref, rhs_ref, resist_ref, storage_ref, x_ref, part_ref, scale_ref = refs[:9]
    refs = refs[9:]
    near_faces, near_fields, refs = (refs[:FACES], refs[FACES : FACES + SWEEPS], refs[FACES + SWEEPS :])
    packed_ref, basis_ref, side_ref, rhs_out_ref, store_out_ref, up_ref, down_ref, sums_ref = refs[:8]
    scale_far, x_far = refs[8:10]
    far_faces, far_fields = (refs[10 : 10 + FACES], refs[10 + FACES :])
    tile_x, tile_y, layers = rhs_ref.shape
    rows = resist_ref.shape[1]
    planes = tile_x + 2 * MARGIN
    shape = (rows, layers)
    anchor_x = lax.axis_index("gx") * tile_x
    total_x = lax.axis_size("gx") * tile_x
    face_mask_y = y_face_mask(shape, tile_y)
    codes = table_ref.shape[0] // 2
    table = [table_ref[i : i + 1] for i in range(2 * codes)]

    def own(plane, depth=0):
        return MARGIN + depth <= plane < MARGIN + tile_x - depth

    def face_x(plane):
        inner = own(plane) and own(plane + 1)
        return x_ref[plane - MARGIN] if inner else x_far[plane]

    def near_or_far(near, far, depth=0):
        return lambda plane: near[plane - MARGIN] if own(plane, depth) else far[plane]

    def faces_of(plane):
        return [near_or_far(near, far)(plane) for near, far in zip(near_faces, far_faces)]

    scale = near_or_far(scale_ref, scale_far, 1)
    resist_last, x_last, part_last = (None, None, None)
    for plane in range(planes):
        part = None
        if own(plane):
            resist = resist_ref[plane - MARGIN]
            part = part_ref[plane - MARGIN]
        else:
            strip = before_ref if plane < MARGIN else after_ref
            facies = strip[plane if plane < MARGIN else plane - MARGIN - tile_x]
            resist = code_select(table[:codes], facies)
            if 0 < plane < planes - 1:
                store = code_select(table[codes:], facies)
                faces, part = plane_faces(resist, store, face_mask_y)
                for ref, face in zip(far_faces, faces):
                    ref[plane] = face
        if plane:
            if own(plane - 1) and own(plane):
                x_face = face_x(plane - 1)
            else:
                here = anchor_x + plane - 1 - MARGIN
                x_face = 2.0 / (resist_last + resist)
                x_face = jnp.where((here >= 0) & (here + 1 < total_x), x_face, 0.0)
                x_far[plane - 1] = x_face
            if plane > 1 and not own(plane - 1, 1):
                scale_far[plane - 1] = RELAX_WEIGHT / (part_last + x_face + x_last)
            x_last = x_face
        resist_last, part_last = (resist, part)

    start = start_field(shape)
    read = lambda plane: start
    for sweep_id in range(SWEEPS):
        depth = 1 + sweep_id
        first_end = min(MARGIN + depth, planes - depth)
        last_start = max(first_end, MARGIN + tile_x - depth)
        for low, high in ((depth, first_end), (last_start, planes - depth)):
            sweep_planes(
                low,
                high,
                read,
                far_fields[sweep_id].__setitem__,
                face_x,
                faces_of,
                scale,
            )
        read = near_or_far(near_fields[sweep_id], far_fields[sweep_id], depth)

    tile = (tile_y, layers)
    cut_0 = face_ends(lane_iota(tile), 0)
    cut_any = cut_0 | face_ends(lane_iota(tile), 1)

    def inner(value):
        return value[:tile_y]

    sums = None
    for plane in range(tile_x):
        at = plane + MARGIN
        here_all = read(at)
        here = inner(here_all)
        step_y_all = up(here_all, 0) - here_all
        y_after, z0_after, z1_after, y_before, z0_before, z1_before = faces_of(at)
        flux_y = inner(y_after * step_y_all)
        flux_y_before = inner(y_before * (here_all - down(here_all, 0)))
        step_x = inner(read(at + 1)) - here
        flux_x = inner(face_x(at)) * step_x
        flux_before = inner(face_x(at - 1)) * (here - inner(read(at - 1)))
        z_face = inner(jnp.maximum(z0_after, z1_after))
        above = up(here, 1)
        step_z = above - here
        energy_z = z_face * step_z * step_z
        other = 1.0 - here
        store = inner(storage_ref[plane])
        factor = inner(scale(at))
        rhs = rhs_ref[plane]
        below_end = jnp.where(cut_0, here, other)
        above_end = jnp.where(cut_0, above, 1.0 - above)
        z_cut = jnp.where(cut_any, z_face, 0.0)
        basis_ref[plane] = here
        side_ref[plane] = factor * (
            (flux_before - flux_x) + (flux_y_before - flux_y)
        )
        rhs_out_ref[plane] = factor * rhs
        store_out_ref[plane] = factor * store
        up_ref[plane] = factor * z_face
        down_ref[plane] = factor * inner(jnp.maximum(z0_before, z1_before))
        terms = (
            store * here * here,
            store * here * other,
            store * other * other,
            flux_x * step_x + flux_y * inner(step_y_all) + jnp.where(cut_any, 0.0, energy_z),
            jnp.where(cut_any, energy_z, 0.0),
            z_cut * below_end * below_end,
            z_cut * above_end * above_end,
            z_cut * below_end * above_end,
            here * rhs,
            other * rhs,
        )
        sums = terms if sums is None else [a + b for a, b in zip(sums, terms)]
    mass_00, mass_01, mass_11, energy, cut, low_2, high_2, low_high, rhs_0, rhs_1 = (
        jnp.sum(total, axis=0, keepdims=True) for total in sums
    )
    line = lane_iota((1, layers))
    count = layers // BLOCK_Z
    ends = (face_ends(line, 0), face_ends(line, 1))
    inside = (in_grid(line, 0, count), in_grid(line, 1, count))
    for parity, mass, right in ((0, mass_00, rhs_0), (1, mass_11, rhs_1)):
        own_end = jnp.where(ends[parity], low_2, cut)
        beyond_end = down(jnp.where(ends[parity], high_2, 0.0), 1)
        entry = mass + energy + own_end + beyond_end
        sums_ref[parity : parity + 1] = jnp.where(inside[parity], entry, 0.0)
        sums_ref[4 + parity : 5 + parity] = jnp.where(inside[parity], right, 0.0)
    sums_ref[2:3] = mass_01 - energy + (low_high - low_2) + down(low_high - high_2, 1)
    sums_ref[3:4] = -low_high
    sums_ref[6:8] = jnp.zeros((2, layers), jnp.float32)
    line = lax.broadcasted_iota(jnp.int32, (layers, layers), 0)
    lane = lane_iota((layers, layers))
    segment = lambda at: lax.rem(at + BLOCK_Z // 2, layers) // BLOCK_Z
    same = jnp.where(segment(line) == segment(lane), 1.0, 0.0)
    window = jnp.dot(sums_ref[...], same, precision=HIGHEST, preferred_element_type=jnp.float32)
    row = lax.broadcasted_iota(jnp.int32, window.shape, 0)
    keep = lax.rem(lane_iota(window.shape), BLOCK_Z) == row
    packed = jnp.sum(jnp.where(keep, window, 0.0), axis=0, keepdims=True)
    packed_ref[...] = jnp.broadcast_to(packed, packed_ref.shape)


def solve_band(diagonal, first, second, right):
    count = len(diagonal)
    matrix = {(k, k): diagonal[k] for k in range(count)}
    for distance, band in ((1, first), (2, second)):
        for k in range(count - distance):
            matrix[k, k + distance] = band[k]
            matrix[k + distance, k] = band[k]
    left = list(range(count))
    steps = []
    while left:
        pivot = left.pop(0 if len(steps) % 2 == 0 else -1)
        inverse = 1.0 / matrix[pivot, pivot]
        linked = [k for k in left if (pivot, k) in matrix]
        lower = {k: matrix[pivot, k] * inverse for k in linked}
        for k in linked:
            right[k] = right[k] - lower[k] * right[pivot]
            for other in linked:
                if other >= k:
                    change = lower[k] * matrix[pivot, other]
                    entry = matrix[k, other] - change if (k, other) in matrix else -change
                    matrix[k, other] = entry
                    matrix[other, k] = entry
        steps.append((pivot, inverse, lower))
    values = [None] * count
    for pivot, inverse, lower in reversed(steps):
        value = right[pivot] * inverse
        for k, factor in lower.items():
            value = value - factor * values[k]
        values[pivot] = value
    return values


def pressure_kernel(
    rows_ref, basis_ref, side_ref, rhs_ref, store_ref, up_ref, down_ref, out_ref, entries
):
    tile_x, tile_y, layers = basis_ref.shape
    count = layers // BLOCK_Z
    half = BLOCK_Z // 2
    shape = (count, layers)
    node = lax.broadcasted_iota(jnp.int32, shape, 0)
    layer = lane_iota(shape)
    packed = jnp.sum(rows_ref[...], axis=0, keepdims=True)

    def held(segment, kind):
        return layer == lax.rem(segment * BLOCK_Z + kind, layers)

    parity = lax.rem(node, 2)
    own = held(node, parity) | held(node + 1, parity)
    right = held(node, parity + 4) | held(node + 1, parity + 4)
    masks = (own, held(node + 1, 2), held(node + 1, 3), right)
    for part_id, mask in enumerate(masks):
        part = jnp.where(mask, packed, 0.0)
        entries[part_id] = jnp.broadcast_to(jnp.sum(part, axis=1, keepdims=True), shape)
    values = solve_band(
        *([entries[part_id, k : k + 1] for k in range(count)] for part_id in range(4))
    )
    line = lane_iota((1, layers))
    fields = [jnp.zeros((1, layers), jnp.float32)] * 2
    for k in range(count):
        support = (line >= k * BLOCK_Z - half) & (line < k * BLOCK_Z + 3 * half)
        fields[k % 2] = jnp.where(support, values[k], fields[k % 2])
    value_0 = jnp.broadcast_to(fields[0], (tile_y, layers))
    value_1 = jnp.broadcast_to(fields[1], (tile_y, layers))
    apart = value_0 - value_1
    for plane in range(tile_x):
        here = basis_ref[plane]
        prolonged = here * value_0 + (1.0 - here) * value_1
        applied = (
            store_ref[plane] * prolonged
            + apart * side_ref[plane]
            + up_ref[plane] * (prolonged - up(prolonged, 1))
            + down_ref[plane] * (prolonged - down(prolonged, 1))
        )
        out_ref[plane] = prolonged + (rhs_ref[plane] - applied)


def column_step(facies, source, facies_perm, facies_store, well_x, well_y, well_rate):
    tile_x, tile_y, layers = facies.shape
    rows = tile_y + 2 * MARGIN
    planes = tile_x + 2 * MARGIN
    size = lax.axis_size(AXES)
    f32 = jnp.float32
    tile = jax.ShapeDtypeStruct(facies.shape, f32)
    wide = jax.ShapeDtypeStruct((tile_x, rows, layers), f32)
    vmem = pl.BlockSpec(memory_space=pltpu.VMEM)
    smem = pl.BlockSpec(memory_space=pltpu.SMEM)
    params = pltpu.CompilerParams(vmem_limit_bytes=VMEM_BYTES)

    own, before, after = wide_tile(facies)
    near = pl.pallas_call(
        tile_kernel,
        out_shape=(jax.ShapeDtypeStruct((2 * facies_perm.shape[0], layers), f32),)
        + (tile,)
        + (wide,) * (5 + FACES + SWEEPS),
        in_specs=[vmem, vmem, smem, smem, vmem, vmem, vmem],
        out_specs=(vmem,) * (7 + FACES + SWEEPS),
        compiler_params=params,
        cost_estimate=pl.CostEstimate(flops=3000000, bytes_accessed=1000000, transcendentals=0),
        name="tile",
    )(
        own,
        source,
        facies_perm,
        facies_store,
        well_x[None, :],
        well_y[None, :],
        well_rate[None, :],
    )
    copies, *fields = pl.pallas_call(
        basis_kernel,
        out_shape=(jax.ShapeDtypeStruct((size, layers), f32),) + (tile,) * 6,
        in_specs=[vmem] * (9 + FACES + SWEEPS),
        out_specs=(vmem,) * 7,
        scratch_shapes=[pltpu.VMEM((8, layers), f32)]
        + [pltpu.VMEM((planes, rows, layers), f32)] * (2 + FACES + SWEEPS),
        compiler_params=params,
        name="basis",
    )(before, after, *near)
    everyone = lax.all_to_all(copies, AXES, 0, 0, tiled=True)
    return pl.pallas_call(
        pressure_kernel,
        out_shape=tile,
        in_specs=[vmem] * 7,
        out_specs=vmem,
        scratch_shapes=[pltpu.VMEM((4, layers // BLOCK_Z, layers), f32)],
        compiler_params=params,
        name="pressure",
    )(everyone, *fields)


def solution(mesh):
    def per_device(facies, *others):
        tile_x, tile_y, layers = facies.shape
        total_x = tile_x * mesh.shape["gx"]
        total_y = tile_y * mesh.shape["gy"]
        one_column = total_x == BLOCK_X and total_y == BLOCK_Y
        fits = layers % 128 == 0 and tile_y % 8 == 0 and min(tile_x, tile_y) >= MARGIN
        step = column_step if one_column and fits else general_step
        return step(facies, *others)

    in_specs = (P("gx", "gy", None), P("gx", "gy", None), P(), P(), P(), P(), P())
    out_specs = P("gx", "gy", None)
    return jax.shard_map(
        per_device, mesh=mesh, in_specs=in_specs, out_specs=out_specs, check_vma=False
    )
```
